32 devices in a mesh: fsdp: 16 (over z, y, x), tp: 2 (over core).
Axes of the slice: x: 2, y: 2, z: 4, core: 2. Of those that a mesh axis runs over, the one named last changes fastest.
Arguments:
- inputs: bfloat16 [16, 1024, 768], P('fsdp', 'tp'), may hold values from -6 to 6
- query_key_value_weight: bfloat16 [3, 768, 768], P(None, 'fsdp', 'tp'), may hold values from -0.21875 to 0.21875
- attention_out_weight: bfloat16 [768, 768], P('tp', 'fsdp'), may hold values from -3.5 to 3.5
- up_weight: bfloat16 [768, 3072], P('fsdp', 'tp'), may hold values from -0.21875 to 0.21875
- down_weight: bfloat16 [3072, 768], P('tp', 'fsdp'), may hold values from -0.109375 to 0.109375
- qk_bias: bfloat16 [2, 768], P(None, 'fsdp'), may hold values from -3 to 3
- value_bias: bfloat16 [768], P('fsdp'), may hold values from -0.119628906 to 0.119628906
- out_bias: bfloat16 [768], P('fsdp'), may hold values from -1.1953125 to 1.1953125
- ffn_in_bias: bfloat16 [3072], P('fsdp'), may hold values from -3 to 3
- ffn_out_bias: bfloat16 [768], P('fsdp'), may hold values from -1.1953125 to 1.1953125
- norm_gains: bfloat16 [2, 768], P(None, 'fsdp'), may hold values from 0.5 to 1.5
- norm_biases: bfloat16 [2, 768], P(None, 'fsdp'), may hold values from -1.1953125 to 1.1953125
- grad_out: bfloat16 [16, 1024, 768], P('fsdp', 'tp'), may hold values from -6 to 6
Outputs:
- output: bfloat16 [16, 1024, 768], P('fsdp', 'tp')
- grad_input: float32 [16, 1024, 768], P('fsdp', 'tp')
- grad_w_qkv: float32 [3, 768, 768], P(None, 'fsdp', 'tp')
- grad_w_out: float32 [768, 768], P('tp', 'fsdp')
- grad_w_up: float32 [768, 3072], P('fsdp', 'tp')
- grad_w_down: float32 [3072, 768], P('tp', 'fsdp')
- grad_qk_bias: float32 [2, 768], P(None, 'fsdp')
- grad_value_bias: float32 [768], P('fsdp')
- grad_out_bias: float32 [768], P('fsdp')
- grad_ffn_in_bias: float32 [3072], P('fsdp')
- grad_ffn_out_bias: float32 [768], P('fsdp')
- grad_norm_gains: float32 [2, 768], P(None, 'fsdp')
- grad_norm_biases: float32 [2, 768], P(None, 'fsdp')
The draws below stay inside these ranges and needn't reach their ends.
All inputs are finite; a program needn't handle non-finite values.
Results may differ from the reference program's by a relative error of at most 0.017.
Values may be sent and summed in bfloat16 or wider, within the bound.
A program may use at most 128 MiB of HBM per device.

```python
import jax
import jax.numpy as jnp
from jax import lax

D = 768
HEADS = 12
HEAD_DIM = 64
FF = 3072
SEQ = 1024
SEQS = 16


def strengthened(entries, own_key, source, target, shards_of, factor):
    owner, partner = [(jnp.arange(entries.shape[dim]) // (entries.shape[dim] // shards_of)).reshape([-1 if axis == dim else 1 for axis in range(entries.ndim)]) for dim in (source, target)]
    chosen = jax.random.permutation(own_key, shards_of)[partner]
    strong = (owner == chosen) | (owner == (partner + shards_of // 2) % shards_of)
    return jnp.where(strong, factor * entries, entries)


def block_levels(stream_key, extent, shards, low, top_value):
    level, own = 1.0, jax.random.fold_in(stream_key, 6)
    for position, blocks in shards:
        heights = jnp.exp(jax.random.uniform(jax.random.fold_in(own, position), (blocks,), jnp.float32, low / len(shards), top_value / len(shards)))
        level = level * jnp.repeat(heights, extent[position] // blocks).reshape([-1 if axis == position else 1 for axis in range(len(extent))])
    return level


def scatter_about(stream_key, extent, deviation, limit, pieces=(), held_as=jnp.bfloat16):
    values = deviation * jax.random.normal(stream_key, extent, jnp.float32)
    if pieces:
        values = values * block_levels(stream_key, extent, pieces, -0.22, 0.18)
    return jnp.clip(values, -limit, limit).astype(held_as)


def heavy_noise(own_key, extent, deviation, reach, split, heavy, kind=jnp.bfloat16):
    values = deviation * jax.random.normal(own_key, extent, jnp.float32)
    if split:
        values = values * block_levels(own_key, extent, split, -0.22, 0.18)
    return jnp.clip(strengthened(values, jax.random.fold_in(own_key, 3), *heavy), -reach, reach).astype(kind)


def setup_inputs(seed: int = 0) -> dict:
    streams_of = jax.random.split(jax.random.key(seed), 14)
    inputs = heavy_noise(streams_of[0], (SEQS, SEQ, D), 1.0, 6.0, ((0, 16), (1, 2)), (0, 2, 16, 2.0))
    query_key_value_weight = scatter_about(streams_of[1], (3, D, D), D ** -0.5, 0.21875, ((1, 16), (2, 2)))
    attention_out_weight = scatter_about(streams_of[2], (D, D), (max(D // 256, 1)) ** -0.5, 3.5, ((0, 2), (1, 16)))
    up_weight = scatter_about(streams_of[3], (D, FF), D ** -0.5, 0.21875, ((0, 16), (1, 2)))
    down_weight = scatter_about(streams_of[4], (FF, D), FF ** -0.5, 0.109375, ((0, 2), (1, 16)))
    qk_bias = scatter_about(streams_of[5], (2, D), 0.5, 3.0, ((1, 16),))
    value_bias = scatter_about(streams_of[6], (D,), 0.02, 0.119628906, ((0, 16),))
    out_bias = scatter_about(streams_of[7], (D,), 0.2, 1.1953125, ((0, 16),))
    ffn_in_bias = scatter_about(streams_of[8], (FF,), 0.5, 3.0, ((0, 16),))
    ffn_out_bias = scatter_about(streams_of[9], (D,), 0.2, 1.1953125, ((0, 16),))
    norm_gains = jnp.clip(1.0 + 0.1 * jax.random.normal(streams_of[10], (2, D), jnp.float32), 0.5, 1.5).astype(jnp.bfloat16)
    norm_biases = scatter_about(streams_of[11], (2, D), 0.2, 1.1953125, ((1, 16),))
    grad_out = heavy_noise(streams_of[12], (SEQS, SEQ, D), 1.0, 6.0, ((0, 16), (1, 2)), (0, 2, 16, 2.0))
    return dict(inputs=inputs, query_key_value_weight=query_key_value_weight, attention_out_weight=attention_out_weight, up_weight=up_weight, down_weight=down_weight, qk_bias=qk_bias, value_bias=value_bias, out_bias=out_bias, ffn_in_bias=ffn_in_bias, ffn_out_bias=ffn_out_bias, norm_gains=norm_gains, norm_biases=norm_biases, grad_out=grad_out)


@jax.custom_vjp
def low(v):
    return lax.optimization_barrier(v.astype(jnp.bfloat16)).astype(jnp.float32)

@jax.custom_vjp
def low_back(v):
    return v

def low_keep(v):
    return (low(v), None)

def low_pass(kept, grad):
    return (grad,)

def back_keep(v):
    return (v, None)

def back_low(kept, grad):
    return (low(grad),)
low.defvjp(low_keep, low_pass)
low_back.defvjp(back_keep, back_low)
HIGHEST_PREC = lax.Precision.HIGHEST
norm_eps = 1e-05

def layer_norm(values, gain, shift):
    center = values - lax.optimization_barrier(jnp.mean(values, -1, keepdims=True))
    spread = lax.optimization_barrier(jnp.mean(center * center, -1, keepdims=True))
    return center * lax.rsqrt(spread + norm_eps) * gain + shift

def one_sequence(params, tokens):
    query_key_value_weight, attention_out_weight, up_weight, down_weight, qk_bias, value_bias, out_bias, ffn_in_bias, ffn_out_bias, norm_gains, norm_biases = params
    proj_bias = jnp.concatenate([qk_bias, value_bias[None, :]], 0)
    projected = low_back(jnp.einsum('ld,mde->mle', tokens, query_key_value_weight, precision=HIGHEST_PREC) + proj_bias[:, None, :])
    angles = jnp.pi / 2.0 * jnp.arange(SEQ, dtype=jnp.float32) / SEQ
    cosine = jnp.cos(angles)[:, None, None]
    sine_w = jnp.sin(angles)[:, None, None]

    def features(pre_act):
        rectified = jax.nn.relu(pre_act).reshape(SEQ, HEADS, HEAD_DIM)
        return low(jnp.concatenate([rectified * cosine, rectified * sine_w], -1))
    q_feat = features(projected[0])
    k_feat = features(projected[1])
    values = low(projected[2]).reshape(SEQ, HEADS, HEAD_DIM)
    positions = jnp.arange(SEQ)
    causal_mask = positions[:, None] >= positions[None, :]
    scores = jnp.einsum('ihf,jhf->hij', q_feat, k_feat, precision=HIGHEST_PREC)
    scores = low_back(jnp.where(causal_mask[None], scores, 0.0))
    totals = lax.optimization_barrier(jnp.sum(scores, -1))
    weighted = low_back(jnp.einsum('hij,jhe->ihe', low(scores), values, precision=HIGHEST_PREC))
    context_rows = low((weighted / jnp.maximum(totals, 1.0).T[:, :, None]).reshape(SEQ, D))
    attended = low_back(jnp.dot(context_rows, attention_out_weight, precision=HIGHEST_PREC) + out_bias)
    normed_one = layer_norm(tokens + attended, norm_gains[0], norm_biases[0])
    hidden_pre = low_back(jnp.dot(low(normed_one), up_weight, precision=HIGHEST_PREC) + ffn_in_bias)
    hidden_activation = low(jax.nn.gelu(hidden_pre, approximate=False))
    branch = low_back(jnp.dot(hidden_activation, down_weight, precision=HIGHEST_PREC) + ffn_out_bias)
    return layer_norm(normed_one + branch, norm_gains[1], norm_biases[1])

def reference(inputs, query_key_value_weight, attention_out_weight, up_weight, down_weight, qk_bias, value_bias, out_bias, ffn_in_bias, ffn_out_bias, norm_gains, norm_biases, grad_out):
    params = (query_key_value_weight.astype(jnp.float32), attention_out_weight.astype(jnp.float32), up_weight.astype(jnp.float32), down_weight.astype(jnp.float32), qk_bias.astype(jnp.float32), value_bias.astype(jnp.float32), out_bias.astype(jnp.float32), ffn_in_bias.astype(jnp.float32), ffn_out_bias.astype(jnp.float32), norm_gains.astype(jnp.float32), norm_biases.astype(jnp.float32))
    stepper = jax.checkpoint(one_sequence)

    def whole_layer(weights, sequences):

        def scan_step(carried, tokens):
            return (carried, stepper(weights, tokens))
        return lax.scan(scan_step, jnp.zeros((), jnp.float32), sequences)[1]
    result, pullback = jax.vjp(whole_layer, params, inputs.astype(jnp.float32))
    param_grads, input_grad = pullback(grad_out.astype(jnp.float32))
    return (result.astype(jnp.bfloat16), input_grad, param_grads[0], param_grads[1], param_grads[2], param_grads[3], param_grads[4], param_grads[5], param_grads[6], param_grads[7], param_grads[8], param_grads[9], param_grads[10])
```

```python
from functools import partial

import jax
import jax.numpy as jnp
from jax import lax
from jax.experimental import pallas as pl
from jax.experimental.pallas import tpu as pltpu
from jax.sharding import PartitionSpec as P

HEAD_DIM = 64
MESH = pl.DeviceIdType.MESH
BF16 = jnp.bfloat16
F32 = jnp.float32

GRID = (4, 2, 2)


def place():
    f = lax.axis_index("fsdp")
    return lax.rem(f, 2), lax.rem(f // 2, 2), f // 4, lax.axis_index("tp")


def rank(x, y, z):
    return (z * 2 + y) * 2 + x


def peers(x, y, z, t):
    return (
        [(rank(x, y, lax.rem(z + k, 4)), t) for k in (1, 2, 3)],
        (rank(1 - x, y, z), t),
        (rank(x, 1 - y, z), t),
        (rank(x, y, z), 1 - t),
    )


def meet(devices):
    barrier = pltpu.get_barrier_semaphore()
    for device in devices:
        pl.semaphore_signal(barrier, inc=1, device_id=device, device_id_type=MESH)
    pl.semaphore_wait(barrier, len(devices))


def remote(source, target, send_sem, recv_sem, device):
    return pltpu.make_async_remote_copy(
        src_ref=source,
        dst_ref=target,
        send_sem=send_sem,
        recv_sem=recv_sem,
        device_id=device,
        device_id_type=MESH,
    )


def gather_kernel(chunks, ahead, w_ref, whole, send, recv, own):
    x, y, z, t = place()
    z_peers, x_peer, y_peer, _ = peers(x, y, z, t)
    meet(z_peers + [x_peer, y_peer])
    local = pltpu.make_async_copy(w_ref, whole.at[:, z, y, x], own)
    local.start()
    sends = []

    def go(source, chunk, stage, device):
        copy = remote(source, source, send.at[chunk, stage], recv.at[chunk, stage], device)
        copy.start()
        sends.append(copy)

    def arrive(target, chunk, stage):
        remote(target, target, send.at[chunk, stage], recv.at[chunk, stage], x_peer).wait_recv()

    def along_z(chunk):
        for k in range(3):
            copy = remote(
                w_ref.at[chunk],
                whole.at[chunk, z, y, x],
                send.at[chunk, k],
                recv.at[chunk, k],
                z_peers[k],
            )
            copy.start()
            sends.append(copy)

    def second(chunk):
        for k in range(3):
            arrive(whole.at[chunk, lax.rem(z + 3 - k, 4), y, x], chunk, k)
        go(whole.at[chunk, :, y, x], chunk, 3, x_peer if chunk % 2 else y_peer)

    def third(chunk):
        if chunk % 2:
            arrive(whole.at[chunk, :, y, 1 - x], chunk, 3)
            go(whole.at[chunk, :, y], chunk, 4, y_peer)
        else:
            arrive(whole.at[chunk, :, 1 - y, x], chunk, 3)
            go(whole.at[chunk, :, :, x], chunk, 4, x_peer)

    for chunk in range(min(ahead, chunks)):
        along_z(chunk)
    local.wait()
    for step in range(chunks + 1):
        if step < chunks:
            second(step)
        if step + ahead < chunks:
            along_z(step + ahead)
        if step >= 1:
            third(step - 1)
    for chunk in range(chunks):
        arrive(whole.at[chunk, :, 1 - y] if chunk % 2 else whole.at[chunk, :, :, 1 - x], chunk, 4)
    for copy in sends:
        copy.wait_send()


def scatter_kernel(chunks, g_ref, s_ref, o_ref, os_ref, r1, r2, r3, q1, q2, q3, q4, send, recv, ssend, srecv):
    x, y, z, t = place()
    z_peers, x_peer, y_peer, partner = peers(x, y, z, t)
    meet(z_peers + [x_peer, y_peer, partner])
    sends = []

    def go(source, target, s, r, device):
        copy = remote(source, target, s, r, device)
        copy.start()
        sends.append(copy)

    def arrive(target, s, r):
        remote(target, target, s, r, x_peer).wait_recv()

    def first(chunk):
        go(
            g_ref.at[chunk, :, 1 - y] if chunk % 2 else g_ref.at[chunk, :, :, 1 - x],
            r1.at[chunk],
            send.at[chunk, 0],
            recv.at[chunk, 0],
            y_peer if chunk % 2 else x_peer,
        )

    def second(chunk):
        arrive(r1.at[chunk], send.at[chunk, 0], recv.at[chunk, 0])
        for q in range(4):
            for r in range(2):
                mine = g_ref[chunk, q, y, r] if chunk % 2 else g_ref[chunk, q, r, x]
                r1[chunk, q, r] = (mine.astype(F32) + r1[chunk, q, r].astype(F32)).astype(BF16)
        go(
            r1.at[chunk, :, 1 - x] if chunk % 2 else r1.at[chunk, :, 1 - y],
            r2.at[chunk],
            send.at[chunk, 1],
            recv.at[chunk, 1],
            x_peer if chunk % 2 else y_peer,
        )

    def third(chunk):
        arrive(r2.at[chunk], send.at[chunk, 1], recv.at[chunk, 1])
        for q in range(4):
            mine = r1[chunk, q, x] if chunk % 2 else r1[chunk, q, y]
            r2[chunk, q] = (mine.astype(F32) + r2[chunk, q].astype(F32)).astype(BF16)
        for k in range(3):
            go(
                r2.at[chunk, lax.rem(z + k + 1, 4)],
                r3.at[chunk, k],
                send.at[chunk, 2 + k],
                recv.at[chunk, 2 + k],
                z_peers[k],
            )

    def last(chunk):
        total = r2[chunk, z].astype(F32)
        for k in range(3):
            arrive(r3.at[chunk, k], send.at[chunk, 2 + k], recv.at[chunk, 2 + k])
            total = total + r3[chunk, k].astype(F32)
        o_ref[chunk] = total

    go(s_ref.at[:, :, 1 - x], q1, ssend.at[0], srecv.at[0], x_peer)
    for chunk in range(chunks):
        first(chunk)
    arrive(q1, ssend.at[0], srecv.at[0])
    q1[...] = q1[...] + s_ref[:, :, x]
    go(q1.at[:, 1 - y], q2, ssend.at[1], srecv.at[1], y_peer)
    for step in range(chunks + 4):
        if step < chunks:
            second(step)
        if step == 1:
            arrive(q2, ssend.at[1], srecv.at[1])
            q2[...] = q2[...] + q1[:, y]
            for k in range(3):
                go(q2.at[lax.rem(z + k + 1, 4)], q3.at[k], ssend.at[2 + k], srecv.at[2 + k], z_peers[k])
        if step == 3:
            total = q2[z]
            for k in range(3):
                arrive(q3.at[k], ssend.at[2 + k], srecv.at[2 + k])
                total = total + q3[k]
            q4[0] = total
            go(q4.at[0], q4.at[1], ssend.at[5], srecv.at[5], partner)
        if 0 <= step - 2 < chunks:
            third(step - 2)
        if 0 <= step - 4 < chunks:
            last(step - 4)
    arrive(q4.at[1], ssend.at[5], srecv.at[5])
    os_ref[...] = q4[0] + q4[1]
    for copy in sends:
        copy.wait_send()


VMEM = pl.BlockSpec(memory_space=pltpu.VMEM)
DMA = pltpu.SemaphoreType.DMA


def gather_rows(stack):
    chunks, rows, cols = stack.shape
    ranks = lax.axis_size("fsdp")
    if ranks != 16 or rows % 16:
        return lax.all_gather(stack, "fsdp", axis=1, tiled=True)
    whole = pl.pallas_call(
        partial(gather_kernel, chunks, 3),
        name="gather_rows",
        out_shape=jax.ShapeDtypeStruct((chunks,) + GRID + (rows, cols), stack.dtype),
        in_specs=[VMEM],
        out_specs=VMEM,
        scratch_shapes=[DMA((chunks, 5)), DMA((chunks, 5)), DMA],
        compiler_params=pltpu.CompilerParams(
            collective_id=0, has_side_effects=True, vmem_limit_bytes=40 << 20
        ),
    )(stack)
    return whole.reshape(chunks, ranks * rows, cols)


def scatter_rows(stack, small):
    chunks, rows, cols = stack.shape
    ranks = lax.axis_size("fsdp")
    rows //= ranks
    if ranks != 16 or rows % 16:
        return (
            lax.psum_scatter(stack, "fsdp", scatter_dimension=1, tiled=True),
            lax.psum(lax.psum_scatter(small, "fsdp", scatter_dimension=0, tiled=True), "tp")[0],
        )
    stack = stack.astype(BF16).reshape((chunks,) + GRID + (rows, cols))
    small = small.reshape(GRID + small.shape[1:])
    tail = small.shape[3:]
    return pl.pallas_call(
        partial(scatter_kernel, chunks),
        name="scatter_rows",
        out_shape=(
            jax.ShapeDtypeStruct((chunks, rows, cols), F32),
            jax.ShapeDtypeStruct(tail, F32),
        ),
        in_specs=[VMEM, VMEM],
        out_specs=(VMEM, VMEM),
        scratch_shapes=[
            pltpu.VMEM((chunks, 4, 2, rows, cols), BF16),
            pltpu.VMEM((chunks, 4, rows, cols), BF16),
            pltpu.VMEM((chunks, 3, rows, cols), BF16),
            pltpu.VMEM((4, 2) + tail, F32),
            pltpu.VMEM((4,) + tail, F32),
            pltpu.VMEM((3,) + tail, F32),
            pltpu.VMEM((2,) + tail, F32),
            DMA((chunks, 5)),
            DMA((chunks, 5)),
            DMA((6,)),
            DMA((6,)),
        ],
        compiler_params=pltpu.CompilerParams(
            collective_id=1, has_side_effects=True, vmem_limit_bytes=48 << 20
        ),
    )(stack, small)


def split_cols(matrix, cols):
    rows = matrix.shape[0]
    return jnp.moveaxis(matrix.reshape(rows, -1, cols), 1, 0)


def join_cols(chunks):
    return jnp.moveaxis(chunks, 0, 1).reshape(chunks.shape[1], -1)


norm_eps = 1e-05


def layer_norm(values, gain, shift):
    center = values - jnp.mean(values, -1, keepdims=True)
    spread = jnp.mean(center * center, -1, keepdims=True)
    return center * lax.rsqrt(spread + norm_eps) * gain + shift


def to_heads(merged, head_count):
    lead = merged.shape[:-3]
    seq_count, length, model_cols = merged.shape[-3:]
    split = merged.reshape(lead + (seq_count, length, head_count, model_cols // head_count))
    split = jnp.moveaxis(split, -2, -3)
    return split.reshape(lead + (seq_count * head_count, length, model_cols // head_count))


def from_heads(split, seq_count):
    lead = split.shape[:-3]
    rows_heads, length, head_size = split.shape[-3:]
    head_count = rows_heads // seq_count
    merged = split.reshape(lead + (seq_count, head_count, length, head_size))
    merged = jnp.moveaxis(merged, -3, -2)
    return merged.reshape(lead + (seq_count, length, head_count * head_size))


def causal_block(begin_row, block_rows, end_row):
    rows_at = begin_row + jnp.arange(block_rows)
    cols_at = jnp.arange(end_row)
    return rows_at[:, None] >= cols_at[None, :]


def attend(pieces):
    q_feat, k_feat, values = pieces
    length = q_feat.shape[0]
    block_rows = min(512, length)
    weighted = []
    totals = []
    for begin_row in range(0, length, block_rows):
        end_row = begin_row + block_rows
        scores = jnp.einsum(
            "if,jf->ij",
            q_feat[begin_row:end_row],
            k_feat[:end_row],
            preferred_element_type=jnp.float32,
        )
        scores = jnp.where(causal_block(begin_row, block_rows, end_row), scores, 0.0)
        totals.append(jnp.sum(scores, 1))
        weighted.append(
            jnp.dot(
                scores.astype(jnp.bfloat16), values[:end_row], preferred_element_type=jnp.float32
            )
        )
    return (jnp.concatenate(weighted, 0), jnp.concatenate(totals, 0))


def attend_back(pieces):
    q_feat, k_feat, values, d_weighted, d_totals = pieces
    length, feat_size = k_feat.shape
    block_rows = min(512, length)
    d_query = []
    d_key = jnp.zeros((length, feat_size), jnp.float32)
    d_value = jnp.zeros(values.shape, jnp.float32)
    for begin_row in range(0, length, block_rows):
        end_row = begin_row + block_rows
        causal_mask = causal_block(begin_row, block_rows, end_row)
        rows_query = q_feat[begin_row:end_row]
        rows_grad = d_weighted[begin_row:end_row]
        scores = jnp.einsum(
            "if,jf->ij", rows_query, k_feat[:end_row], preferred_element_type=jnp.float32
        )
        scores_low = jnp.where(causal_mask, scores, 0.0).astype(jnp.bfloat16)
        grad_scores = (
            jnp.einsum("ie,je->ij", rows_grad, values[:end_row], preferred_element_type=jnp.float32)
            + d_totals[begin_row:end_row, None]
        )
        grad_scores = jnp.where(causal_mask, grad_scores, 0.0).astype(jnp.bfloat16)
        d_query.append(jnp.dot(grad_scores, k_feat[:end_row], preferred_element_type=jnp.float32))
        d_key = d_key.at[:end_row].add(
            jnp.einsum("ij,if->jf", grad_scores, rows_query, preferred_element_type=jnp.float32)
        )
        d_value = d_value.at[:end_row].add(
            jnp.einsum("ij,ie->je", scores_low, rows_grad, preferred_element_type=jnp.float32)
        )
    return (jnp.concatenate(d_query, 0), d_key, d_value)


def position_weights(length):
    angles = jnp.pi / 2.0 * jnp.arange(length, dtype=jnp.float32) / length
    return (jnp.cos(angles)[:, None], jnp.sin(angles)[:, None])


def fetch_params(
    query_key_value_weight,
    attention_out_weight,
    up_weight,
    down_weight,
    qk_bias,
    value_bias,
    out_bias,
    ffn_in_bias,
    ffn_out_bias,
    norm_gains,
    norm_biases,
):
    col_part = query_key_value_weight.shape[2]
    hidden_chunks = up_weight.shape[1] // col_part
    rows = query_key_value_weight.shape[1]
    small = jnp.concatenate(
        [
            v.reshape(-1, rows)
            for v in (qk_bias, value_bias, out_bias, ffn_in_bias, ffn_out_bias, norm_gains, norm_biases)
        ],
        0,
    )
    small = jnp.pad(small.T, ((0, 0), (0, col_part - small.shape[0])))
    stack = jnp.concatenate(
        [
            small[None],
            query_key_value_weight,
            attention_out_weight.T[None],
            split_cols(up_weight, col_part),
            split_cols(down_weight.T, col_part),
        ],
        0,
    )
    whole = gather_rows(stack)
    small = whole[0].T
    hidden = ffn_in_bias.shape[0] // rows
    ranks = lax.axis_size("fsdp")
    in_bias = small[4 : 4 + hidden].reshape(hidden, ranks, rows)
    in_bias = jnp.moveaxis(in_bias, 1, 0).reshape(-1)
    after = 4 + hidden
    return (
        whole[1:4],
        whole[4].T,
        join_cols(whole[5 : 5 + hidden_chunks]),
        join_cols(whole[5 + hidden_chunks :]).T,
        small[0:2],
        small[2],
        small[3],
        in_bias,
        small[after],
        small[after + 1 : after + 3],
        small[after + 3 : after + 5],
    )


def run_forward(params, inputs):
    (
        query_key_value_weight,
        attention_out_weight,
        up_weight,
        down_weight,
        qk_bias,
        value_bias,
        out_bias,
        ffn_in_bias,
        ffn_out_bias,
        norm_gains,
        norm_biases,
    ) = params
    col_part = query_key_value_weight.shape[2]
    hidden_part = up_weight.shape[1]
    head_count = col_part // HEAD_DIM
    tp_place = lax.axis_index("tp")
    collected_rows = lax.all_gather(inputs, "tp", axis=1, tiled=True)
    seq_count, length = (collected_rows.shape[0], collected_rows.shape[1])
    proj_bias = jnp.concatenate(
        [
            lax.dynamic_slice_in_dim(qk_bias, tp_place * col_part, col_part, 1),
            lax.dynamic_slice_in_dim(value_bias[None, :], tp_place * col_part, col_part, 1),
        ],
        0,
    ).astype(jnp.float32)
    projected = (
        jnp.einsum(
            "ugn,anr->augr",
            collected_rows,
            query_key_value_weight,
            preferred_element_type=jnp.float32,
        )
        + proj_bias[:, None, None, :]
    )
    by_head = to_heads(projected, head_count)
    cosine, sine_w = position_weights(length)
    rect_query = jax.nn.relu(by_head[0])
    rect_key = jax.nn.relu(by_head[1])
    q_feat = jnp.concatenate([rect_query * cosine, rect_query * sine_w], -1).astype(jnp.bfloat16)
    k_feat = jnp.concatenate([rect_key * cosine, rect_key * sine_w], -1).astype(jnp.bfloat16)
    values = by_head[2].astype(jnp.bfloat16)
    weighted, totals = lax.map(attend, (q_feat, k_feat, values))
    context_rows = from_heads(weighted / jnp.maximum(totals, 1.0)[..., None], seq_count).astype(
        jnp.bfloat16
    )
    attention_partial_sum = jnp.einsum(
        "rtq,qj->rtj", context_rows, attention_out_weight, preferred_element_type=jnp.float32
    )
    attended = lax.psum_scatter(
        attention_partial_sum, "tp", scatter_dimension=1, tiled=True
    ) + out_bias.astype(jnp.float32)
    resid_one = inputs.astype(jnp.float32) + attended
    gains = norm_gains.astype(jnp.float32)
    shifts = norm_biases.astype(jnp.float32)
    normed_one = layer_norm(resid_one, gains[0], shifts[0])
    normalized_rows = lax.all_gather(normed_one.astype(jnp.bfloat16), "tp", axis=1, tiled=True)
    hidden_bias = lax.dynamic_slice_in_dim(ffn_in_bias, tp_place * hidden_part, hidden_part, 0)
    hidden_pre = jnp.einsum(
        "xwq,qp->xwp", normalized_rows, up_weight, preferred_element_type=jnp.float32
    ) + hidden_bias.astype(jnp.float32)
    hidden_activation = jax.nn.gelu(hidden_pre, approximate=False).astype(jnp.bfloat16)
    feedforward_partial_sum = jnp.einsum(
        "pem,mn->pen", hidden_activation, down_weight, preferred_element_type=jnp.float32
    )
    resid_two = (
        normed_one
        + lax.psum_scatter(feedforward_partial_sum, "tp", scatter_dimension=1, tiled=True)
        + ffn_out_bias.astype(jnp.float32)
    )
    result = layer_norm(resid_two, gains[1], shifts[1])
    return (
        result,
        collected_rows,
        by_head,
        q_feat,
        k_feat,
        values,
        weighted,
        totals,
        context_rows,
        resid_one,
        normed_one,
        normalized_rows,
        hidden_pre,
        hidden_activation,
        resid_two,
    )


def shards(
    inputs,
    query_key_value_weight,
    attention_out_weight,
    up_weight,
    down_weight,
    qk_bias,
    value_bias,
    out_bias,
    ffn_in_bias,
    ffn_out_bias,
    norm_gains,
    norm_biases,
    grad_out,
):
    params_back = fetch_params(
        query_key_value_weight,
        attention_out_weight,
        up_weight,
        down_weight,
        qk_bias,
        value_bias,
        out_bias,
        ffn_in_bias,
        ffn_out_bias,
        norm_gains,
        norm_biases,
    )
    (
        result,
        collected_rows,
        by_head,
        q_feat,
        k_feat,
        values,
        weighted,
        totals,
        context_rows,
        resid_one,
        normed_one,
        normalized_rows,
        hidden_pre,
        hidden_activation,
        resid_two,
    ) = run_forward(params_back, inputs)
    output = result.astype(jnp.bfloat16)
    (
        gathered_query_key_value,
        gathered_out_weight,
        gathered_up_weight,
        gathered_down_weight,
        full_qk_bias,
        full_value_bias,
        full_out_bias,
        full_ffn_in,
        full_ffn_out,
        full_gains,
        full_shifts,
    ) = params_back
    col_part = gathered_query_key_value.shape[2]
    hidden_part = gathered_up_weight.shape[1]
    model_width = inputs.shape[2]
    seq_count, length = (collected_rows.shape[0], collected_rows.shape[1])
    tp_place = lax.axis_index("tp")
    gains = full_gains.astype(jnp.float32)
    shifts = full_shifts.astype(jnp.float32)
    primal_two, second_back = jax.vjp(layer_norm, resid_two, gains[1], shifts[1])
    d_resid_two, d_gain_two, d_shift_two = second_back(grad_out.astype(jnp.float32))
    d_branch = d_resid_two.astype(jnp.bfloat16)
    d_ffn_out = jnp.sum(d_branch.astype(jnp.float32), (0, 1))
    branch_row_gradient = lax.all_gather(d_branch, "tp", axis=1, tiled=True)
    d_activated = jnp.einsum(
        "rcw,ew->rce", branch_row_gradient, gathered_down_weight, preferred_element_type=jnp.float32
    )
    grad_down = jnp.einsum(
        "job,joe->be", hidden_activation, branch_row_gradient, preferred_element_type=jnp.float32
    )
    primal_gelu, gelu_back = jax.vjp(partial(jax.nn.gelu, approximate=False), hidden_pre)
    hidden_gradient = gelu_back(d_activated)[0].astype(jnp.bfloat16)
    d_ffn_in = lax.dynamic_update_slice_in_dim(
        jnp.zeros((hidden_part * lax.axis_size("tp"),), jnp.float32),
        jnp.sum(hidden_gradient.astype(jnp.float32), (0, 1)),
        tp_place * hidden_part,
        0,
    )
    up_weight_gradient = jnp.einsum(
        "auf,aub->fb", normalized_rows, hidden_gradient, preferred_element_type=jnp.float32
    )
    normed_part_gradient = jnp.einsum(
        "oiu,ru->oir", hidden_gradient, gathered_up_weight, preferred_element_type=jnp.float32
    )
    d_normed = d_resid_two + lax.psum_scatter(
        normed_part_gradient, "tp", scatter_dimension=1, tiled=True
    )
    primal_one, first_back = jax.vjp(layer_norm, resid_one, gains[0], shifts[0])
    d_resid_one, d_gain_one, d_shift_one = first_back(d_normed)
    d_attended = d_resid_one.astype(jnp.bfloat16)
    d_out_bias = jnp.sum(d_attended.astype(jnp.float32), (0, 1))
    attention_row_gradient = lax.all_gather(d_attended, "tp", axis=1, tiled=True)
    d_context = to_heads(
        jnp.einsum(
            "prq,fq->prf",
            attention_row_gradient,
            gathered_out_weight,
            preferred_element_type=jnp.float32,
        ),
        col_part // HEAD_DIM,
    )
    grad_out_proj = jnp.einsum(
        "etz,etb->zb", context_rows, attention_row_gradient, preferred_element_type=jnp.float32
    )
    floor_den = jnp.maximum(totals, 1.0)
    d_weighted = (d_context / floor_den[..., None]).astype(jnp.bfloat16)
    d_totals = jnp.where(totals > 1.0, -jnp.sum(d_context * weighted, -1) / (totals * totals), 0.0)
    d_query, d_key, d_value = lax.map(attend_back, (q_feat, k_feat, values, d_weighted, d_totals))
    cosine, sine_w = position_weights(length)
    d_pre_query = (d_query[..., :HEAD_DIM] * cosine + d_query[..., HEAD_DIM:] * sine_w) * (
        by_head[0] > 0
    )
    d_pre_key = (d_key[..., :HEAD_DIM] * cosine + d_key[..., HEAD_DIM:] * sine_w) * (by_head[1] > 0)
    projected_gradient = from_heads(
        jnp.stack([d_pre_query, d_pre_key, d_value], 0), seq_count
    ).astype(jnp.bfloat16)
    d_proj_bias = jnp.sum(projected_gradient.astype(jnp.float32), (1, 2))
    d_qk_bias = lax.dynamic_update_slice_in_dim(
        jnp.zeros((2, model_width), jnp.float32), d_proj_bias[:2], tp_place * col_part, 1
    )
    d_value_bias = lax.dynamic_update_slice_in_dim(
        jnp.zeros((model_width,), jnp.float32), d_proj_bias[2], tp_place * col_part, 0
    )
    grad_qkv = jnp.einsum(
        "bkr,gbkn->grn", collected_rows, projected_gradient, preferred_element_type=jnp.float32
    )
    d_input_part = jnp.einsum(
        "chxr,cqr->hxq",
        projected_gradient,
        gathered_query_key_value,
        preferred_element_type=jnp.float32,
    )
    grad_input = d_resid_one + lax.psum_scatter(
        d_input_part.astype(jnp.bfloat16), "tp", scatter_dimension=1, tiled=True
    ).astype(jnp.float32)
    ranks = lax.axis_size("fsdp")
    rows = model_width // ranks
    small = jnp.concatenate(
        [
            jnp.moveaxis(v.reshape(-1, ranks, rows), 1, 0)
            for v in (
                d_qk_bias,
                d_value_bias,
                d_out_bias,
                d_ffn_out,
                d_gain_one,
                d_gain_two,
                d_shift_one,
                d_shift_two,
            )
        ]
        + [d_ffn_in.reshape(ranks, -1, rows)],
        1,
    )
    kinds = small.shape[1]
    small = jnp.pad(small.reshape(ranks, -1), ((0, 0), (0, 1024 - kinds * rows)))
    stack = jnp.concatenate(
        [
            grad_qkv,
            grad_out_proj.T[None],
            split_cols(up_weight_gradient, col_part),
            split_cols(grad_down.T, col_part),
        ],
        0,
    )
    owned, small = scatter_rows(stack, small.reshape(ranks, 8, 128))
    small = small.reshape(-1)[: kinds * rows].reshape(kinds, rows)
    hidden_chunks = hidden_part // col_part
    return (
        output,
        grad_input,
        owned[:3],
        owned[3].T,
        join_cols(owned[4 : 4 + hidden_chunks]),
        join_cols(owned[4 + hidden_chunks :]).T,
        small[:2],
        small[2],
        small[3],
        small[9:].reshape(-1),
        small[4],
        small[5:7],
        small[7:9],
    )


def solution(mesh):
    return jax.shard_map(
        shards,
        mesh=mesh,
        in_specs=(
            P("fsdp", "tp", None),
            P(None, "fsdp", "tp"),
            P("tp", "fsdp"),
            P("fsdp", "tp"),
            P("tp", "fsdp"),
            P(None, "fsdp"),
            P("fsdp"),
            P("fsdp"),
            P("fsdp"),
            P("fsdp"),
            P(None, "fsdp"),
            P(None, "fsdp"),
            P("fsdp", "tp", None),
        ),
        out_specs=(
            P("fsdp", "tp", None),
            P("fsdp", "tp", None),
            P(None, "fsdp", "tp"),
            P("tp", "fsdp"),
            P("fsdp", "tp"),
            P("tp", "fsdp"),
            P(None, "fsdp"),
            P("fsdp"),
            P("fsdp"),
            P("fsdp"),
            P("fsdp"),
            P(None, "fsdp"),
            P(None, "fsdp"),
        ),
        check_vma=False,
    )
```

```python
from functools import partial

import jax
import jax.numpy as jnp
import numpy as np
from jax import lax
from jax.experimental import pallas as pl
from jax.experimental.pallas import tpu as pltpu
from jax.sharding import PartitionSpec as P

HEAD_DIM = 64
EPS = 1e-05
MESH = pl.DeviceIdType.MESH
BF16 = jnp.bfloat16
F32 = jnp.float32
TILE = 256
PIECE = 384
SMALL_ROWS = 32
QK_BIAS, VALUE_BIAS, OUT_BIAS, OUT2_BIAS, GAINS, SHIFTS, IN_BIAS = 0, 4, 6, 8, 10, 14, 18
AHEAD = 4


def nn(a, b):
    return jnp.dot(a, b, preferred_element_type=F32)


def nt(a, b):
    return lax.dot_general(a, b, (((1,), (1,)), ((), ())), preferred_element_type=F32)


def tn(a, b):
    return lax.dot_general(a, b, (((0,), (0,)), ((), ())), preferred_element_type=F32)


def place():
    f = lax.axis_index("fsdp")
    return lax.rem(f, 2), lax.rem(f // 2, 2), f // 4, lax.axis_index("tp")


def rank(x, y, z):
    return (z * 2 + y) * 2 + x


def meet(devices):
    barrier = pltpu.get_barrier_semaphore()
    for device in devices:
        pl.semaphore_signal(barrier, inc=1, device_id=device, device_id_type=MESH)
    pl.semaphore_wait(barrier, len(devices))


def remote(source, target, send_sem, recv_sem, device):
    return pltpu.make_async_remote_copy(
        src_ref=source,
        dst_ref=target,
        send_sem=send_sem,
        recv_sem=recv_sem,
        device_id=device,
        device_id_type=MESH,
    )


class Sends:
    def __init__(self):
        self.copies = []

    def start(self, *args):
        copy = remote(*args)
        copy.start()
        self.copies.append(copy)
        return copy

    def settle(self, copies):
        for copy in copies:
            copy.wait_send()
        self.copies = [c for c in self.copies if not any(c is copy for copy in copies)]

    def finish(self):
        self.settle(list(self.copies))


class Gather:
    def __init__(self, pieces, where, send, recv, sends):
        self.pieces, self.send, self.recv, self.sends = pieces, send, recv, sends
        self.x, self.y, self.z, t = where
        x, y, z = self.x, self.y, self.z
        self.z_peers = [(rank(x, y, lax.rem(z + k, 4)), t) for k in (1, 2, 3)]
        self.x_peer, self.y_peer = (rank(1 - x, y, z), t), (rank(x, 1 - y, z), t)
        count = len(pieces)
        self.steps = []
        for step in range(count + 1):
            if step < count:
                self.steps.append(partial(self.second, step))
            if step + AHEAD < count:
                self.steps.append(partial(self.along_z, step + AHEAD))
            if step >= 1:
                self.steps.append(partial(self.third, step - 1))
        self.done_at = {}
        self.at = 0
        self.finished = set()

    def begin(self):
        for piece in range(min(AHEAD, len(self.pieces))):
            self.along_z(piece)

    def view(self, piece, *index):
        _, whole, cols = self.pieces[piece]
        return whole.at[(*index, slice(None), cols)]

    def sems(self, piece, stage):
        return self.send.at[piece, stage], self.recv.at[piece, stage]

    def arrive(self, piece, stage, *index):
        target = self.view(piece, *index)
        remote(target, target, *self.sems(piece, stage), self.x_peer).wait_recv()

    def along_z(self, piece):
        slab, _, cols = self.pieces[piece]
        for k in range(3):
            self.sends.start(
                slab.at[:, cols],
                self.view(piece, self.z, self.y, self.x),
                *self.sems(piece, k),
                self.z_peers[k],
            )

    def second(self, piece):
        for k in range(3):
            self.arrive(piece, k, lax.rem(self.z + 3 - k, 4), self.y, self.x)
        own = self.view(piece, slice(None), self.y, self.x)
        self.sends.start(own, own, *self.sems(piece, 3), self.x_peer if piece % 2 else self.y_peer)

    def third(self, piece):
        if piece % 2:
            self.arrive(piece, 3, slice(None), self.y, 1 - self.x)
            own = self.view(piece, slice(None), self.y, slice(None))
        else:
            self.arrive(piece, 3, slice(None), 1 - self.y, self.x)
            own = self.view(piece, slice(None), slice(None), self.x)
        self.sends.start(own, own, *self.sems(piece, 4), self.y_peer if piece % 2 else self.x_peer)

    def pump(self, count):
        for step in self.steps[self.at : self.at + count]:
            step()
        self.at = min(self.at + count, len(self.steps))

    def need(self, piece):
        while self.at < len(self.steps) and any(
            step.func == self.third and step.args[0] <= piece for step in self.steps[self.at :]
        ):
            self.pump(1)
        for p in range(piece + 1):
            if p not in self.finished:
                self.finished.add(p)
                if p % 2:
                    self.arrive(p, 4, slice(None), 1 - self.y, slice(None))
                else:
                    self.arrive(p, 4, slice(None), slice(None), 1 - self.x)


class Scatter:
    def __init__(self, pieces, where, r1, r2, r3, send, recv, sends):
        self.pieces, self.r1, self.r2, self.r3 = pieces, r1, r2, r3
        self.send, self.recv, self.sends = send, recv, sends
        self.x, self.y, self.z, t = where
        x, y, z = self.x, self.y, self.z
        self.z_peers = [(rank(x, y, lax.rem(z + k, 4)), t) for k in (1, 2, 3)]
        self.x_peer, self.y_peer = (rank(1 - x, y, z), t), (rank(x, 1 - y, z), t)
        self.steps = []
        count = len(pieces)
        self.stage = [0] * count
        self.order = []

    def sems(self, piece, stage):
        return self.send.at[piece, stage], self.recv.at[piece, stage]

    def arrive(self, target, piece, stage):
        remote(target, target, *self.sems(piece, stage), self.x_peer).wait_recv()

    def part(self, piece, *index):
        grads, cols, _ = self.pieces[piece]
        return grads.at[(*index, slice(None), cols)]

    def first(self, piece):
        every = slice(None)
        source = (
            self.part(piece, every, 1 - self.y, every)
            if piece % 2
            else self.part(piece, every, every, 1 - self.x)
        )
        self.sends.start(
            source, self.r1.at[piece], *self.sems(piece, 0), self.y_peer if piece % 2 else self.x_peer
        )
        self.order.append(piece)
        n = len(self.order)
        self.steps.append(partial(self.second, piece))
        if n > 1:
            self.steps.append(partial(self.third, self.order[n - 2]))
        if n > 3:
            self.steps.append(partial(self.last, self.order[n - 4]))

    def second(self, piece):
        self.arrive(self.r1.at[piece], piece, 0)
        grads, cols, _ = self.pieces[piece]
        for q in range(4):
            for r in range(2):
                mine = grads[q, self.y, r, :, cols] if piece % 2 else grads[q, r, self.x, :, cols]
                self.r1[piece, q, r] = (mine.astype(F32) + self.r1[piece, q, r].astype(F32)).astype(BF16)
        other = self.r1.at[piece, :, 1 - self.x] if piece % 2 else self.r1.at[piece, :, 1 - self.y]
        self.sends.start(
            other, self.r2.at[piece], *self.sems(piece, 1), self.x_peer if piece % 2 else self.y_peer
        )

    def third(self, piece):
        self.arrive(self.r2.at[piece], piece, 1)
        for q in range(4):
            mine = self.r1[piece, q, self.x] if piece % 2 else self.r1[piece, q, self.y]
            self.r2[piece, q] = (mine.astype(F32) + self.r2[piece, q].astype(F32)).astype(BF16)
        for k in range(3):
            self.sends.start(
                self.r2.at[piece, lax.rem(self.z + k + 1, 4)],
                self.r3.at[piece, k],
                *self.sems(piece, 2 + k),
                self.z_peers[k],
            )

    def last(self, piece):
        total = self.r2[piece, self.z].astype(F32)
        for k in range(3):
            self.arrive(self.r3.at[piece, k], piece, 2 + k)
            total = total + self.r3[piece, k].astype(F32)
        self.pieces[piece][2](total)

    def pump(self, count):
        for step in self.steps[:count]:
            step()
        self.steps = self.steps[count:]

    def finish(self):
        n = len(self.order)
        self.steps.append(partial(self.third, self.order[n - 1]))
        for k in range(max(n - 3, 0), n):
            self.steps.append(partial(self.last, self.order[k]))
        self.pump(len(self.steps))


def layer_kernel(fused, names, *refs):
    r = dict(zip(names, refs))
    where = x, y, z, t = place()
    partner = (lax.axis_index("fsdp"), 1 - t)
    sends = Sends()
    gy, xs = r["grad_out"], r["inputs"]
    wqkv, wo, wup, wdn = r["wqkv"], r["wo"], r["wup"], r["wdn"]
    gqkv, go, gup, gdn = r["gqkv"], r["go"], r["gup"], r["gdn"]
    X, HB, DF = r["X"], r["HB"], r["DF"]
    DATT = DF
    FQ, FK, VA, SS, DN = r["FQ"], r["FK"], r["VA"], r["SS"], r["DN"]
    DEN, CTX, N1, RS1, DR = r["DEN"], r["CTX"], r["N1"], r["RS1"], r["DR"]
    ACT, GP, DPRE, SB, RB = r["ACT"], r["GP"], r["DPRE"], r["SB"], r["RB"]
    BV, SG, table = r["BV"], r["SG"], r["table"]
    tps, tpr = r["tps"], r["tpr"]
    length, width = X.shape
    local = length // 2
    tiles = local // TILE
    cols = wo.shape[-1]
    hidden = wup.shape[-1]
    pairs = cols // 128
    chunks = length // TILE
    halves = hidden // (2 * PIECE)
    mine, other = t * local, (1 - t) * local

    def rows_at(base, tile):
        return pl.ds(pl.multiple_of(base + tile * TILE, TILE), TILE)

    passed = {}

    def to_partner(source, target, index):
        passed[index] = sends.start(source, target, tps.at[index], tpr.at[index], partner)

    def leave(first):
        sends.settle([passed[first + tile] for tile in range(tiles)])

    def from_partner(target, index):
        remote(target, target, tps.at[index], tpr.at[index], partner).wait_recv()

    def flat(ref, begin=0, size=None):
        size = ref.shape[-1] if size is None else size
        return ref[:, :, :, :, begin : begin + size].reshape(width, size)

    if fused:
        x_peer, y_peer = (rank(1 - x, y, z), t), (rank(x, 1 - y, z), t)
        z_peers = [(rank(x, y, lax.rem(z + k, 4)), t) for k in (1, 2, 3)]
        meet(z_peers + [x_peer, y_peer, partner])
        sl = r["small"]
        span = [slice(k * PIECE, (k + 1) * PIECE) for k in range(max(pairs, 2 * halves))]
        sources = (
            [(sl, r["SM"], span[0])]
            + [(r["sqkv"], wqkv, span[p]) for p in range(pairs)]
            + [(r["so"], wo, span[0])]
            + [(r["sup"], wup, span[k]) for k in range(2 * halves)]
            + [(r["sdn"], wdn, span[k]) for k in range(2 * halves)]
        )
        gather = Gather(sources, where, r["ags"], r["agr"], sends)
        first_up = 2 + pairs
        first_dn = first_up + 2 * halves
        gather.begin()
        own = []
        for k, (slab, whole) in enumerate(
            [(sl, r["SM"]), (r["sqkv"], wqkv), (r["so"], wo), (r["sup"], wup), (r["sdn"], wdn)]
        ):
            own.append(pltpu.make_async_copy(slab, whole.at[z, y, x], r["own"].at[k]))
            own[-1].start()
        pump_in, need = gather.pump, gather.need
    else:
        meet([partner])
        first_up = first_dn = 0
        pump_in = need = lambda count: None

    here = pltpu.make_async_copy(xs.at[0], X.at[pl.ds(mine, local)], r["own"].at[5])
    here.start()
    to_partner(xs.at[0], X.at[pl.ds(mine, local)], 0)
    if fused:
        for copy in own:
            copy.wait()
    here.wait()
    SG[...] = jnp.zeros_like(SG)
    r["SI"][...] = jnp.zeros_like(r["SI"])
    pump_in(1)
    from_partner(X.at[pl.ds(other, local)], 0)

    lane = lax.broadcasted_iota(jnp.int32, (TILE, 128), 1)
    low = lane < 64

    def swap(v):
        return pltpu.roll(v, 64, 1)

    need(0)
    if fused:
        total = jnp.zeros((SMALL_ROWS, PIECE), F32)
        for a in range(4):
            for b in range(2):
                for c in range(2):
                    total = total + r["SM"][a, b, c].astype(F32)
        BV[...] = total
    else:
        BV[...] = r["small"][...]

    def small_row(row):
        return jnp.concatenate([BV[row : row + 1, :], BV[row + 1 : row + 2, :]], 1)

    def own_half(row):
        return jnp.where(t == 0, BV[row : row + 1, :], BV[row + 1 : row + 2, :])

    out_bias, out2_bias = small_row(OUT_BIAS), small_row(OUT2_BIAS)
    gain0, gain1 = small_row(GAINS), small_row(GAINS + 2)
    shift0, shift1 = small_row(SHIFTS), small_row(SHIFTS + 2)
    in_bias = []
    for j in range(halves):
        at = IN_BIAS + 2 * j
        in_bias.append(
            jnp.where(t == 0, small_row(at), small_row(at + 2 * halves))
        )
    bq, bk, bv = own_half(QK_BIAS), own_half(QK_BIAS + 2), own_half(VALUE_BIAS)

    for p in range(pairs):
        need(1 + p)
        at = p * 128

        @pl.loop(0, chunks)
        def _(i):
            rows = rows_at(0, i)
            pre = nn(X[rows, :], flat(wqkv, p * 384, 384))
            cs = table[rows, :]
            q = jnp.maximum(pre[:, :128] + bq[:, at : at + 128], 0.0)
            k = jnp.maximum(pre[:, 128:256] + bk[:, at : at + 128], 0.0)
            v = pre[:, 256:] + bv[:, at : at + 128]
            qs, ks, vs = swap(q), swap(k), swap(v)
            FQ[2 * p, rows, :] = (jnp.where(low, q, qs) * cs).astype(BF16)
            FQ[2 * p + 1, rows, :] = (jnp.where(low, qs, q) * cs).astype(BF16)
            FK[2 * p, rows, :] = (jnp.where(low, k, ks) * cs).astype(BF16)
            FK[2 * p + 1, rows, :] = (jnp.where(low, ks, k) * cs).astype(BF16)
            VA[2 * p, rows, :] = jnp.where(low, v, 1.0).astype(BF16)
            VA[2 * p + 1, rows, :] = jnp.where(low, vs, 1.0).astype(BF16)

        pump_in(1)

        def attend(i, states):
            rows = rows_at(0, i)
            ahead = lax.broadcasted_iota(jnp.int32, (TILE, TILE), 0) >= lax.broadcasted_iota(
                jnp.int32, (TILE, TILE), 1
            )
            both, after = [], []
            for h in range(2):
                q, k, va = FQ[2 * p + h, rows, :], FK[2 * p + h, rows, :], VA[2 * p + h, rows, :]
                before = states[h].astype(BF16)
                SS[2 * p + h, i] = before
                scores = jnp.where(ahead, nt(q, k), 0.0).astype(BF16)
                both.append(nn(scores, va) + nn(q, before))
                after.append(states[h] + tn(k, va))
            num = jnp.where(low, both[0], swap(both[1]))
            den = jnp.where(low, swap(both[0]), both[1])
            DEN[rows, at : at + 128] = den
            CTX[rows, at : at + 128] = (num / jnp.maximum(den, 1.0)).astype(BF16)
            return tuple(after)

        start = (jnp.zeros((128, 128), F32), jnp.zeros((128, 128), F32))
        lax.fori_loop(0, chunks, attend, start)
        pump_in(2)

    need(1 + pairs)
    for tile in range(tiles):
        rows = rows_at(other, tile)
        SB[0, tile] = nt(CTX[rows, :], flat(wo)).astype(BF16)
        to_partner(SB.at[0, tile], RB.at[0, tile], 1 + tile)
    pump_in(1)
    for tile in range(tiles):
        rows, here_rows = rows_at(mine, tile), rows_at(0, tile)
        part = nt(CTX[rows, :], flat(wo))
        from_partner(RB.at[0, tile], 1 + tile)
        resid = X[rows, :].astype(F32) + (part + RB[0, tile].astype(F32) + out_bias)
        center = resid - jnp.mean(resid, -1, keepdims=True)
        rstd = lax.rsqrt(jnp.mean(center * center, -1, keepdims=True) + EPS)
        normed = center * rstd
        N1[here_rows, :] = normed
        RS1[here_rows, :] = jnp.broadcast_to(rstd, (TILE, 128))
        HB[rows, :] = (normed * gain0 + shift0).astype(BF16)
        to_partner(HB.at[rows], HB.at[rows], 3 + tile)
        pump_in(1)

    for j in range(halves):
        need(first_up + 2 * j + 1)
        for half in range(2):
            if j == 0 and half == 1:
                for tile in range(tiles):
                    from_partner(HB.at[rows_at(other, tile)], 3 + tile)
            begin = j * 2 * PIECE

            @pl.loop(0, tiles)
            def _(tile):
                rows = rows_at(other if half else mine, tile)
                u = nn(HB[rows, :], flat(wup, begin, 2 * PIECE)) + in_bias[j]
                cdf = 0.5 * (1.0 + lax.erf(u * np.float32(0.5**0.5)))
                pdf = jnp.exp(-0.5 * u * u) * np.float32((2.0 * np.pi) ** -0.5)
                ACT[rows, begin : begin + 2 * PIECE] = (u * cdf).astype(BF16)
                GP[rows, begin : begin + 2 * PIECE] = (cdf + u * pdf).astype(BF16)

            pump_in(3)

    if fused:
        need(first_dn + 2 * halves - 1)
    for tile in range(tiles):
        rows = rows_at(other, tile)
        SB[1, tile] = nt(ACT[rows, :], flat(wdn)).astype(BF16)
        to_partner(SB.at[1, tile], RB.at[1, tile], 5 + tile)
    sum_df = jnp.zeros((1, width), F32)
    sum_gy, sum_gn = sum_df, sum_df
    for tile in range(tiles):
        rows, here_rows = rows_at(mine, tile), rows_at(0, tile)
        part = nt(ACT[rows, :], flat(wdn))
        from_partner(RB.at[1, tile], 5 + tile)
        h1 = N1[here_rows, :] * gain0 + shift0
        resid = h1 + (part + RB[1, tile].astype(F32)) + out2_bias
        center = resid - jnp.mean(resid, -1, keepdims=True)
        rstd = lax.rsqrt(jnp.mean(center * center, -1, keepdims=True) + EPS)
        normed = center * rstd
        r["output"][0, here_rows, :] = (normed * gain1 + shift1).astype(BF16)
        g = gy[0, here_rows, :].astype(F32)
        sum_gn = sum_gn + jnp.sum(g * normed, 0, keepdims=True)
        sum_gy = sum_gy + jnp.sum(g, 0, keepdims=True)
        e = g * gain1
        back = rstd * (
            e - jnp.mean(e, -1, keepdims=True) - normed * jnp.mean(e * normed, -1, keepdims=True)
        )
        DR[here_rows, :] = back
        low_back = back.astype(BF16)
        sum_df = sum_df + jnp.sum(low_back.astype(F32), 0, keepdims=True)
        DF[rows, :] = low_back
        to_partner(DF.at[rows], DF.at[rows], 7 + tile)

    def keep(row, vector):
        SG[row : row + 1, :] = vector[:, :PIECE]
        SG[row + 1 : row + 2, :] = vector[:, PIECE:]

    keep(OUT2_BIAS, sum_df)
    keep(GAINS + 2, sum_gn)
    keep(SHIFTS + 2, sum_gy)

    if fused:

        def write(name, begin):
            def put(total):
                r[name][:, begin : begin + PIECE] = total

            return put

        def write_qkv(p):
            def put(total):
                for m in range(3):
                    r["oqkv"][m, :, p * 128 : (p + 1) * 128] = total[:, m * 128 : (m + 1) * 128]

            return put

        targets = (
            [(gdn, span[k], write("odn", k * PIECE)) for k in range(2 * halves)]
            + [(gup, span[k], write("oup", k * PIECE)) for k in range(2 * halves)]
            + [(go, span[0], write("oo", 0))]
            + [(gqkv, span[p], write_qkv(p)) for p in range(pairs)]
        )
        scatter = Scatter(targets, where, r["R1"], r["R2"], r["R3"], r["rss"], r["rsr"], sends)
        first_out, pump_out = scatter.first, scatter.pump
    else:
        first_out = pump_out = lambda count: None

    def store(ref, begin, value):
        ref[:, :, :, :, begin : begin + value.shape[1]] = value.astype(BF16).reshape(
            ref.shape[:4] + (value.shape[1],)
        )

    for half in range(2):
        if half == 1:
            for tile in range(tiles):
                from_partner(DF.at[rows_at(other, tile)], 7 + tile)

        @pl.loop(0, tiles)
        def _(tile):
            rows = rows_at(other if half else mine, tile)
            for j in range(halves):
                at = slice(j * 2 * PIECE, (j + 1) * 2 * PIECE)
                dact = nn(DF[rows, :], flat(wdn, j * 2 * PIECE, 2 * PIECE))
                du = (dact * GP[rows, at].astype(F32)).astype(BF16)
                GP[rows, at] = du
                sums = jnp.sum(du.astype(F32), 0, keepdims=True)
                r["SI"][j : j + 1, :] = r["SI"][j : j + 1, :] + sums

    for j in range(halves):
        sums = r["SI"][j : j + 1, :]
        keep(IN_BIAS + 2 * j, jnp.where(t == 0, sums, 0.0))
        keep(IN_BIAS + 2 * halves + 2 * j, jnp.where(t == 0, 0.0, sums))
    for j in range(halves):
        store(gdn, j * 2 * PIECE, tn(DF[...], ACT[:, j * 2 * PIECE : (j + 1) * 2 * PIECE]))
        first_out(2 * j)
        first_out(2 * j + 1)
    leave(1)
    for tile in range(tiles):
        rows = rows_at(other, tile)
        SB[0, tile] = nt(GP[rows, :], flat(wup)).astype(BF16)
        to_partner(SB.at[0, tile], RB.at[0, tile], 9 + tile)
    for j in range(halves):
        store(gup, j * 2 * PIECE, tn(HB[...], GP[:, j * 2 * PIECE : (j + 1) * 2 * PIECE]))
        first_out(2 * halves + 2 * j)
        first_out(2 * halves + 2 * j + 1)

    leave(7)
    sum_da = jnp.zeros((1, width), F32)
    sum_dh, sum_dn = sum_da, sum_da
    for tile in range(tiles):
        rows, here_rows = rows_at(mine, tile), rows_at(0, tile)
        part = nt(GP[rows, :], flat(wup))
        from_partner(RB.at[0, tile], 9 + tile)
        g = DR[here_rows, :] + (part + RB[0, tile].astype(F32))
        normed = N1[here_rows, :]
        sum_dn = sum_dn + jnp.sum(g * normed, 0, keepdims=True)
        sum_dh = sum_dh + jnp.sum(g, 0, keepdims=True)
        e = g * gain0
        rstd = RS1[here_rows, :][:, :1]
        back = rstd * (
            e - jnp.mean(e, -1, keepdims=True) - normed * jnp.mean(e * normed, -1, keepdims=True)
        )
        DR[here_rows, :] = back
        low_back = back.astype(BF16)
        sum_da = sum_da + jnp.sum(low_back.astype(F32), 0, keepdims=True)
        DATT[rows, :] = low_back
        to_partner(DATT.at[rows], DATT.at[rows], 11 + tile)
        pump_out(1)
    keep(OUT_BIAS, sum_da)
    keep(GAINS, sum_dn)
    keep(SHIFTS, sum_dh)

    def project_back(base):
        @pl.loop(0, tiles)
        def _(tile):
            rows = rows_at(base, tile)
            dctx = nn(DATT[rows, :], flat(wo))
            for p in range(pairs):
                at = slice(p * 128, (p + 1) * 128)
                d, den, ctx = dctx[:, at], DEN[rows, at], CTX[rows, at].astype(F32)
                dnum = d / jnp.maximum(den, 1.0)
                product = d * ctx
                shifted = swap(dnum)
                for h in range(2):
                    inside = low if h == 0 else jnp.logical_not(low)
                    total = den[:, h * 64 : h * 64 + 1]
                    dden = -jnp.sum(jnp.where(inside, product, 0.0), -1, keepdims=True) / total
                    dden = jnp.where(total > 1.0, dden, 0.0)
                    high = dden.astype(BF16).astype(F32)
                    rest = jnp.where(lane == 64, high, jnp.where(lane == 65, dden - high, 0.0))
                    DN[2 * p + h, rows, :] = jnp.where(low, shifted if h else dnum, rest).astype(BF16)

    project_back(mine)
    for tile in range(tiles):
        from_partner(DATT.at[rows_at(other, tile)], 11 + tile)
    project_back(other)
    pump_out(1)
    store(go, 0, tn(DATT[...], CTX[...]))
    first_out(4 * halves)
    pump_out(1)

    for p in range(pairs):
        at = p * 384

        def attend_back(step, states):
            i = chunks - 1 - step
            rows = rows_at(0, i)
            cs = table[rows, :]
            ahead = lax.broadcasted_iota(jnp.int32, (TILE, TILE), 0) >= lax.broadcasted_iota(
                jnp.int32, (TILE, TILE), 1
            )
            dqs, dks, dvs, after = [], [], [], []
            for h in range(2):
                q, k, va = FQ[2 * p + h, rows, :], FK[2 * p + h, rows, :], VA[2 * p + h, rows, :]
                dn = DN[2 * p + h, rows, :]
                later = states[h].astype(BF16)
                scores = jnp.where(ahead, nt(q, k), 0.0).astype(BF16)
                dscores = jnp.where(ahead, nt(dn, va), 0.0).astype(BF16)
                dq = (nn(dscores, k) + nt(dn, SS[2 * p + h, i])) * cs
                dk = (tn(dscores, q) + nt(va, later)) * cs
                dvs.append(tn(scores, dn) + nn(k, later))
                dqs.append(dq + swap(dq))
                dks.append(dk + swap(dk))
                after.append(states[h] + tn(q, dn))

            def live(feat):
                a, b = feat[2 * p, rows, :].astype(F32), feat[2 * p + 1, rows, :].astype(F32)
                return jnp.where(low, a, swap(b)) > 0.0

            dq = jnp.where(live(FQ), jnp.where(low, dqs[0], dqs[1]), 0.0)
            dk = jnp.where(live(FK), jnp.where(low, dks[0], dks[1]), 0.0)
            dv = jnp.where(low, dvs[0], swap(dvs[1]))
            dpre = jnp.concatenate([dq, dk, dv], 1).astype(BF16)
            DPRE[rows, at : at + 384] = dpre
            return tuple(after)

        start = (jnp.zeros((128, 128), F32), jnp.zeros((128, 128), F32))
        lax.fori_loop(0, chunks, attend_back, start)
        pump_out(2)
        piece = DPRE[:, at : at + 384]
        store(gqkv, at, tn(X[...], piece))
        first_out(4 * halves + 1 + p)
        sums = jnp.sum(piece.astype(F32), 0, keepdims=True)
        for m, row in enumerate((QK_BIAS, QK_BIAS + 2, VALUE_BIAS)):
            here_sums = sums[:, m * 128 : (m + 1) * 128]
            SG[row : row + 1, p * 128 : (p + 1) * 128] = jnp.where(t == 0, here_sums, 0.0)
            SG[row + 1 : row + 2, p * 128 : (p + 1) * 128] = jnp.where(t == 0, 0.0, here_sums)
        pump_out(2)

    leave(5)
    for tile in range(tiles):
        rows = rows_at(other, tile)
        SB[1, tile] = nt(DPRE[rows, :], flat(wqkv)).astype(BF16)
        to_partner(SB.at[1, tile], RB.at[1, tile], 13 + tile)
    if fused:
        Q, ss, sr = r["Q"], r["sms"], r["smr"]
        sends.start(SG, Q.at[0], ss.at[0], sr.at[0], partner)
        pump_out(2)
        remote(SG, Q.at[0], ss.at[0], sr.at[0], partner).wait_recv()
        Q[1] = SG[...] + Q[0]
        sends.start(Q.at[1], Q.at[2], ss.at[1], sr.at[1], x_peer)
    for tile in range(tiles):
        rows, here_rows = rows_at(mine, tile), rows_at(0, tile)
        part = nt(DPRE[rows, :], flat(wqkv))
        from_partner(RB.at[1, tile], 13 + tile)
        r["grad_input"][0, here_rows, :] = DR[here_rows, :] + (part + RB[1, tile].astype(F32))
        pump_out(1)
    if fused:
        remote(Q.at[2], Q.at[2], ss.at[1], sr.at[1], partner).wait_recv()
        Q[3] = Q[1] + Q[2]
        sends.start(Q.at[3], Q.at[4], ss.at[2], sr.at[2], y_peer)
        pump_out(2)
        remote(Q.at[4], Q.at[4], ss.at[2], sr.at[2], partner).wait_recv()
        Q[5] = Q[3] + Q[4]
        for k in range(3):
            sends.start(Q.at[5], Q.at[6 + k], ss.at[3 + k], sr.at[3 + k], z_peers[k])
        scatter.finish()
        total = Q[5]
        for k in range(3):
            remote(Q.at[6 + k], Q.at[6 + k], ss.at[3 + k], sr.at[3 + k], partner).wait_recv()
            total = total + Q[6 + k]
        r["smalls"][...] = total
    else:
        r["smalls"][...] = SG[...]
    sends.finish()


def layer(fused, inputs, grad_out, slabs, small):
    sqkv, so, sup, sdn = slabs
    _, local, width = inputs.shape
    length, cols, hidden = 2 * local, so.shape[-1], sup.shape[-1]
    heads, chunks, tiles = cols // HEAD_DIM, length // TILE, local // TILE
    part = width // 16
    lead = (4, 2, 2, part)
    angles = np.pi / 2.0 * np.arange(length, dtype=np.float64) / length
    table = np.concatenate(
        [np.repeat(np.cos(angles)[:, None], 64, 1), np.repeat(np.sin(angles)[:, None], 64, 1)], 1
    ).astype(np.float32)
    vmem = pl.BlockSpec(memory_space=pltpu.VMEM)
    hbm = pl.BlockSpec(memory_space=pl.ANY)
    dma = pltpu.SemaphoreType.DMA
    sizes = dict(qkv=3 * cols, o=cols, up=hidden, dn=hidden)
    pieces = (4 * cols + 2 * hidden) // PIECE

    ins = [("inputs", inputs, hbm), ("grad_out", grad_out, vmem), ("table", jnp.asarray(table), vmem)]
    if fused:
        ins += [("sqkv", sqkv, vmem), ("so", so, vmem), ("sup", sup, vmem), ("sdn", sdn, vmem)]
    else:
        wholes = [slab.reshape(lead + slab.shape[-1:]) for slab in slabs]
        ins += [(name, value, vmem) for name, value in zip(("wqkv", "wo", "wup", "wdn"), wholes)]
    ins += [("small", small, vmem)]

    outs = [
        ("output", (1, local, width), BF16),
        ("grad_input", (1, local, width), F32),
        ("smalls", (SMALL_ROWS, PIECE), F32),
    ]
    if fused:
        outs += [
            ("oqkv", (3, part, cols), F32),
            ("oo", (part, cols), F32),
            ("oup", (part, hidden), F32),
            ("odn", (part, hidden), F32),
        ]
    else:
        outs += [("g" + name, lead + (size,), BF16) for name, size in sizes.items()]

    def v(*shape, dtype=BF16):
        return pltpu.VMEM(shape, dtype)

    scratch = dict(
        X=v(length, width),
        HB=v(length, width),
        DF=v(length, width),
        FQ=v(heads, length, 128),
        FK=v(heads, length, 128),
        VA=v(heads, length, 128),
        DN=v(heads, length, 128),
        SS=v(heads, chunks, 128, 128),
        DEN=v(length, cols, dtype=F32),
        CTX=v(length, cols),
        N1=v(local, width, dtype=F32),
        RS1=v(local, 128, dtype=F32),
        DR=v(local, width, dtype=F32),
        ACT=v(length, hidden),
        GP=v(length, hidden),
        DPRE=v(length, 3 * cols),
        SB=v(2, tiles, TILE, width),
        RB=v(2, tiles, TILE, width),
        BV=v(SMALL_ROWS, PIECE, dtype=F32),
        SG=v(SMALL_ROWS, PIECE, dtype=F32),
        SI=v(8, 2 * PIECE, dtype=F32),
        tps=dma((16,)),
        tpr=dma((16,)),
        own=dma((6,)),
    )
    if fused:
        scratch.update({"w" + name: v(*lead, size) for name, size in sizes.items()})
        scratch.update({"g" + name: v(*lead, size) for name, size in sizes.items()})
        scratch.update(
            SM=v(4, 2, 2, SMALL_ROWS, PIECE),
            Q=v(9, SMALL_ROWS, PIECE, dtype=F32),
            R1=v(pieces, 4, 2, part, PIECE),
            R2=v(pieces, 4, part, PIECE),
            R3=v(pieces, 3, part, PIECE),
            ags=dma((pieces + 1, 5)),
            agr=dma((pieces + 1, 5)),
            rss=dma((pieces, 5)),
            rsr=dma((pieces, 5)),
            sms=dma((6,)),
            smr=dma((6,)),
        )
    names = [name for name, _, _ in ins] + [name for name, _, _ in outs] + list(scratch)
    results = pl.pallas_call(
        partial(layer_kernel, fused, names),
        name="layer",
        out_shape=tuple(jax.ShapeDtypeStruct(shape, dtype) for _, shape, dtype in outs),
        in_specs=[spec for _, _, spec in ins],
        out_specs=tuple(vmem for _ in outs),
        scratch_shapes=list(scratch.values()),
        compiler_params=pltpu.CompilerParams(
            collective_id=0, has_side_effects=True, vmem_limit_bytes=64 << 20
        ),
    )(*[value for _, value, _ in ins])
    output, grad_input, smalls, *grads = results
    return output, grad_input, smalls, grads


def shards(
    inputs,
    query_key_value_weight,
    attention_out_weight,
    up_weight,
    down_weight,
    qk_bias,
    value_bias,
    out_bias,
    ffn_in_bias,
    ffn_out_bias,
    norm_gains,
    norm_biases,
    grad_out,
):
    rank_here, ranks = lax.axis_index("fsdp"), lax.axis_size("fsdp")
    _, rows, cols = query_key_value_weight.shape
    pairs = cols // 128
    width = inputs.shape[2]
    fused = ranks == 16 and rows % 16 == 0
    sqkv = query_key_value_weight.reshape(3, rows, pairs, 128)
    sqkv = jnp.transpose(sqkv, (1, 2, 0, 3)).reshape(rows, 3 * cols)
    slabs = (sqkv, attention_out_weight.T, up_weight, down_weight.T)

    at_home = (jnp.arange(ranks) == rank_here).astype(BF16)[None, :, None]
    kinds = jnp.concatenate(
        [qk_bias, value_bias[None], out_bias[None], ffn_out_bias[None], norm_gains, norm_biases], 0
    )
    vectors = (kinds[:, None, :] * at_home).reshape(-1, width)
    inner = (ffn_in_bias[None, None, :] * at_home).reshape(-1, width)
    small = jnp.concatenate([vectors, inner], 0)
    small = jnp.pad(small, ((0, SMALL_ROWS * PIECE // width - small.shape[0]), (0, 0)))
    small = small.reshape(SMALL_ROWS, PIECE)

    if not fused:
        slabs = tuple(lax.all_gather(slab, "fsdp", axis=0, tiled=True) for slab in slabs)
        small = lax.psum(small.astype(F32), "fsdp")
    output, grad_input, smalls, grads = layer(fused, inputs, grad_out, slabs, small)
    if fused:
        dqkv, do, dup, ddn = grads
    else:
        dqkv, do, dup, ddn = [
            lax.psum_scatter(g.reshape(width, -1).astype(F32), "fsdp", scatter_dimension=0, tiled=True)
            for g in grads
        ]
        dqkv = jnp.transpose(dqkv.reshape(rows, pairs, 3, 128), (2, 0, 1, 3)).reshape(3, rows, cols)
        smalls = lax.psum(smalls, ("fsdp", "tp"))
    vectors = smalls.reshape(-1, width)
    mine = lax.dynamic_slice_in_dim(vectors[:9], rank_here * rows, rows, 1)
    inner_rows = ffn_in_bias.shape[0]
    inner = vectors[9 : 9 + inner_rows * ranks // width].reshape(-1)
    return (
        output,
        grad_input,
        dqkv,
        do.T,
        dup,
        ddn.T,
        mine[0:2],
        mine[2],
        mine[3],
        lax.dynamic_slice_in_dim(inner, rank_here * inner_rows, inner_rows, 0),
        mine[4],
        mine[5:7],
        mine[7:9],
    )


def solution(mesh):
    return jax.shard_map(
        shards,
        mesh=mesh,
        in_specs=(
            P("fsdp", "tp", None),
            P(None, "fsdp", "tp"),
            P("tp", "fsdp"),
            P("fsdp", "tp"),
            P("tp", "fsdp"),
            P(None, "fsdp"),
            P("fsdp"),
            P("fsdp"),
            P("fsdp"),
            P("fsdp"),
            P(None, "fsdp"),
            P(None, "fsdp"),
            P("fsdp", "tp", None),
        ),
        out_specs=(
            P("fsdp", "tp", None),
            P("fsdp", "tp", None),
            P(None, "fsdp", "tp"),
            P("tp", "fsdp"),
            P("fsdp", "tp"),
            P("tp", "fsdp"),
            P(None, "fsdp"),
            P("fsdp"),
            P("fsdp"),
            P("fsdp"),
            P("fsdp"),
            P(None, "fsdp"),
            P(None, "fsdp"),
        ),
        check_vma=False,
    )
```

```python
from functools import partial

import jax
import jax.numpy as jnp
import numpy as np
from jax import lax
from jax.experimental import pallas as pl
from jax.experimental.pallas import tpu as pltpu
from jax.sharding import PartitionSpec as P

HEAD_DIM = 64
EPS = 1e-05
MESH = pl.DeviceIdType.MESH
BF16 = jnp.bfloat16
F32 = jnp.float32
TILE = 256
PIECE = 384
QK_BIAS, VALUE_BIAS, OUT_BIAS, OUT2_BIAS, GAINS, SHIFTS, IN_BIAS, SMALL_ROWS = 0, 2, 3, 4, 5, 7, 9, 16
SMALLS = (
    ("qk_bias", QK_BIAS),
    ("value_bias", VALUE_BIAS),
    ("out_bias", OUT_BIAS),
    ("ffn_out_bias", OUT2_BIAS),
    ("norm_gains", GAINS),
    ("norm_biases", SHIFTS),
    ("ffn_in_bias", IN_BIAS),
)
GATHER_ORDERS = (
    "zxy", "zyx", "zxy", "zyx", "zxy", "zyx", "zxy", "yzx", "xzy", "zxy", "zyx", "xzy", "yzx",
)
GATHER_PLAN = (
    ((0, 0), (1, 0), (12, 0), (2, 0), (7, 0), (3, 0)),
    ((0, 1), (8, 0), (1, 1), (4, 0), (6, 0), (5, 0), (0, 2), (2, 1), (1, 2), (3, 1)),
    ((2, 2),),
    ((9, 0), (10, 0), (4, 1), (3, 2)),
    ((7, 1),),
    (),
    (),
    ((11, 0), (5, 1)),
    ((6, 1), (4, 2)),
    (),
    (),
    (),
    ((9, 1), (8, 1)),
    (),
    (),
    (),
    (),
    ((12, 1), (10, 1), (5, 2)),
    ((6, 2), (8, 2)),
    ((7, 2),),
    (),
    (),
    ((11, 1),),
    ((9, 2),),
    ((12, 2),),
    (),
    (),
    (),
    (),
    (),
    ((10, 2),),
    (),
    ((11, 2),),
    (),
    (),
    (),
    (),
    (),
    (),
    (),
    (),
    (),
    (),
    (),
)
SCATTER_ORDERS = (
    "xyz", "yzx", "xzy", "yzx", "yxz", "xyz", "yxz", "xyz", "xzy", "yxz", "xyz", "yxz",
)
SCATTER_PLAN = (
    (),
    (),
    (),
    (),
    (),
    (),
    (),
    (),
    (),
    (),
    (),
    (),
    (),
    (),
    ((1, 1),),
    ((0, 1),),
    (),
    (),
    ((3, 1),),
    ((2, 1),),
    (),
    ((5, 1),),
    ((4, 1),),
    (),
    (),
    (),
    (),
    (),
    (),
    ((0, 2),),
    (),
    (),
    ((4, 2), (7, 1)),
    (),
    ((6, 1), (5, 2)),
    (),
    (),
    ((8, 1),),
    (),
    (),
    (),
    (),
    (),
    ((6, 2), (9, 1), (7, 2), (0, 3), (3, 2), (10, 1), (4, 3), (9, 2)),
    ((11, 1),),
    ((7, 3), (6, 3), (2, 2), (10, 2)),
    (),
    (),
    ((11, 2), (9, 3), (1, 2), (2, 3), (8, 2), (3, 3), (8, 3), (1, 3), (10, 3), (5, 3), (11, 3)),
)
BAND = 32


def nn(a, b):
    return jnp.dot(a, b, preferred_element_type=F32)


def nt(a, b):
    return lax.dot_general(a, b, (((1,), (1,)), ((), ())), preferred_element_type=F32)


def tn(a, b):
    return lax.dot_general(a, b, (((0,), (0,)), ((), ())), preferred_element_type=F32)


def place():
    f = lax.axis_index("fsdp")
    return lax.rem(f, 2), lax.rem(f // 2, 2), f // 4, lax.axis_index("tp")


def rank(x, y, z):
    return (z * 2 + y) * 2 + x


def greet(devices):
    barrier = pltpu.get_barrier_semaphore()
    for device in devices:
        pl.semaphore_signal(barrier, inc=1, device_id=device, device_id_type=MESH)


def await_greetings(devices):
    pl.semaphore_wait(pltpu.get_barrier_semaphore(), len(devices))


def remote(source, target, send_sem, recv_sem, device):
    return pltpu.make_async_remote_copy(
        src_ref=source,
        dst_ref=target,
        send_sem=send_sem,
        recv_sem=recv_sem,
        device_id=device,
        device_id_type=MESH,
    )


class Sends:
    def __init__(self):
        self.copies = []

    def start(self, *args):
        copy = remote(*args)
        copy.start()
        self.copies.append(copy)
        return copy

    def settle(self, copies):
        for copy in copies:
            copy.wait_send()
        self.copies = [c for c in self.copies if not any(c is copy for copy in copies)]

    def finish(self):
        self.settle(list(self.copies))


class Gather:
    SLOT = {"x": 0, "y": 1, "z": 2}

    def __init__(self, pieces, where, send, recv, sends):
        self.pieces, self.send, self.recv, self.sends = pieces, send, recv, sends
        self.x, self.y, self.z, t = where
        x, y, z = self.x, self.y, self.z
        self.z_peers = [(rank(x, y, lax.rem(z + k, 4)), t) for k in (1, 2, 3)]
        self.peer = {"x": (rank(1 - x, y, z), t), "y": (rank(x, 1 - y, z), t)}
        self.orders = GATHER_ORDERS
        self.plan = iter(GATHER_PLAN)

    def view(self, piece, have, **at):
        whole, cols = self.pieces[piece]
        index = [
            at.get(axis, slice(None) if axis in have else own)
            for axis, own in (("z", self.z), ("y", self.y), ("x", self.x))
        ]
        return whole.at[(*index, slice(None), cols)]

    def sems(self, piece, slot):
        return self.send.at[piece, slot], self.recv.at[piece, slot]

    def arrive(self, piece, stage):
        order = self.orders[piece]
        axis, have = order[stage], order[:stage]
        if axis == "z":
            for k in range(3):
                target = self.view(piece, have, z=lax.rem(self.z + 3 - k, 4))
                remote(target, target, *self.sems(piece, 2 + k), self.peer["x"]).wait_recv()
        else:
            target = self.view(piece, have, **{axis: 1 - getattr(self, axis)})
            remote(target, target, *self.sems(piece, self.SLOT[axis]), self.peer["x"]).wait_recv()

    def step(self, piece, stage):
        order = self.orders[piece]
        axis, have = order[stage], order[:stage]
        if stage:
            self.arrive(piece, stage - 1)
        own = self.view(piece, have)
        if axis == "z":
            for k in range(3):
                self.sends.start(own, own, *self.sems(piece, 2 + k), self.z_peers[k])
        else:
            self.sends.start(own, own, *self.sems(piece, self.SLOT[axis]), self.peer[axis])

    def turn(self):
        for piece, stage in next(self.plan):
            self.step(piece, stage)

    def need(self, *pieces):
        for piece in pieces:
            self.arrive(piece, 2)
            self.turn()


class Scatter:
    def __init__(self, pieces, where, r1, r2, r3, send, recv, sends):
        self.pieces, self.r1, self.r2, self.r3 = pieces, r1, r2, r3
        self.send, self.recv, self.sends = send, recv, sends
        self.x, self.y, self.z, t = where
        x, y, z = self.x, self.y, self.z
        self.z_at = [lax.rem(z + k, 4) for k in (1, 2, 3)]
        self.z_peers = [(rank(x, y, q), t) for q in self.z_at]
        self.peer = {"x": (rank(1 - x, y, z), t), "y": (rank(x, 1 - y, z), t)}
        self.orders = SCATTER_ORDERS
        self.plan = iter(SCATTER_PLAN)

    def sems(self, piece, slot):
        return self.send.at[piece, slot], self.recv.at[piece, slot]

    def arrive(self, target, piece, slot):
        remote(target, target, *self.sems(piece, slot), self.peer["x"]).wait_recv()

    def first(self, piece):
        axis = self.orders[piece][0]
        grads, cols, _ = self.pieces[piece]
        every = slice(None)
        away = 1 - getattr(self, axis)
        index = (every, every, away) if axis == "x" else (every, away, every)
        self.sends.start(
            grads.at[(*index, every, cols)], self.r1.at[piece], *self.sems(piece, 0), self.peer[axis]
        )
        self.turn()

    def second(self, piece):
        axis, after, _ = self.orders[piece]
        self.arrive(self.r1.at[piece], piece, 0)
        grads, cols, _ = self.pieces[piece]
        for q in range(4):
            for r in range(2):
                mine = grads[q, r, self.x, :, cols] if axis == "x" else grads[q, self.y, r, :, cols]
                self.r1[piece, q, r] = (mine.astype(F32) + self.r1[piece, q, r].astype(F32)).astype(BF16)
        if after == "z":
            for k in range(3):
                self.sends.start(
                    self.r1.at[piece, self.z_at[k]],
                    self.r2.at[piece, pl.ds(2 * k, 2)],
                    *self.sems(piece, 2 + k),
                    self.z_peers[k],
                )
        else:
            self.sends.start(
                self.r1.at[piece, :, 1 - getattr(self, after)],
                self.r2.at[piece, pl.ds(0, 4)],
                *self.sems(piece, 1),
                self.peer[after],
            )

    def third(self, piece):
        _, after, final = self.orders[piece]
        if after == "z":
            for k in range(3):
                self.arrive(self.r2.at[piece, pl.ds(2 * k, 2)], piece, 2 + k)
            for r in range(2):
                total = self.r1[piece, self.z, r].astype(F32)
                for k in range(3):
                    total = total + self.r2[piece, 2 * k + r].astype(F32)
                self.r1[piece, self.z, r] = total.astype(BF16)
            self.sends.start(
                self.r1.at[piece, self.z, 1 - getattr(self, final)],
                self.r3.at[piece, 0],
                *self.sems(piece, 1),
                self.peer[final],
            )
        else:
            self.arrive(self.r2.at[piece, pl.ds(0, 4)], piece, 1)
            own = getattr(self, after)
            for q in range(4):
                mine = self.r1[piece, q, own]
                self.r2[piece, q] = (mine.astype(F32) + self.r2[piece, q].astype(F32)).astype(BF16)
            for k in range(3):
                self.sends.start(
                    self.r2.at[piece, self.z_at[k]],
                    self.r3.at[piece, k],
                    *self.sems(piece, 2 + k),
                    self.z_peers[k],
                )

    def last(self, piece):
        _, after, final = self.orders[piece]
        if after == "z":
            self.arrive(self.r3.at[piece, 0], piece, 1)
            total = self.r1[piece, self.z, getattr(self, final)].astype(F32) + self.r3[piece, 0].astype(F32)
        else:
            total = self.r2[piece, self.z].astype(F32)
            for k in range(3):
                self.arrive(self.r3.at[piece, k], piece, 2 + k)
                total = total + self.r3[piece, k].astype(F32)
        self.pieces[piece][2](total)

    def turn(self):
        for piece, stage in next(self.plan):
            (self.second, self.third, self.last)[stage - 1](piece)


def layer_kernel(fused, names, *refs):
    r = dict(zip(names, refs))
    where = x, y, z, t = place()
    partner = (lax.axis_index("fsdp"), 1 - t)
    sends = Sends()
    gy, xs = r["grad_out"], r["inputs"]
    wqkv, wo, wup, wdn = r["wqkv"], r["wo"], r["wup"], r["wdn"]
    gqkv, go, gup, gdn = r["gqkv"], r["go"], r["gup"], r["gdn"]
    X, HB, DF = r["X"], r["HB"], r["DF"]
    DATT = DF
    FQ, FK, VA, SS, DN = r["FQ"], r["FK"], r["VA"], r["SS"], r["DN"]
    DEN, CTX, N1, RS1, DR = r["DEN"], r["CTX"], r["N1"], r["RS1"], r["DR"]
    ACT, GP, DPRE, SB, RB = r["ACT"], r["GP"], r["DPRE"], r["SB"], r["RB"]
    BV, SG, table = r["BV"], r["SG"], r["table"]
    tps, tpr = r["tps"], r["tpr"]
    length, width = X.shape
    local = length // 2
    tiles = local // TILE
    cols = wo.shape[-1]
    hidden = wup.shape[-1]
    pairs = cols // 128
    chunks = length // TILE
    halves = hidden // (2 * PIECE)
    mine, other = t * local, (1 - t) * local

    def rows_at(base, tile):
        return pl.ds(pl.multiple_of(base + tile * TILE, TILE), TILE)

    passed = {}

    def to_partner(source, target, index):
        passed[index] = sends.start(source, target, tps.at[index], tpr.at[index], partner)

    def leave(first):
        sends.settle([passed[first + tile] for tile in range(tiles)])

    def from_partner(target, index):
        remote(target, target, tps.at[index], tpr.at[index], partner).wait_recv()

    def flat(ref, begin=0, size=None):
        size = ref.shape[-1] if size is None else size
        return ref[:, :, :, :, begin : begin + size].reshape(width, size)

    here = pltpu.make_async_copy(xs.at[0], X.at[pl.ds(mine, local)], r["own"].at[0])
    here.start()
    first_up = 2 + pairs
    first_dn = first_up + 2 * halves
    if fused:
        x_peer, y_peer = (rank(1 - x, y, z), t), (rank(x, 1 - y, z), t)
        z_peers = [(rank(x, y, lax.rem(z + k, 4)), t) for k in (1, 2, 3)]
        friends = z_peers + [x_peer, y_peer, partner]
        greet(friends)
        f = lax.axis_index("fsdp")
        Z = r["Z"]
        owns = wqkv.shape[3]
        Z[...] = jnp.zeros_like(Z)
        for name, row in SMALLS:
            piece = r[name]
            Z[row : row + piece.shape[0], 0 : piece.shape[1]] = piece[...].astype(F32)
        inner = r["ffn_in_bias"].shape[1]
        per_row = width // inner
        table_row = lax.broadcasted_iota(jnp.int32, (SMALL_ROWS, width), 0)
        line = jnp.broadcast_to(Z[IN_BIAS : IN_BIAS + 1, :], (8, width))
        line = pltpu.roll(line, lax.rem(f, per_row) * inner, 1)[:1]
        placed = pltpu.roll(Z[...], f * owns, 1)
        own_row = table_row == IN_BIAS + f // per_row
        placed = jnp.where(table_row < IN_BIAS, placed, jnp.where(own_row, line, 0.0))
        r["SM"][z, y, x] = placed.astype(BF16)
        for p in range(pairs):
            for m in range(3):
                begin = p * 384 + m * 128
                wqkv[z, y, x, :, begin : begin + 128] = r["sqkv"][m, :, p * 128 : (p + 1) * 128]
        wo[z, y, x] = r["so"][...]
        wup[z, y, x] = r["sup"][...]
        wdn[z, y, x] = r["sdn"][...]
        span = [slice(k * PIECE, (k + 1) * PIECE) for k in range(max(pairs, 2 * halves))]
        sources = (
            [(r["SM"], slice(0, width))]
            + [(wqkv, span[p]) for p in range(pairs)]
            + [(wo, span[0])]
            + [(wup, span[k]) for k in range(2 * halves)]
            + [(wdn, span[k]) for k in range(2 * halves)]
        )
        gather = Gather(sources, where, r["ags"], r["agr"], sends)
        await_greetings(friends)
        gather.turn()
        turn_in, need = gather.turn, gather.need
    else:
        greet([partner])
        await_greetings([partner])
        turn_in, need = lambda: None, lambda *pieces: None
    to_partner(xs.at[0], X.at[pl.ds(mine, local)], 0)
    SG[...] = jnp.zeros_like(SG)
    r["SI"][...] = jnp.zeros_like(r["SI"])
    here.wait()
    from_partner(X.at[pl.ds(other, local)], 0)
    turn_in()

    lane = lax.broadcasted_iota(jnp.int32, (TILE, 128), 1)
    low = lane < 64

    def swap(v):
        return pltpu.roll(v, 64, 1)

    need(0)
    if fused:
        total = jnp.zeros((SMALL_ROWS, width), F32)
        for a in range(4):
            for b in range(2):
                for c in range(2):
                    total = total + r["SM"][a, b, c].astype(F32)
        BV[...] = total
    else:
        BV[...] = r["small"][...]

    def small_row(row):
        return BV[row : row + 1, :]

    def own_half(row):
        return jnp.where(t == 0, BV[row : row + 1, :cols], BV[row : row + 1, cols:])

    out_bias, out2_bias = small_row(OUT_BIAS), small_row(OUT2_BIAS)
    gain0, gain1 = small_row(GAINS), small_row(GAINS + 1)
    shift0, shift1 = small_row(SHIFTS), small_row(SHIFTS + 1)
    in_bias = [
        jnp.where(t == 0, small_row(IN_BIAS + j), small_row(IN_BIAS + halves + j)) for j in range(halves)
    ]
    bq, bk, bv = own_half(QK_BIAS), own_half(QK_BIAS + 1), own_half(VALUE_BIAS)
    turn_in()

    ahead = lax.broadcasted_iota(jnp.int32, (TILE, TILE), 0) >= lax.broadcasted_iota(
        jnp.int32, (TILE, TILE), 1
    )
    for p in range(pairs):
        need(1 + p)
        at = p * 128
        states = [None, None]
        for i in range(chunks):
            rows = slice(i * TILE, (i + 1) * TILE)
            pre = nn(X[rows, :], flat(wqkv, p * 384, 384))
            cs = table[rows, :]
            q = jnp.maximum(pre[:, :128] + bq[:, at : at + 128], 0.0)
            k = jnp.maximum(pre[:, 128:256] + bk[:, at : at + 128], 0.0)
            v = pre[:, 256:] + bv[:, at : at + 128]
            qs, ks, vs = swap(q), swap(k), swap(v)
            feats = (
                ((jnp.where(low, q, qs) * cs).astype(BF16), (jnp.where(low, qs, q) * cs).astype(BF16)),
                ((jnp.where(low, k, ks) * cs).astype(BF16), (jnp.where(low, ks, k) * cs).astype(BF16)),
                (jnp.where(low, v, 1.0).astype(BF16), jnp.where(low, vs, 1.0).astype(BF16)),
            )
            both = []
            for h in range(2):
                fq, fk, va = (feat[h] for feat in feats)
                FQ[2 * p + h, rows, :], FK[2 * p + h, rows, :], VA[2 * p + h, rows, :] = fq, fk, va
                scores = jnp.where(ahead, nt(fq, fk), 0.0).astype(BF16)
                sums = nn(scores, va)
                if i:
                    before = states[h].astype(BF16)
                    SS[2 * p + h, i] = before
                    sums = sums + nn(fq, before)
                both.append(sums)
                if i + 1 < chunks:
                    grown = tn(fk, va)
                    states[h] = states[h] + grown if i else grown
            num = jnp.where(low, both[0], swap(both[1]))
            den = jnp.where(low, swap(both[0]), both[1])
            DEN[rows, at : at + 128] = den
            CTX[rows, at : at + 128] = (num / jnp.maximum(den, 1.0)).astype(BF16)
            turn_in()

    P = r["P"]

    def bands(body, count):
        def step(b, sums):
            rows = pl.ds(pl.multiple_of(b * BAND, BAND), BAND)
            terms = body(rows, b * BAND)
            return tuple(
                total + jnp.sum(term.reshape(BAND // 8, 8, width), 0) for total, term in zip(sums, terms)
            )

        zero = jnp.zeros((8, width), F32)
        return lax.fori_loop(0, TILE // BAND, step, (zero,) * count, unroll=4)

    def mean(v):
        return jnp.mean(v, -1, keepdims=True)

    def normalize(resid):
        center = resid - mean(resid)
        rstd = lax.rsqrt(mean(center * center) + EPS)
        return center * rstd, rstd

    need(1 + pairs)
    for tile in range(tiles):
        rows = rows_at(other, tile)
        SB[0, tile] = nt(CTX[rows, :], flat(wo)).astype(BF16)
        to_partner(SB.at[0, tile], RB.at[0, tile], 1 + tile)
        turn_in()
    for tile in range(tiles):
        rows = rows_at(mine, tile)
        P[...] = nt(CTX[rows, :], flat(wo))
        from_partner(RB.at[0, tile], 1 + tile)

        def first_norm(band, begin):
            whole = pl.ds(pl.multiple_of(mine + tile * TILE + begin, BAND), BAND)
            local_rows = pl.ds(pl.multiple_of(tile * TILE + begin, BAND), BAND)
            resid = X[whole, :].astype(F32) + (P[band, :] + RB[0, tile, band, :].astype(F32) + out_bias)
            normed, rstd = normalize(resid)
            N1[local_rows, :] = normed
            RS1[local_rows, :] = jnp.broadcast_to(rstd, (BAND, 128))
            HB[whole, :] = (normed * gain0 + shift0).astype(BF16)
            return ()

        bands(first_norm, 0)
        to_partner(HB.at[rows], HB.at[rows], 3 + tile)
        turn_in()

    for j in range(halves):
        need(first_up + 2 * j, first_up + 2 * j + 1)
        for half in range(2):
            if j == 0 and half == 1:
                for tile in range(tiles):
                    from_partner(HB.at[rows_at(other, tile)], 3 + tile)
            begin = j * 2 * PIECE
            for tile in range(tiles):
                rows = rows_at(other if half else mine, tile)
                u = nn(HB[rows, :], flat(wup, begin, 2 * PIECE)) + in_bias[j]
                cdf = 0.5 * (1.0 + lax.erf(u * np.float32(0.5**0.5)))
                pdf = jnp.exp(-0.5 * u * u) * np.float32((2.0 * np.pi) ** -0.5)
                ACT[rows, begin : begin + 2 * PIECE] = (u * cdf).astype(BF16)
                GP[rows, begin : begin + 2 * PIECE] = (cdf + u * pdf).astype(BF16)
                turn_in()

    need(*range(first_dn, first_dn + 2 * halves))
    for tile in range(tiles):
        rows = rows_at(other, tile)
        SB[1, tile] = nt(ACT[rows, :], flat(wdn)).astype(BF16)
        to_partner(SB.at[1, tile], RB.at[1, tile], 5 + tile)
        turn_in()
    totals = []
    for tile in range(tiles):
        rows = rows_at(mine, tile)
        P[...] = nt(ACT[rows, :], flat(wdn))
        from_partner(RB.at[1, tile], 5 + tile)

        def second_norm(band, begin):
            whole = pl.ds(pl.multiple_of(mine + tile * TILE + begin, BAND), BAND)
            local_rows = pl.ds(pl.multiple_of(tile * TILE + begin, BAND), BAND)
            h1 = N1[local_rows, :] * gain0 + shift0
            resid = h1 + (P[band, :] + RB[1, tile, band, :].astype(F32)) + out2_bias
            normed, rstd = normalize(resid)
            r["output"][0, local_rows, :] = (normed * gain1 + shift1).astype(BF16)
            g = gy[0, local_rows, :].astype(F32)
            e = g * gain1
            back = rstd * (e - mean(e) - normed * mean(e * normed))
            DR[local_rows, :] = back
            low_back = back.astype(BF16)
            DF[whole, :] = low_back
            return low_back.astype(F32), g * normed, g

        totals.append(bands(second_norm, 3))
        to_partner(DF.at[rows], DF.at[rows], 7 + tile)
        turn_in()
    sum_df, sum_gn, sum_gy = [
        jnp.sum(sum(parts[1:], parts[0]), 0, keepdims=True) for parts in zip(*totals)
    ]

    def keep(row, vector):
        SG[row : row + 1, :] = vector

    keep(OUT2_BIAS, sum_df)
    keep(GAINS + 1, sum_gn)
    keep(SHIFTS + 1, sum_gy)

    if fused:

        def write(name, begin):
            def put(total):
                r[name][:, begin : begin + PIECE] = total

            return put

        def write_qkv(p):
            def put(total):
                for m in range(3):
                    r["oqkv"][m, :, p * 128 : (p + 1) * 128] = total[:, m * 128 : (m + 1) * 128]

            return put

        targets = (
            [(gdn, span[k], write("odn", k * PIECE)) for k in range(2 * halves)]
            + [(gup, span[k], write("oup", k * PIECE)) for k in range(2 * halves)]
            + [(go, span[0], write("oo", 0))]
            + [(gqkv, span[p], write_qkv(p)) for p in range(pairs)]
        )
        scatter = Scatter(targets, where, r["R1"], r["R2"], r["R3"], r["rss"], r["rsr"], sends)
        first_out, turn_out = scatter.first, scatter.turn
    else:
        first_out, turn_out = lambda piece: None, lambda: None

    def store(ref, begin, value):
        ref[:, :, :, :, begin : begin + value.shape[1]] = value.astype(BF16).reshape(
            ref.shape[:4] + (value.shape[1],)
        )

    for tile in range(tiles):
        from_partner(DF.at[rows_at(other, tile)], 7 + tile)
    for j in range(halves):
        store(gdn, j * 2 * PIECE, tn(DF[...], ACT[:, j * 2 * PIECE : (j + 1) * 2 * PIECE]))
        turn_out()
        first_out(2 * j)
        first_out(2 * j + 1)
    for base in (mine, other):
        for tile in range(tiles):
            rows = rows_at(base, tile)
            for j in range(halves):
                at = slice(j * 2 * PIECE, (j + 1) * 2 * PIECE)
                dact = nn(DF[rows, :], flat(wdn, j * 2 * PIECE, 2 * PIECE))
                du = (dact * GP[rows, at].astype(F32)).astype(BF16)
                GP[rows, at] = du
                sums = jnp.sum(du.astype(F32), 0, keepdims=True)
                r["SI"][j : j + 1, :] = r["SI"][j : j + 1, :] + sums
            turn_out()

    for j in range(halves):
        sums = r["SI"][j : j + 1, :]
        keep(IN_BIAS + j, jnp.where(t == 0, sums, 0.0))
        keep(IN_BIAS + halves + j, jnp.where(t == 0, 0.0, sums))
    leave(1)
    for tile in range(tiles):
        rows = rows_at(other, tile)
        SB[0, tile] = nt(GP[rows, :], flat(wup)).astype(BF16)
        to_partner(SB.at[0, tile], RB.at[0, tile], 9 + tile)
        turn_out()
    for j in range(halves):
        store(gup, j * 2 * PIECE, tn(HB[...], GP[:, j * 2 * PIECE : (j + 1) * 2 * PIECE]))
        turn_out()
        first_out(2 * halves + 2 * j)
        first_out(2 * halves + 2 * j + 1)

    leave(7)
    totals = []
    for tile in range(tiles):
        rows = rows_at(mine, tile)
        P[...] = nt(GP[rows, :], flat(wup))
        from_partner(RB.at[0, tile], 9 + tile)

        def first_norm_back(band, begin):
            whole = pl.ds(pl.multiple_of(mine + tile * TILE + begin, BAND), BAND)
            local_rows = pl.ds(pl.multiple_of(tile * TILE + begin, BAND), BAND)
            g = DR[local_rows, :] + (P[band, :] + RB[0, tile, band, :].astype(F32))
            normed = N1[local_rows, :]
            e = g * gain0
            rstd = RS1[local_rows, :][:, :1]
            back = rstd * (e - mean(e) - normed * mean(e * normed))
            DR[local_rows, :] = back
            low_back = back.astype(BF16)
            DATT[whole, :] = low_back
            return low_back.astype(F32), g * normed, g

        totals.append(bands(first_norm_back, 3))
        to_partner(DATT.at[rows], DATT.at[rows], 11 + tile)
        turn_out()
    sum_da, sum_dn, sum_dh = [
        jnp.sum(sum(parts[1:], parts[0]), 0, keepdims=True) for parts in zip(*totals)
    ]
    keep(OUT_BIAS, sum_da)
    keep(GAINS, sum_dn)
    keep(SHIFTS, sum_dh)

    def project_back(base):
        for tile in range(tiles):
            rows = rows_at(base, tile)
            dctx = nn(DATT[rows, :], flat(wo))
            for p in range(pairs):
                at = slice(p * 128, (p + 1) * 128)
                d, den, ctx = dctx[:, at], DEN[rows, at], CTX[rows, at].astype(F32)
                dnum = d / jnp.maximum(den, 1.0)
                product = d * ctx
                shifted = swap(dnum)
                for h in range(2):
                    inside = low if h == 0 else jnp.logical_not(low)
                    total = den[:, h * 64 : h * 64 + 1]
                    dden = -jnp.sum(jnp.where(inside, product, 0.0), -1, keepdims=True) / total
                    dden = jnp.where(total > 1.0, dden, 0.0)
                    high = dden.astype(BF16).astype(F32)
                    rest = jnp.where(lane == 64, high, jnp.where(lane == 65, dden - high, 0.0))
                    DN[2 * p + h, rows, :] = jnp.where(low, shifted if h else dnum, rest).astype(BF16)
            turn_out()

    project_back(mine)
    for tile in range(tiles):
        from_partner(DATT.at[rows_at(other, tile)], 11 + tile)
    project_back(other)
    store(go, 0, tn(DATT[...], CTX[...]))
    turn_out()
    first_out(4 * halves)

    for p in range(pairs):
        at = p * 384

        states = [None, None]
        for i in reversed(range(chunks)):
            rows = slice(i * TILE, (i + 1) * TILE)
            cs = table[rows, :]
            dqs, dks, dvs = [], [], []
            for h in range(2):
                q, k, va = FQ[2 * p + h, rows, :], FK[2 * p + h, rows, :], VA[2 * p + h, rows, :]
                dn = DN[2 * p + h, rows, :]
                scores = jnp.where(ahead, nt(q, k), 0.0).astype(BF16)
                dscores = jnp.where(ahead, nt(dn, va), 0.0).astype(BF16)
                dq, dk, dv = nn(dscores, k), tn(dscores, q), tn(scores, dn)
                if i:
                    dq = dq + nt(dn, SS[2 * p + h, i])
                if i + 1 < chunks:
                    later = states[h].astype(BF16)
                    dk = dk + nt(va, later)
                    dv = dv + nn(k, later)
                if i:
                    grown = tn(q, dn)
                    states[h] = states[h] + grown if i + 1 < chunks else grown
                dq, dk = dq * cs, dk * cs
                dqs.append(dq + swap(dq))
                dks.append(dk + swap(dk))
                dvs.append(dv)

            def live(feat):
                a, b = feat[2 * p, rows, :].astype(F32), feat[2 * p + 1, rows, :].astype(F32)
                return jnp.where(low, a, swap(b)) > 0.0

            dq = jnp.where(live(FQ), jnp.where(low, dqs[0], dqs[1]), 0.0)
            dk = jnp.where(live(FK), jnp.where(low, dks[0], dks[1]), 0.0)
            dv = jnp.where(low, dvs[0], swap(dvs[1]))
            DPRE[rows, at : at + 384] = jnp.concatenate([dq, dk, dv], 1).astype(BF16)
            turn_out()
        piece = DPRE[:, at : at + 384]
        store(gqkv, at, tn(X[...], piece))
        sums = jnp.sum(piece.astype(F32), 0, keepdims=True)
        for m, row in enumerate((QK_BIAS, QK_BIAS + 1, VALUE_BIAS)):
            here_sums = sums[:, m * 128 : (m + 1) * 128]
            SG[row : row + 1, p * 128 : (p + 1) * 128] = jnp.where(t == 0, here_sums, 0.0)
            begin = cols + p * 128
            SG[row : row + 1, begin : begin + 128] = jnp.where(t == 0, 0.0, here_sums)
        turn_out()
        first_out(4 * halves + 1 + p)

    leave(5)
    if fused:
        Q, ss, sr = r["Q"], r["sms"], r["smr"]

        def arrive(slot, index):
            remote(Q.at[slot], Q.at[slot], ss.at[index], sr.at[index], partner).wait_recv()

        sends.start(SG, Q.at[0], ss.at[0], sr.at[0], partner)
    for tile in range(tiles):
        rows = rows_at(other, tile)
        SB[1, tile] = nt(DPRE[rows, :], flat(wqkv)).astype(BF16)
        to_partner(SB.at[1, tile], RB.at[1, tile], 13 + tile)
        if fused and tile == 0:
            arrive(0, 0)
            Q[1] = SG[...] + Q[0]
            sends.start(Q.at[1], Q.at[2], ss.at[1], sr.at[1], x_peer)
        turn_out()
    for tile in range(tiles):
        rows, here_rows = rows_at(mine, tile), rows_at(0, tile)
        part = nt(DPRE[rows, :], flat(wqkv))
        from_partner(RB.at[1, tile], 13 + tile)
        r["grad_input"][0, here_rows, :] = DR[here_rows, :] + (part + RB[1, tile].astype(F32))
        if fused and tile == 0:
            arrive(2, 1)
            Q[3] = Q[1] + Q[2]
            sends.start(Q.at[3], Q.at[4], ss.at[2], sr.at[2], y_peer)
        turn_out()
    if fused:
        arrive(4, 2)
        Q[5] = Q[3] + Q[4]
        for k in range(3):
            sends.start(Q.at[5], Q.at[6 + k], ss.at[3 + k], sr.at[3 + k], z_peers[k])
        turn_out()
        total = Q[5]
        for k in range(3):
            arrive(6 + k, 3 + k)
            total = total + Q[6 + k]
        owned = pltpu.roll(total, lax.rem(width - f * owns, width), 1)
        line = jnp.sum(jnp.where(own_row, total, 0.0), 0, keepdims=True)
        line = jnp.broadcast_to(line, (8, width))
        line = pltpu.roll(line, lax.rem(width - lax.rem(f, per_row) * inner, width), 1)[:1]
        r["smalls"][...] = jnp.where(table_row < IN_BIAS, owned, line)
    else:
        r["smalls"][...] = SG[...]
    sends.finish()


def layer(fused, inputs, grad_out, slabs, small):
    sqkv, so, sup, sdn = slabs
    _, local, width = inputs.shape
    length, cols, hidden = 2 * local, sqkv.shape[-1] if fused else so.shape[-1], sup.shape[-1]
    heads, chunks, tiles = cols // HEAD_DIM, length // TILE, local // TILE
    part = width // 16
    lead = (4, 2, 2, part)
    angles = np.pi / 2.0 * np.arange(length, dtype=np.float64) / length
    table = np.concatenate(
        [np.repeat(np.cos(angles)[:, None], 64, 1), np.repeat(np.sin(angles)[:, None], 64, 1)], 1
    ).astype(np.float32)
    vmem = pl.BlockSpec(memory_space=pltpu.VMEM)
    hbm = pl.BlockSpec(memory_space=pl.ANY)
    dma = pltpu.SemaphoreType.DMA
    sizes = dict(qkv=3 * cols, o=cols, up=hidden, dn=hidden)
    pieces = (4 * cols + 2 * hidden) // PIECE

    ins = [("inputs", inputs, hbm), ("grad_out", grad_out, vmem), ("table", jnp.asarray(table), vmem)]
    if fused:
        ins += [("sqkv", sqkv, vmem), ("so", so, vmem), ("sup", sup, vmem), ("sdn", sdn, vmem)]
        ins += [(name, piece, vmem) for (name, _), piece in zip(SMALLS, small)]
    else:
        wholes = [slab.reshape(lead + slab.shape[-1:]) for slab in slabs]
        ins += [(name, value, vmem) for name, value in zip(("wqkv", "wo", "wup", "wdn"), wholes)]
        ins += [("small", small, vmem)]

    outs = [
        ("output", (1, local, width), BF16),
        ("grad_input", (1, local, width), F32),
        ("smalls", (SMALL_ROWS, width), F32),
    ]
    if fused:
        outs += [
            ("oqkv", (3, part, cols), F32),
            ("oo", (part, cols), F32),
            ("oup", (part, hidden), F32),
            ("odn", (part, hidden), F32),
        ]
    else:
        outs += [("g" + name, lead + (size,), BF16) for name, size in sizes.items()]

    def v(*shape, dtype=BF16):
        return pltpu.VMEM(shape, dtype)

    scratch = dict(
        X=v(length, width),
        HB=v(length, width),
        DF=v(length, width),
        FQ=v(heads, length, 128),
        FK=v(heads, length, 128),
        VA=v(heads, length, 128),
        DN=v(heads, length, 128),
        SS=v(heads, chunks, 128, 128),
        DEN=v(length, cols, dtype=F32),
        CTX=v(length, cols),
        N1=v(local, width, dtype=F32),
        RS1=v(local, 128, dtype=F32),
        DR=v(local, width, dtype=F32),
        ACT=v(length, hidden),
        GP=v(length, hidden),
        DPRE=v(length, 3 * cols),
        SB=v(2, tiles, TILE, width),
        RB=v(2, tiles, TILE, width),
        P=v(TILE, width, dtype=F32),
        BV=v(SMALL_ROWS, width, dtype=F32),
        SG=v(SMALL_ROWS, width, dtype=F32),
        SI=v(8, 2 * PIECE, dtype=F32),
        tps=dma((16,)),
        tpr=dma((16,)),
        own=dma((1,)),
    )
    if fused:
        scratch.update({"w" + name: v(*lead, size) for name, size in sizes.items()})
        scratch.update({"g" + name: v(*lead, size) for name, size in sizes.items()})
        scratch.update(
            SM=v(4, 2, 2, SMALL_ROWS, width),
            Z=v(SMALL_ROWS, width, dtype=F32),
            Q=v(9, SMALL_ROWS, width, dtype=F32),
            R1=v(pieces, 4, 2, part, PIECE),
            R2=v(pieces, 6, part, PIECE),
            R3=v(pieces, 3, part, PIECE),
            ags=dma((pieces + 1, 5)),
            agr=dma((pieces + 1, 5)),
            rss=dma((pieces, 5)),
            rsr=dma((pieces, 5)),
            sms=dma((6,)),
            smr=dma((6,)),
        )
    names = [name for name, _, _ in ins] + [name for name, _, _ in outs] + list(scratch)
    results = pl.pallas_call(
        partial(layer_kernel, fused, names),
        name="layer",
        out_shape=tuple(jax.ShapeDtypeStruct(shape, dtype) for _, shape, dtype in outs),
        in_specs=[spec for _, _, spec in ins],
        out_specs=tuple(vmem for _ in outs),
        scratch_shapes=list(scratch.values()),
        compiler_params=pltpu.CompilerParams(
            collective_id=0, has_side_effects=True, vmem_limit_bytes=64 << 20
        ),
    )(*[value for _, value, _ in ins])
    output, grad_input, smalls, *grads = results
    return output, grad_input, smalls, grads


def hand_over_kernel(count, *refs):
    large, smalls, targets, pieces = refs[:count], refs[count], refs[count + 1 : 2 * count + 1], refs[2 * count + 1 :]
    for source, target in zip(large, targets):
        target[...] = source[...]
    for (_, row), piece in zip(SMALLS, pieces):
        piece[...] = smalls[row : row + piece.shape[0], 0 : piece.shape[1]]


def hand_over(large, smalls, shapes):
    steps = 4
    specs = []
    for v in large:
        axis = 1 if v.shape[0] == 1 else v.ndim - 1
        if v.shape[axis] % (steps * 128) == 0:
            block = v.shape[:axis] + (v.shape[axis] // steps,) + v.shape[axis + 1 :]
            specs.append(pl.BlockSpec(block, partial(lambda at, n, i: tuple(i * (k == at) for k in range(n)), axis, v.ndim)))
        else:
            specs.append(pl.BlockSpec(v.shape, partial(lambda n, i: (0,) * n, v.ndim)))
    whole = [pl.BlockSpec(shape, lambda i: (0, 0)) for shape in shapes]
    count = len(large)
    results = pl.pallas_call(
        partial(hand_over_kernel, count),
        name="hand_over",
        grid=(steps,),
        out_shape=tuple(jax.ShapeDtypeStruct(v.shape, v.dtype) for v in large)
        + tuple(jax.ShapeDtypeStruct(shape, F32) for shape in shapes),
        in_specs=specs + [pl.BlockSpec(smalls.shape, lambda i: (0, 0))],
        out_specs=tuple(specs + whole),
        compiler_params=pltpu.CompilerParams(vmem_limit_bytes=60 << 20),
    )(*large, smalls)
    return results[:count], results[count:]


def shards(
    inputs,
    query_key_value_weight,
    attention_out_weight,
    up_weight,
    down_weight,
    qk_bias,
    value_bias,
    out_bias,
    ffn_in_bias,
    ffn_out_bias,
    norm_gains,
    norm_biases,
    grad_out,
):
    rank_here, ranks = lax.axis_index("fsdp"), lax.axis_size("fsdp")
    _, rows, cols = query_key_value_weight.shape
    pairs = cols // 128
    width = inputs.shape[2]
    fused = ranks == 16 and rows % 16 == 0 and 4 * cols + 2 * up_weight.shape[1] == 12 * PIECE
    small = (
        qk_bias,
        value_bias[None],
        out_bias[None],
        ffn_out_bias[None],
        norm_gains,
        norm_biases,
        ffn_in_bias[None],
    )
    if fused:
        slabs = (query_key_value_weight, attention_out_weight.T, up_weight, down_weight.T)
    else:
        sqkv = query_key_value_weight.reshape(3, rows, pairs, 128)
        sqkv = jnp.transpose(sqkv, (1, 2, 0, 3)).reshape(rows, 3 * cols)
        slabs = (sqkv, attention_out_weight.T, up_weight, down_weight.T)
        small_shapes = small[:6]
        slabs = tuple(lax.all_gather(slab, "fsdp", axis=0, tiled=True) for slab in slabs)
        at_home = (jnp.arange(ranks) == rank_here).astype(F32)[None, :, None]
        vectors = (jnp.concatenate(small[:6], 0)[:, None, :].astype(F32) * at_home).reshape(-1, width)
        inner = (ffn_in_bias[None, None, :].astype(F32) * at_home).reshape(-1, width)
        small = jnp.concatenate([vectors, inner], 0)
        small = lax.psum(jnp.pad(small, ((0, SMALL_ROWS - small.shape[0]), (0, 0))), "fsdp")
    output, grad_input, smalls, grads = layer(fused, inputs, grad_out, slabs, small)
    if fused:
        large, small = hand_over((output, grad_input, *grads), smalls, [piece.shape for piece in small])
        output, grad_input, dqkv, do, dup, ddn = large
        dqk, dvalue, dout, dout2, dgains, dshifts, dinner = small
    else:
        dqkv, do, dup, ddn = [
            lax.psum_scatter(g.reshape(width, -1).astype(F32), "fsdp", scatter_dimension=0, tiled=True)
            for g in grads
        ]
        dqkv = jnp.transpose(dqkv.reshape(rows, pairs, 3, 128), (2, 0, 1, 3)).reshape(3, rows, cols)
        smalls = lax.psum(smalls, ("fsdp", "tp"))
        mine = lax.dynamic_slice_in_dim(smalls[:IN_BIAS], rank_here * rows, rows, 1)
        dqk, dvalue, dout, dout2, dgains, dshifts = [
            mine[row : row + piece.shape[0]] for (_, row), piece in zip(SMALLS, small_shapes)
        ]
        inner_rows = ffn_in_bias.shape[0]
        inner = smalls[IN_BIAS : IN_BIAS + inner_rows * ranks // width].reshape(-1)
        dinner = lax.dynamic_slice_in_dim(inner, rank_here * inner_rows, inner_rows, 0)
    return (
        output,
        grad_input,
        dqkv,
        do.T,
        dup,
        ddn.T,
        dqk,
        dvalue.reshape(-1),
        dout.reshape(-1),
        dinner.reshape(-1),
        dout2.reshape(-1),
        dgains,
        dshifts,
    )


def solution(mesh):
    return jax.shard_map(
        shards,
        mesh=mesh,
        in_specs=(
            P("fsdp", "tp", None),
            P(None, "fsdp", "tp"),
            P("tp", "fsdp"),
            P("fsdp", "tp"),
            P("tp", "fsdp"),
            P(None, "fsdp"),
            P("fsdp"),
            P("fsdp"),
            P("fsdp"),
            P("fsdp"),
            P(None, "fsdp"),
            P(None, "fsdp"),
            P("fsdp", "tp", None),
        ),
        out_specs=(
            P("fsdp", "tp", None),
            P("fsdp", "tp", None),
            P(None, "fsdp", "tp"),
            P("tp", "fsdp"),
            P("fsdp", "tp"),
            P("tp", "fsdp"),
            P(None, "fsdp"),
            P("fsdp"),
            P("fsdp"),
            P("fsdp"),
            P("fsdp"),
            P(None, "fsdp"),
            P(None, "fsdp"),
        ),
        check_vma=False,
    )
```

```python
from functools import partial

import jax
import jax.numpy as jnp
import numpy as np
from jax import lax
from jax.experimental import pallas as pl
from jax.experimental.pallas import tpu as pltpu
from jax.sharding import PartitionSpec as P

HEAD_DIM = 64
EPS = 1e-05
MESH = pl.DeviceIdType.MESH
BF16 = jnp.bfloat16
F32 = jnp.float32
TILE = 256
PIECE = 384
QK_BIAS, VALUE_BIAS, OUT_BIAS, OUT2_BIAS, GAINS, SHIFTS, IN_BIAS, SMALL_ROWS = 0, 2, 3, 4, 5, 7, 9, 16
HOP = -1
SMALLS = (
    ("qk_bias", QK_BIAS),
    ("value_bias", VALUE_BIAS),
    ("out_bias", OUT_BIAS),
    ("ffn_out_bias", OUT2_BIAS),
    ("norm_gains", GAINS),
    ("norm_biases", SHIFTS),
    ("ffn_in_bias", IN_BIAS),
)
GATHER_ORDERS = (
    "abcxy", "abcxy", "aybcx", "xabcy", "aybcx", "aybcx", "axbcy", "aybcx", "axbcy", "abcyx", "yabcx", "xabcy", "xabcy",
)
GATHER_PLAN = (
    ((2, 0), (8, 0), (0, 0), (6, 0), (3, 0), (1, 0)),
    ((8, 1), (0, 1), (2, 1), (5, 0), (7, 0), (4, 0), (1, 1), (10, 0), (0, 2), (3, 1), (7, 1), (11, 0), (4, 1), (2, 2), (1, 2), (0, 3), (9, 0), (5, 1), (12, 0), (11, 1), (3, 2), (1, 3), (4, 2), (0, 4), (6, 1), (2, 3), (3, 3), (1, 4), (2, 4), (6, 2), (3, 4), (4, 3), (5, 2)),
    ((9, 1), (6, 3), (4, 4)),
    (),
    (),
    ((7, 2), (5, 3)),
    (),
    (),
    ((9, 2), (6, 4), (8, 2)),
    (),
    (),
    ((5, 4), (7, 3), (10, 1), (7, 4), (9, 3)),
    (),
    ((11, 2), (10, 2)),
    ((8, 3),),
    ((12, 1),),
    ((8, 4),),
    (),
    (),
    (),
    (),
    ((9, 4), (11, 3), (10, 3)),
    ((12, 2),),
    ((11, 4), (10, 4)),
    ((12, 3),),
    (),
    (),
    (),
    (),
    (),
    ((12, 4),),
    (),
    (),
    (),
    (),
    (),
    (),
    (),
    (),
    (),
    (),
    (),
    (),
    (),
    (),
    (),
    (),
    (),
)
SCATTER_ORDERS = (
    "ycbax", "xcbay", "xcbay", "ycbxa", "ycbax", "xcbay", "xycba", "ycbxa", "yxcba", "xcbya", "xycba", "yxcba",
)
SCATTER_PLAN = (
    (),
    (),
    (),
    (),
    (),
    (),
    (),
    (),
    (),
    (),
    (),
    (),
    ((1, 1),),
    (),
    (),
    (),
    (),
    ((0, 1),),
    (),
    (),
    ((2, 1),),
    ((3, 1), (0, 2)),
    (),
    (),
    ((1, 2),),
    (),
    (),
    ((4, 1),),
    (),
    (),
    ((3, 2),),
    ((5, 1),),
    (),
    (),
    (),
    ((4, 2), (7, 1)),
    (),
    (),
    ((1, 3),),
    ((6, 1), (2, 2)),
    ((0, 3),),
    (),
    ((5, 2),),
    ((9, 1),),
    (),
    ((7, 2),),
    ((HOP, 1), (2, 3), (4, 3), (8, 1), (6, 2)),
    ((9, 2), (3, 3), (5, 3)),
    ((HOP, 2),),
    ((10, 1),),
    ((11, 1), (6, 3), (HOP, 3), (8, 2), (9, 3), (10, 2), (7, 3), (1, 4), (4, 4), (5, 4), (8, 3), (11, 2), (3, 4), (10, 3), (9, 4), (0, 4), (7, 4), (11, 3), (8, 4), (10, 4), (HOP, 4), (6, 4), (9, 5), (2, 4), (4, 5), (5, 5), (11, 4), (2, 5), (0, 5), (1, 5), (6, 5), (3, 5), (7, 5), (10, 5), (8, 5), (11, 5)),
)
BAND = 32


def nn(a, b):
    return jnp.dot(a, b, preferred_element_type=F32)


def nt(a, b):
    return lax.dot_general(a, b, (((1,), (1,)), ((), ())), preferred_element_type=F32)


def tn(a, b):
    return lax.dot_general(a, b, (((0,), (0,)), ((), ())), preferred_element_type=F32)


def place():
    f = lax.axis_index("fsdp")
    return lax.rem(f, 2), lax.rem(f // 2, 2), f // 4, lax.axis_index("tp")


def rank(x, y, z):
    return (z * 2 + y) * 2 + x


def greet(devices):
    barrier = pltpu.get_barrier_semaphore()
    for device in devices:
        pl.semaphore_signal(barrier, inc=1, device_id=device, device_id_type=MESH)


def await_greetings(devices):
    pl.semaphore_wait(pltpu.get_barrier_semaphore(), len(devices))


def remote(source, target, send_sem, recv_sem, device):
    return pltpu.make_async_remote_copy(
        src_ref=source,
        dst_ref=target,
        send_sem=send_sem,
        recv_sem=recv_sem,
        device_id=device,
        device_id_type=MESH,
    )


class Where:
    def __init__(self, condition, copy):
        self.condition, self.copy = condition, copy

    def wait_send(self):
        pl.when(self.condition)(self.copy.wait_send)


class Sends:
    def __init__(self):
        self.copies = []

    def start(self, *args):
        copy = remote(*args)
        copy.start()
        self.copies.append(copy)
        return copy

    def start_where(self, condition, *args):
        copy = remote(*args)
        pl.when(condition)(copy.start)
        self.copies.append(Where(condition, copy))

    def settle(self, copies):
        for copy in copies:
            copy.wait_send()
        self.copies = [c for c in self.copies if not any(c is copy for copy in copies)]

    def finish(self):
        self.settle(list(self.copies))


class Gather:
    SLOT = {"x": 0, "y": 1, "a": 2, "b": 3, "c": 4}

    def __init__(self, pieces, where, send, recv, sends):
        self.pieces, self.send, self.recv, self.sends = pieces, send, recv, sends
        self.x, self.y, self.z, t = where
        x, y, z = self.x, self.y, self.z
        self.half = z // 2
        self.inner = jnp.logical_or(z == 1, z == 2)
        self.outer = jnp.logical_not(self.inner)
        self.pair = z + 1 - 2 * lax.rem(z, 2)
        self.peer = {
            "x": (rank(1 - x, y, z), t),
            "y": (rank(x, 1 - y, z), t),
            "a": (rank(x, y, self.pair), t),
            "b": (rank(x, y, 3 - z), t),
            "c": (rank(x, y, self.pair), t),
        }
        self.orders = GATHER_ORDERS
        self.plan = iter(GATHER_PLAN)

    def view(self, piece, have, **at):
        whole, cols = self.pieces[piece]
        if "c" in have:
            along_z = slice(None)
        elif "a" in have:
            along_z = pl.ds(2 * self.half, 2)
        else:
            along_z = self.z
        index = [at.get("z", along_z)]
        for axis, own in (("y", self.y), ("x", self.x)):
            index.append(at.get(axis, slice(None) if axis in have else own))
        return whole.at[(*index, slice(None), cols)]

    def sems(self, piece, axis):
        slot = self.SLOT[axis]
        return self.send.at[piece, slot], self.recv.at[piece, slot]

    def arrive(self, piece, stage):
        order = self.orders[piece]
        axis, have = order[stage], order[:stage]
        if axis == "a":
            target = self.view(piece, have, z=self.pair)
        elif axis in "bc":
            target = self.view(piece, have, z=pl.ds(2 * (1 - self.half), 2))
        else:
            target = self.view(piece, have, **{axis: 1 - getattr(self, axis)})
        wait = remote(target, target, *self.sems(piece, axis), self.peer["x"]).wait_recv
        if axis in "bc":
            pl.when(self.inner if axis == "b" else self.outer)(wait)
        else:
            wait()

    def step(self, piece, stage):
        order = self.orders[piece]
        axis, have = order[stage], order[:stage]
        if stage:
            self.arrive(piece, stage - 1)
        if axis == "c":
            source = self.view(piece, have, z=pl.ds(2 * (1 - self.half), 2))
        else:
            source = self.view(piece, have)
        args = (source, source, *self.sems(piece, axis), self.peer[axis])
        if axis in "bc":
            self.sends.start_where(self.inner, *args)
        else:
            self.sends.start(*args)

    def turn(self):
        for piece, stage in next(self.plan):
            self.step(piece, stage)

    def need(self, *pieces):
        for piece in pieces:
            self.arrive(piece, len(self.orders[piece]) - 1)
            self.turn()


def slabs_of(order):
    counts, chips, lanes = [], 4, 2
    for axis in order[1:]:
        if axis in "xy":
            counts.append(chips)
            lanes = 1
        elif axis == "a":
            counts.append(lanes)
            chips = 1
        else:
            counts.append(2 * lanes)
            chips = 2
    return counts, [sum(counts[:k]) for k in range(len(counts))]


class Scatter:
    def __init__(self, pieces, where, held, pool, send, recv, sends):
        self.pieces, self.held, self.pool = pieces, held, pool
        self.send, self.recv, self.sends = send, recv, sends
        self.x, self.y, self.z, t = where
        x, y, z = self.x, self.y, self.z
        self.half = z // 2
        self.inner = jnp.logical_or(z == 1, z == 2)
        self.outer = jnp.logical_not(self.inner)
        self.pair = z + 1 - 2 * lax.rem(z, 2)
        self.peer = {
            "x": (rank(1 - x, y, z), t),
            "y": (rank(x, 1 - y, z), t),
            "a": (rank(x, y, self.pair), t),
            "b": (rank(x, y, 3 - z), t),
            "c": (rank(x, y, self.pair), t),
        }
        self.orders = SCATTER_ORDERS
        self.plan = iter(SCATTER_PLAN)
        self.base = [0]
        for order in self.orders:
            self.base.append(self.base[-1] + sum(slabs_of(order)[0]))

    def copies(self, piece, stage):
        order = self.orders[piece]
        axis, done = order[stage], order[:stage]
        if stage == 0:
            grads, cols, _ = self.pieces[piece]
            every, away = slice(None), 1 - getattr(self, axis)
            index = (every, every, away) if axis == "x" else (every, away, every)
            return [(grads.at[(*index, every, cols)], self.held.at[piece], 0)], None, None
        held, pool = self.held, self.pool
        at = self.base[piece] + slabs_of(order)[1][stage - 1]
        lane = "y" if order[0] == "x" else "x"
        own = getattr(self, lane)
        if axis == lane:
            if "a" in done:
                return [(held.at[piece, self.z, 1 - own], pool.at[at], 1)], None, None
            chips, count = (pl.ds(2 * self.half, 2), 2) if "b" in done else (slice(None), 4)
            return [(held.at[piece, chips, 1 - own], pool.at[pl.ds(at, count)], 1)], None, None
        if axis == "a":
            if lane in done:
                return [(held.at[piece, self.pair, own], pool.at[at], 2)], None, None
            return [(held.at[piece, self.pair], pool.at[pl.ds(at, 2)], 2)], None, None
        far = 2 * (1 - self.half)
        slot = 3 if axis == "c" else 5
        senders = self.outer if axis == "c" else self.inner
        if lane in done:
            return [(held.at[piece, pl.ds(far, 2), own], pool.at[pl.ds(at, 2)], slot)], senders, self.inner
        return (
            [(held.at[piece, far + k], pool.at[pl.ds(at + 2 * k, 2)], slot + k) for k in range(2)],
            senders,
            self.inner,
        )

    def emit(self, piece, stage):
        copies, senders, _ = self.copies(piece, stage)
        device = self.peer[self.orders[piece][stage]]
        for source, target, slot in copies:
            args = (source, target, self.send.at[piece, slot], self.recv.at[piece, slot], device)
            if senders is None:
                self.sends.start(*args)
            else:
                self.sends.start_where(senders, *args)

    def first(self, piece):
        self.emit(piece, 0)
        self.turn()

    def absorb(self, piece, stage, final):
        copies, _, receivers = self.copies(piece, stage)
        order = self.orders[piece]
        axis, done = order[stage], order[:stage]
        held, pool = self.held, self.pool

        def wait():
            for _, target, slot in copies:
                sems = self.send.at[piece, slot], self.recv.at[piece, slot]
                remote(target, target, *sems, self.peer["x"]).wait_recv()

        if stage == 0:
            wait()
            grads, cols, _ = self.pieces[piece]
            for q in range(4):
                for o in range(2):
                    mine = grads[q, o, self.x, :, cols] if axis == "x" else grads[q, self.y, o, :, cols]
                    held[piece, q, o] = (mine.astype(F32) + held[piece, q, o].astype(F32)).astype(BF16)
            return
        at = self.base[piece] + slabs_of(order)[1][stage - 1]
        lane = "y" if order[0] == "x" else "x"
        own = getattr(self, lane)
        lanes = [own] if lane in done or axis == lane else [0, 1]
        if axis == lane:
            chips = [self.z] if "a" in done else [2 * self.half, 2 * self.half + 1] if "b" in done else range(4)
        elif axis == "a":
            chips = [self.z]
        else:
            near = 2 * self.half if axis == "b" else 2 * (1 - self.half)
            chips = [near, near + 1]

        def add():
            wait()
            for k, (q, o) in enumerate([(q, o) for q in chips for o in lanes]):
                total = held[piece, q, o].astype(F32) + pool[at + k].astype(F32)
                if final:
                    self.pieces[piece][2](total)
                else:
                    held[piece, q, o] = total.astype(BF16)

        if receivers is None:
            add()
        else:
            pl.when(receivers)(add)

    def turn(self):
        for piece, stage in next(self.plan):
            if piece == HOP:
                self.hops[stage - 1]()
                continue
            self.absorb(piece, stage - 1, stage == len(self.orders[piece]))
            if stage < len(self.orders[piece]):
                self.emit(piece, stage)


def layer_kernel(fused, names, *refs):
    r = dict(zip(names, refs))
    where = x, y, z, t = place()
    partner = (lax.axis_index("fsdp"), 1 - t)
    sends = Sends()
    gy, xs = r["grad_out"], r["inputs"]
    wqkv, wo, wup, wdn = r["wqkv"], r["wo"], r["wup"], r["wdn"]
    gqkv, go, gup, gdn = r["gqkv"], r["go"], r["gup"], r["gdn"]
    X, HB, DF = r["X"], r["HB"], r["DF"]
    DATT = DF
    FQ, FK, VA, SS, DN = r["FQ"], r["FK"], r["VA"], r["SS"], r["DN"]
    DEN, CTX, N1, RS1, DR = r["DEN"], r["CTX"], r["N1"], r["RS1"], r["DR"]
    ACT, GP, DPRE, SB, RB = r["ACT"], r["GP"], r["DPRE"], r["SB"], r["RB"]
    BV, SG, table = r["BV"], r["SG"], r["table"]
    tps, tpr = r["tps"], r["tpr"]
    length, width = X.shape
    local = length // 2
    tiles = local // TILE
    cols = wo.shape[-1]
    hidden = wup.shape[-1]
    pairs = cols // 128
    chunks = length // TILE
    halves = hidden // (2 * PIECE)
    mine, other = t * local, (1 - t) * local

    def rows_at(base, tile):
        return pl.ds(pl.multiple_of(base + tile * TILE, TILE), TILE)

    passed = {}

    def to_partner(source, target, index):
        passed[index] = sends.start(source, target, tps.at[index], tpr.at[index], partner)

    def leave(first):
        sends.settle([passed[first + tile] for tile in range(tiles)])

    def from_partner(target, index):
        remote(target, target, tps.at[index], tpr.at[index], partner).wait_recv()

    def flat(ref, begin=0, size=None):
        size = ref.shape[-1] if size is None else size
        return ref[:, :, :, :, begin : begin + size].reshape(width, size)

    here = pltpu.make_async_copy(xs.at[0], X.at[pl.ds(mine, local)], r["own"].at[0])
    here.start()
    first_up = 2 + pairs
    first_dn = first_up + 2 * halves
    if fused:
        x_peer, y_peer = (rank(1 - x, y, z), t), (rank(x, 1 - y, z), t)
        z_peers = [(rank(x, y, lax.rem(z + k, 4)), t) for k in (1, 2, 3)]
        friends = z_peers + [x_peer, y_peer, partner]
        greet(friends)
        f = lax.axis_index("fsdp")
        Z = r["Z"]
        owns = wqkv.shape[3]
        Z[...] = jnp.zeros_like(Z)
        for name, row in SMALLS:
            piece = r[name]
            Z[row : row + piece.shape[0], 0 : piece.shape[1]] = piece[...].astype(F32)
        inner = r["ffn_in_bias"].shape[1]
        per_row = width // inner
        table_row = lax.broadcasted_iota(jnp.int32, (SMALL_ROWS, width), 0)
        line = jnp.broadcast_to(Z[IN_BIAS : IN_BIAS + 1, :], (8, width))
        line = pltpu.roll(line, lax.rem(f, per_row) * inner, 1)[:1]
        placed = pltpu.roll(Z[...], f * owns, 1)
        own_row = table_row == IN_BIAS + f // per_row
        placed = jnp.where(table_row < IN_BIAS, placed, jnp.where(own_row, line, 0.0))
        r["SM"][z, y, x] = placed.astype(BF16)
        for p in range(pairs):
            for m in range(3):
                begin = p * 384 + m * 128
                wqkv[z, y, x, :, begin : begin + 128] = r["sqkv"][m, :, p * 128 : (p + 1) * 128]
        wo[z, y, x] = r["so"][...]
        wup[z, y, x] = r["sup"][...]
        wdn[z, y, x] = r["sdn"][...]
        span = [slice(k * PIECE, (k + 1) * PIECE) for k in range(max(pairs, 2 * halves))]
        sources = (
            [(r["SM"], slice(0, width))]
            + [(wqkv, span[p]) for p in range(pairs)]
            + [(wo, span[0])]
            + [(wup, span[k]) for k in range(2 * halves)]
            + [(wdn, span[k]) for k in range(2 * halves)]
        )
        gather = Gather(sources, where, r["ags"], r["agr"], sends)
        await_greetings(friends)
        gather.turn()
        turn_in, need = gather.turn, gather.need
    else:
        greet([partner])
        await_greetings([partner])
        turn_in, need = lambda: None, lambda *pieces: None
    to_partner(xs.at[0], X.at[pl.ds(mine, local)], 0)
    SG[...] = jnp.zeros_like(SG)
    r["SI"][...] = jnp.zeros_like(r["SI"])
    here.wait()
    from_partner(X.at[pl.ds(other, local)], 0)
    turn_in()

    lane = lax.broadcasted_iota(jnp.int32, (TILE, 128), 1)
    low = lane < 64

    def swap(v):
        return pltpu.roll(v, 64, 1)

    need(0)
    if fused:
        total = jnp.zeros((SMALL_ROWS, width), F32)
        for a in range(4):
            for b in range(2):
                for c in range(2):
                    total = total + r["SM"][a, b, c].astype(F32)
        BV[...] = total
    else:
        BV[...] = r["small"][...]

    def small_row(row):
        return BV[row : row + 1, :]

    def own_half(row):
        return jnp.where(t == 0, BV[row : row + 1, :cols], BV[row : row + 1, cols:])

    out_bias, out2_bias = small_row(OUT_BIAS), small_row(OUT2_BIAS)
    gain0, gain1 = small_row(GAINS), small_row(GAINS + 1)
    shift0, shift1 = small_row(SHIFTS), small_row(SHIFTS + 1)
    in_bias = [
        jnp.where(t == 0, small_row(IN_BIAS + j), small_row(IN_BIAS + halves + j)) for j in range(halves)
    ]
    bq, bk, bv = own_half(QK_BIAS), own_half(QK_BIAS + 1), own_half(VALUE_BIAS)
    turn_in()

    ahead = lax.broadcasted_iota(jnp.int32, (TILE, TILE), 0) >= lax.broadcasted_iota(
        jnp.int32, (TILE, TILE), 1
    )
    for p in range(pairs):
        need(1 + p)
        at = p * 128
        states = [None, None]
        for i in range(chunks):
            rows = slice(i * TILE, (i + 1) * TILE)
            pre = nn(X[rows, :], flat(wqkv, p * 384, 384))
            cs = table[rows, :]
            q = jnp.maximum(pre[:, :128] + bq[:, at : at + 128], 0.0)
            k = jnp.maximum(pre[:, 128:256] + bk[:, at : at + 128], 0.0)
            v = pre[:, 256:] + bv[:, at : at + 128]
            qs, ks, vs = swap(q), swap(k), swap(v)
            feats = (
                ((jnp.where(low, q, qs) * cs).astype(BF16), (jnp.where(low, qs, q) * cs).astype(BF16)),
                ((jnp.where(low, k, ks) * cs).astype(BF16), (jnp.where(low, ks, k) * cs).astype(BF16)),
                (jnp.where(low, v, 1.0).astype(BF16), jnp.where(low, vs, 1.0).astype(BF16)),
            )
            both = []
            for h in range(2):
                fq, fk, va = (feat[h] for feat in feats)
                FQ[2 * p + h, rows, :], FK[2 * p + h, rows, :], VA[2 * p + h, rows, :] = fq, fk, va
                scores = jnp.where(ahead, nt(fq, fk), 0.0).astype(BF16)
                sums = nn(scores, va)
                if i:
                    before = states[h].astype(BF16)
                    SS[2 * p + h, i] = before
                    sums = sums + nn(fq, before)
                both.append(sums)
                if i + 1 < chunks:
                    grown = tn(fk, va)
                    states[h] = states[h] + grown if i else grown
            num = jnp.where(low, both[0], swap(both[1]))
            den = jnp.where(low, swap(both[0]), both[1])
            DEN[rows, at : at + 128] = den
            CTX[rows, at : at + 128] = (num / jnp.maximum(den, 1.0)).astype(BF16)
            turn_in()

    P = r["P"]

    def bands(body, count):
        def step(b, sums):
            rows = pl.ds(pl.multiple_of(b * BAND, BAND), BAND)
            terms = body(rows, b * BAND)
            return tuple(
                total + jnp.sum(term.reshape(BAND // 8, 8, width), 0) for total, term in zip(sums, terms)
            )

        zero = jnp.zeros((8, width), F32)
        return lax.fori_loop(0, TILE // BAND, step, (zero,) * count, unroll=4)

    def mean(v):
        return jnp.mean(v, -1, keepdims=True)

    def normalize(resid):
        center = resid - mean(resid)
        rstd = lax.rsqrt(mean(center * center) + EPS)
        return center * rstd, rstd

    need(1 + pairs)
    for tile in range(tiles):
        rows = rows_at(other, tile)
        SB[0, tile] = nt(CTX[rows, :], flat(wo)).astype(BF16)
        to_partner(SB.at[0, tile], RB.at[0, tile], 1 + tile)
        turn_in()
    for tile in range(tiles):
        rows = rows_at(mine, tile)
        P[...] = nt(CTX[rows, :], flat(wo))
        from_partner(RB.at[0, tile], 1 + tile)

        def first_norm(band, begin):
            whole = pl.ds(pl.multiple_of(mine + tile * TILE + begin, BAND), BAND)
            local_rows = pl.ds(pl.multiple_of(tile * TILE + begin, BAND), BAND)
            resid = X[whole, :].astype(F32) + (P[band, :] + RB[0, tile, band, :].astype(F32) + out_bias)
            normed, rstd = normalize(resid)
            N1[local_rows, :] = normed
            RS1[local_rows, :] = jnp.broadcast_to(rstd, (BAND, 128))
            HB[whole, :] = (normed * gain0 + shift0).astype(BF16)
            return ()

        bands(first_norm, 0)
        to_partner(HB.at[rows], HB.at[rows], 3 + tile)
        turn_in()

    for j in range(halves):
        need(first_up + 2 * j, first_up + 2 * j + 1)
        for half in range(2):
            if j == 0 and half == 1:
                for tile in range(tiles):
                    from_partner(HB.at[rows_at(other, tile)], 3 + tile)
            begin = j * 2 * PIECE
            for tile in range(tiles):
                rows = rows_at(other if half else mine, tile)
                u = nn(HB[rows, :], flat(wup, begin, 2 * PIECE)) + in_bias[j]
                cdf = 0.5 * (1.0 + lax.erf(u * np.float32(0.5**0.5)))
                pdf = jnp.exp(-0.5 * u * u) * np.float32((2.0 * np.pi) ** -0.5)
                ACT[rows, begin : begin + 2 * PIECE] = (u * cdf).astype(BF16)
                GP[rows, begin : begin + 2 * PIECE] = (cdf + u * pdf).astype(BF16)
                turn_in()

    ACC = r["ACC"]
    early = hidden - PIECE
    need(*range(first_dn, first_dn + 2 * halves - 1))
    for base, partial_sums in ((other, ACC), (mine, DR)):
        for tile in range(tiles):
            partial_sums[rows_at(0, tile), :] = nt(ACT[rows_at(base, tile), :early], flat(wdn, 0, early))
            turn_in()
    need(first_dn + 2 * halves - 1)

    def whole_sum(base, tile, partial_sums):
        late = nt(ACT[rows_at(base, tile), early:], flat(wdn, early, PIECE))
        return partial_sums[rows_at(0, tile), :] + late

    for tile in range(tiles):
        SB[1, tile] = whole_sum(other, tile, ACC).astype(BF16)
        to_partner(SB.at[1, tile], RB.at[1, tile], 5 + tile)
        turn_in()
    N2 = ACC
    for tile in range(tiles):
        rows = rows_at(mine, tile)
        P[...] = whole_sum(mine, tile, DR)
        from_partner(RB.at[1, tile], 5 + tile)

        def second_norm(band, begin):
            whole = pl.ds(pl.multiple_of(mine + tile * TILE + begin, BAND), BAND)
            local_rows = pl.ds(pl.multiple_of(tile * TILE + begin, BAND), BAND)
            h1 = N1[local_rows, :] * gain0 + shift0
            resid = h1 + (P[band, :] + RB[1, tile, band, :].astype(F32)) + out2_bias
            normed, rstd = normalize(resid)
            N2[local_rows, :] = normed
            e = gy[0, local_rows, :].astype(F32) * gain1
            back = rstd * (e - mean(e) - normed * mean(e * normed))
            DR[local_rows, :] = back
            DF[whole, :] = back.astype(BF16)
            return ()

        bands(second_norm, 0)
        to_partner(DF.at[rows], DF.at[rows], 7 + tile)
        turn_in()

    def keep(row, vector):
        SG[row : row + 1, :] = vector


    if fused:

        def write(name, begin):
            def put(total):
                r[name][:, begin : begin + PIECE] = total

            return put

        def write_qkv(p):
            def put(total):
                for m in range(3):
                    r["oqkv"][m, :, p * 128 : (p + 1) * 128] = total[:, m * 128 : (m + 1) * 128]

            return put

        targets = (
            [(gdn, span[k], write("odn", k * PIECE)) for k in range(2 * halves)]
            + [(gup, span[k], write("oup", k * PIECE)) for k in range(2 * halves)]
            + [(go, span[0], write("oo", 0))]
            + [(gqkv, span[p], write_qkv(p)) for p in range(pairs)]
        )
        scatter = Scatter(targets, where, r["held"], r["pool"], r["rss"], r["rsr"], sends)
        first_out, turn_out = scatter.first, scatter.turn
    else:
        first_out, turn_out = lambda piece: None, lambda: None

    def store(ref, begin, value):
        ref[:, :, :, :, begin : begin + value.shape[1]] = value.astype(BF16).reshape(
            ref.shape[:4] + (value.shape[1],)
        )

    for tile in range(tiles):
        from_partner(DF.at[rows_at(other, tile)], 7 + tile)
    for j in range(halves):
        store(gdn, j * 2 * PIECE, tn(DF[...], ACT[:, j * 2 * PIECE : (j + 1) * 2 * PIECE]))
        turn_out()
        first_out(2 * j)
        first_out(2 * j + 1)
    for base in (mine, other):
        for tile in range(tiles):
            rows = rows_at(base, tile)
            for j in range(halves):
                at = slice(j * 2 * PIECE, (j + 1) * 2 * PIECE)
                dact = nn(DF[rows, :], flat(wdn, j * 2 * PIECE, 2 * PIECE))
                du = (dact * GP[rows, at].astype(F32)).astype(BF16)
                GP[rows, at] = du
                sums = jnp.sum(du.astype(F32), 0, keepdims=True)
                r["SI"][j : j + 1, :] = r["SI"][j : j + 1, :] + sums
            turn_out()

    for j in range(halves):
        sums = r["SI"][j : j + 1, :]
        keep(IN_BIAS + j, jnp.where(t == 0, sums, 0.0))
        keep(IN_BIAS + halves + j, jnp.where(t == 0, 0.0, sums))
    leave(1)
    for tile in range(tiles):
        rows = rows_at(other, tile)
        SB[0, tile] = nt(GP[rows, :], flat(wup)).astype(BF16)
        to_partner(SB.at[0, tile], RB.at[0, tile], 9 + tile)
        turn_out()
    for j in range(halves):
        store(gup, j * 2 * PIECE, tn(HB[...], GP[:, j * 2 * PIECE : (j + 1) * 2 * PIECE]))
        turn_out()
        first_out(2 * halves + 2 * j)
        first_out(2 * halves + 2 * j + 1)

    totals = []
    for tile in range(tiles):

        def second_norm_rest(band, begin):
            whole = pl.ds(pl.multiple_of(mine + tile * TILE + begin, BAND), BAND)
            local_rows = pl.ds(pl.multiple_of(tile * TILE + begin, BAND), BAND)
            normed, g = N2[local_rows, :], gy[0, local_rows, :].astype(F32)
            r["output"][0, local_rows, :] = (normed * gain1 + shift1).astype(BF16)
            return DF[whole, :].astype(F32), g * normed, g

        totals.append(bands(second_norm_rest, 3))
        turn_out()
    for row, parts in zip((OUT2_BIAS, GAINS + 1, SHIFTS + 1), zip(*totals)):
        keep(row, jnp.sum(sum(parts[1:], parts[0]), 0, keepdims=True))

    leave(7)
    totals = []
    for tile in range(tiles):
        rows = rows_at(mine, tile)
        P[...] = nt(GP[rows, :], flat(wup))
        from_partner(RB.at[0, tile], 9 + tile)

        def first_norm_back(band, begin):
            whole = pl.ds(pl.multiple_of(mine + tile * TILE + begin, BAND), BAND)
            local_rows = pl.ds(pl.multiple_of(tile * TILE + begin, BAND), BAND)
            g = DR[local_rows, :] + (P[band, :] + RB[0, tile, band, :].astype(F32))
            normed = N1[local_rows, :]
            e = g * gain0
            rstd = RS1[local_rows, :][:, :1]
            back = rstd * (e - mean(e) - normed * mean(e * normed))
            DR[local_rows, :] = back
            low_back = back.astype(BF16)
            DATT[whole, :] = low_back
            return low_back.astype(F32), g * normed, g

        totals.append(bands(first_norm_back, 3))
        to_partner(DATT.at[rows], DATT.at[rows], 11 + tile)
        turn_out()
    sum_da, sum_dn, sum_dh = [
        jnp.sum(sum(parts[1:], parts[0]), 0, keepdims=True) for parts in zip(*totals)
    ]
    keep(OUT_BIAS, sum_da)
    keep(GAINS, sum_dn)
    keep(SHIFTS, sum_dh)

    def project_back(base):
        for tile in range(tiles):
            rows = rows_at(base, tile)
            dctx = nn(DATT[rows, :], flat(wo))
            for p in range(pairs):
                at = slice(p * 128, (p + 1) * 128)
                d, den, ctx = dctx[:, at], DEN[rows, at], CTX[rows, at].astype(F32)
                dnum = d / jnp.maximum(den, 1.0)
                product = d * ctx
                shifted = swap(dnum)
                for h in range(2):
                    inside = low if h == 0 else jnp.logical_not(low)
                    total = den[:, h * 64 : h * 64 + 1]
                    dden = -jnp.sum(jnp.where(inside, product, 0.0), -1, keepdims=True) / total
                    dden = jnp.where(total > 1.0, dden, 0.0)
                    high = dden.astype(BF16).astype(F32)
                    rest = jnp.where(lane == 64, high, jnp.where(lane == 65, dden - high, 0.0))
                    DN[2 * p + h, rows, :] = jnp.where(low, shifted if h else dnum, rest).astype(BF16)
            turn_out()

    project_back(mine)
    for tile in range(tiles):
        from_partner(DATT.at[rows_at(other, tile)], 11 + tile)
    project_back(other)
    store(go, 0, tn(DATT[...], CTX[...]))
    turn_out()
    first_out(4 * halves)

    for p in range(pairs):
        at = p * 384

        states = [None, None]
        for i in reversed(range(chunks)):
            rows = slice(i * TILE, (i + 1) * TILE)
            cs = table[rows, :]
            dqs, dks, dvs = [], [], []
            for h in range(2):
                q, k, va = FQ[2 * p + h, rows, :], FK[2 * p + h, rows, :], VA[2 * p + h, rows, :]
                dn = DN[2 * p + h, rows, :]
                scores = jnp.where(ahead, nt(q, k), 0.0).astype(BF16)
                dscores = jnp.where(ahead, nt(dn, va), 0.0).astype(BF16)
                dq, dk, dv = nn(dscores, k), tn(dscores, q), tn(scores, dn)
                if i:
                    dq = dq + nt(dn, SS[2 * p + h, i])
                if i + 1 < chunks:
                    later = states[h].astype(BF16)
                    dk = dk + nt(va, later)
                    dv = dv + nn(k, later)
                if i:
                    grown = tn(q, dn)
                    states[h] = states[h] + grown if i + 1 < chunks else grown
                dq, dk = dq * cs, dk * cs
                dqs.append(dq + swap(dq))
                dks.append(dk + swap(dk))
                dvs.append(dv)

            def live(feat):
                a, b = feat[2 * p, rows, :].astype(F32), feat[2 * p + 1, rows, :].astype(F32)
                return jnp.where(low, a, swap(b)) > 0.0

            dq = jnp.where(live(FQ), jnp.where(low, dqs[0], dqs[1]), 0.0)
            dk = jnp.where(live(FK), jnp.where(low, dks[0], dks[1]), 0.0)
            dv = jnp.where(low, dvs[0], swap(dvs[1]))
            DPRE[rows, at : at + 384] = jnp.concatenate([dq, dk, dv], 1).astype(BF16)
            turn_out()
        piece = DPRE[:, at : at + 384]
        store(gqkv, at, tn(X[...], piece))
        sums = jnp.sum(piece.astype(F32), 0, keepdims=True)
        for m, row in enumerate((QK_BIAS, QK_BIAS + 1, VALUE_BIAS)):
            here_sums = sums[:, m * 128 : (m + 1) * 128]
            SG[row : row + 1, p * 128 : (p + 1) * 128] = jnp.where(t == 0, here_sums, 0.0)
            begin = cols + p * 128
            SG[row : row + 1, begin : begin + 128] = jnp.where(t == 0, 0.0, here_sums)
        turn_out()
        first_out(4 * halves + 1 + p)

    leave(5)
    if fused:
        Q, ss, sr = r["Q"], r["sms"], r["smr"]

        def arrive(slot, index):
            remote(Q.at[slot], Q.at[slot], ss.at[index], sr.at[index], partner).wait_recv()

        def hop(slot, index, before, device):
            arrive(slot, index)
            Q[slot + 1] = before[...] + Q[slot]
            sends.start(Q.at[slot + 1], Q.at[slot + 2], ss.at[index + 1], sr.at[index + 1], device)

        def fan_out():
            arrive(4, 2)
            Q[5] = Q[3] + Q[4]
            for k in range(3):
                sends.start(Q.at[5], Q.at[6 + k], ss.at[3 + k], sr.at[3 + k], z_peers[k])

        def collect():
            for k in range(3):
                arrive(6 + k, 3 + k)

        scatter.hops = (
            lambda: hop(0, 0, SG, x_peer),
            lambda: hop(2, 1, Q.at[1], y_peer),
            fan_out,
            collect,
        )
        sends.start(SG, Q.at[0], ss.at[0], sr.at[0], partner)
    for tile in range(tiles):
        rows = rows_at(other, tile)
        SB[1, tile] = nt(DPRE[rows, :], flat(wqkv)).astype(BF16)
        to_partner(SB.at[1, tile], RB.at[1, tile], 13 + tile)
        turn_out()
    for tile in range(tiles):
        rows, here_rows = rows_at(mine, tile), rows_at(0, tile)
        part = nt(DPRE[rows, :], flat(wqkv))
        from_partner(RB.at[1, tile], 13 + tile)
        r["grad_input"][0, here_rows, :] = DR[here_rows, :] + (part + RB[1, tile].astype(F32))
        turn_out()
    if fused:
        turn_out()
        total = Q[5] + Q[6] + Q[7] + Q[8]
        owned = pltpu.roll(total, lax.rem(width - f * owns, width), 1)
        line = jnp.sum(jnp.where(own_row, total, 0.0), 0, keepdims=True)
        line = jnp.broadcast_to(line, (8, width))
        line = pltpu.roll(line, lax.rem(width - lax.rem(f, per_row) * inner, width), 1)[:1]
        r["smalls"][...] = jnp.where(table_row < IN_BIAS, owned, line)
    else:
        r["smalls"][...] = SG[...]
    sends.finish()


def layer(fused, inputs, grad_out, slabs, small):
    sqkv, so, sup, sdn = slabs
    _, local, width = inputs.shape
    length, cols, hidden = 2 * local, sqkv.shape[-1] if fused else so.shape[-1], sup.shape[-1]
    heads, chunks, tiles = cols // HEAD_DIM, length // TILE, local // TILE
    part = width // 16
    lead = (4, 2, 2, part)
    angles = np.pi / 2.0 * np.arange(length, dtype=np.float64) / length
    table = np.concatenate(
        [np.repeat(np.cos(angles)[:, None], 64, 1), np.repeat(np.sin(angles)[:, None], 64, 1)], 1
    ).astype(np.float32)
    vmem = pl.BlockSpec(memory_space=pltpu.VMEM)
    hbm = pl.BlockSpec(memory_space=pl.ANY)
    dma = pltpu.SemaphoreType.DMA
    sizes = dict(qkv=3 * cols, o=cols, up=hidden, dn=hidden)
    pieces = (4 * cols + 2 * hidden) // PIECE

    ins = [("inputs", inputs, hbm), ("grad_out", grad_out, vmem), ("table", jnp.asarray(table), vmem)]
    if fused:
        ins += [("sqkv", sqkv, vmem), ("so", so, vmem), ("sup", sup, vmem), ("sdn", sdn, vmem)]
        ins += [(name, piece, vmem) for (name, _), piece in zip(SMALLS, small)]
    else:
        wholes = [slab.reshape(lead + slab.shape[-1:]) for slab in slabs]
        ins += [(name, value, vmem) for name, value in zip(("wqkv", "wo", "wup", "wdn"), wholes)]
        ins += [("small", small, vmem)]

    outs = [
        ("output", (1, local, width), BF16),
        ("grad_input", (1, local, width), F32),
        ("smalls", (SMALL_ROWS, width), F32),
    ]
    if fused:
        outs += [
            ("oqkv", (3, part, cols), F32),
            ("oo", (part, cols), F32),
            ("oup", (part, hidden), F32),
            ("odn", (part, hidden), F32),
        ]
    else:
        outs += [("g" + name, lead + (size,), BF16) for name, size in sizes.items()]

    def v(*shape, dtype=BF16):
        return pltpu.VMEM(shape, dtype)

    scratch = dict(
        X=v(length, width),
        HB=v(length, width),
        DF=v(length, width),
        FQ=v(heads, length, 128),
        FK=v(heads, length, 128),
        VA=v(heads, length, 128),
        DN=v(heads, length, 128),
        SS=v(heads, chunks, 128, 128),
        DEN=v(length, cols, dtype=F32),
        CTX=v(length, cols),
        N1=v(local, width, dtype=F32),
        RS1=v(local, 128, dtype=F32),
        DR=v(local, width, dtype=F32),
        ACT=v(length, hidden),
        GP=v(length, hidden),
        DPRE=v(length, 3 * cols),
        SB=v(2, tiles, TILE, width),
        RB=v(2, tiles, TILE, width),
        P=v(TILE, width, dtype=F32),
        ACC=v(local, width, dtype=F32),
        BV=v(SMALL_ROWS, width, dtype=F32),
        SG=v(SMALL_ROWS, width, dtype=F32),
        SI=v(8, 2 * PIECE, dtype=F32),
        tps=dma((16,)),
        tpr=dma((16,)),
        own=dma((1,)),
    )
    if fused:
        scratch.update({"w" + name: v(*lead, size) for name, size in sizes.items()})
        scratch.update({"g" + name: v(*lead, size) for name, size in sizes.items()})
        scratch.update(
            SM=v(4, 2, 2, SMALL_ROWS, width),
            Z=v(SMALL_ROWS, width, dtype=F32),
            Q=v(9, SMALL_ROWS, width, dtype=F32),
            held=v(pieces, 4, 2, part, PIECE),
            pool=v(sum(sum(slabs_of(order)[0]) for order in SCATTER_ORDERS), part, PIECE),
            ags=dma((pieces + 1, 5)),
            agr=dma((pieces + 1, 5)),
            rss=dma((pieces, 7)),
            rsr=dma((pieces, 7)),
            sms=dma((6,)),
            smr=dma((6,)),
        )
    names = [name for name, _, _ in ins] + [name for name, _, _ in outs] + list(scratch)
    results = pl.pallas_call(
        partial(layer_kernel, fused, names),
        name="layer",
        out_shape=tuple(jax.ShapeDtypeStruct(shape, dtype) for _, shape, dtype in outs),
        in_specs=[spec for _, _, spec in ins],
        out_specs=tuple(vmem for _ in outs),
        scratch_shapes=list(scratch.values()),
        compiler_params=pltpu.CompilerParams(
            collective_id=0, has_side_effects=True, vmem_limit_bytes=64 << 20
        ),
    )(*[value for _, value, _ in ins])
    output, grad_input, smalls, *grads = results
    return output, grad_input, smalls, grads


def hand_over_kernel(count, *refs):
    large, smalls, targets, pieces = refs[:count], refs[count], refs[count + 1 : 2 * count + 1], refs[2 * count + 1 :]
    for source, target in zip(large, targets):
        target[...] = source[...]
    for (_, row), piece in zip(SMALLS, pieces):
        piece[...] = smalls[row : row + piece.shape[0], 0 : piece.shape[1]]


def hand_over(large, smalls, shapes):
    steps = 4
    specs = []
    for v in large:
        axis = 1 if v.shape[0] == 1 else v.ndim - 1
        if v.shape[axis] % (steps * 128) == 0:
            block = v.shape[:axis] + (v.shape[axis] // steps,) + v.shape[axis + 1 :]
            specs.append(pl.BlockSpec(block, partial(lambda at, n, i: tuple(i * (k == at) for k in range(n)), axis, v.ndim)))
        else:
            specs.append(pl.BlockSpec(v.shape, partial(lambda n, i: (0,) * n, v.ndim)))
    whole = [pl.BlockSpec(shape, lambda i: (0, 0)) for shape in shapes]
    count = len(large)
    results = pl.pallas_call(
        partial(hand_over_kernel, count),
        name="hand_over",
        grid=(steps,),
        out_shape=tuple(jax.ShapeDtypeStruct(v.shape, v.dtype) for v in large)
        + tuple(jax.ShapeDtypeStruct(shape, F32) for shape in shapes),
        in_specs=specs + [pl.BlockSpec(smalls.shape, lambda i: (0, 0))],
        out_specs=tuple(specs + whole),
        compiler_params=pltpu.CompilerParams(vmem_limit_bytes=60 << 20),
    )(*large, smalls)
    return results[:count], results[count:]


def shards(
    inputs,
    query_key_value_weight,
    attention_out_weight,
    up_weight,
    down_weight,
    qk_bias,
    value_bias,
    out_bias,
    ffn_in_bias,
    ffn_out_bias,
    norm_gains,
    norm_biases,
    grad_out,
):
    rank_here, ranks = lax.axis_index("fsdp"), lax.axis_size("fsdp")
    _, rows, cols = query_key_value_weight.shape
    pairs = cols // 128
    width = inputs.shape[2]
    fused = ranks == 16 and rows % 16 == 0 and 4 * cols + 2 * up_weight.shape[1] == 12 * PIECE
    small = (
        qk_bias,
        value_bias[None],
        out_bias[None],
        ffn_out_bias[None],
        norm_gains,
        norm_biases,
        ffn_in_bias[None],
    )
    if fused:
        slabs = (query_key_value_weight, attention_out_weight.T, up_weight, down_weight.T)
    else:
        sqkv = query_key_value_weight.reshape(3, rows, pairs, 128)
        sqkv = jnp.transpose(sqkv, (1, 2, 0, 3)).reshape(rows, 3 * cols)
        slabs = (sqkv, attention_out_weight.T, up_weight, down_weight.T)
        small_shapes = small[:6]
        slabs = tuple(lax.all_gather(slab, "fsdp", axis=0, tiled=True) for slab in slabs)
        at_home = (jnp.arange(ranks) == rank_here).astype(F32)[None, :, None]
        vectors = (jnp.concatenate(small[:6], 0)[:, None, :].astype(F32) * at_home).reshape(-1, width)
        inner = (ffn_in_bias[None, None, :].astype(F32) * at_home).reshape(-1, width)
        small = jnp.concatenate([vectors, inner], 0)
        small = lax.psum(jnp.pad(small, ((0, SMALL_ROWS - small.shape[0]), (0, 0))), "fsdp")
    output, grad_input, smalls, grads = layer(fused, inputs, grad_out, slabs, small)
    if fused:
        large, small = hand_over((output, grad_input, *grads), smalls, [piece.shape for piece in small])
        output, grad_input, dqkv, do, dup, ddn = large
        dqk, dvalue, dout, dout2, dgains, dshifts, dinner = small
    else:
        dqkv, do, dup, ddn = [
            lax.psum_scatter(g.reshape(width, -1).astype(F32), "fsdp", scatter_dimension=0, tiled=True)
            for g in grads
        ]
        dqkv = jnp.transpose(dqkv.reshape(rows, pairs, 3, 128), (2, 0, 1, 3)).reshape(3, rows, cols)
        smalls = lax.psum(smalls, ("fsdp", "tp"))
        mine = lax.dynamic_slice_in_dim(smalls[:IN_BIAS], rank_here * rows, rows, 1)
        dqk, dvalue, dout, dout2, dgains, dshifts = [
            mine[row : row + piece.shape[0]] for (_, row), piece in zip(SMALLS, small_shapes)
        ]
        inner_rows = ffn_in_bias.shape[0]
        inner = smalls[IN_BIAS : IN_BIAS + inner_rows * ranks // width].reshape(-1)
        dinner = lax.dynamic_slice_in_dim(inner, rank_here * inner_rows, inner_rows, 0)
    return (
        output,
        grad_input,
        dqkv,
        do.T,
        dup,
        ddn.T,
        dqk,
        dvalue.reshape(-1),
        dout.reshape(-1),
        dinner.reshape(-1),
        dout2.reshape(-1),
        dgains,
        dshifts,
    )


def solution(mesh):
    return jax.shard_map(
        shards,
        mesh=mesh,
        in_specs=(
            P("fsdp", "tp", None),
            P(None, "fsdp", "tp"),
            P("tp", "fsdp"),
            P("fsdp", "tp"),
            P("tp", "fsdp"),
            P(None, "fsdp"),
            P("fsdp"),
            P("fsdp"),
            P("fsdp"),
            P("fsdp"),
            P(None, "fsdp"),
            P(None, "fsdp"),
            P("fsdp", "tp", None),
        ),
        out_specs=(
            P("fsdp", "tp", None),
            P("fsdp", "tp", None),
            P(None, "fsdp", "tp"),
            P("tp", "fsdp"),
            P("fsdp", "tp"),
            P("tp", "fsdp"),
            P(None, "fsdp"),
            P("fsdp"),
            P("fsdp"),
            P("fsdp"),
            P("fsdp"),
            P(None, "fsdp"),
            P(None, "fsdp"),
        ),
        check_vma=False,
    )
```

```python
from functools import partial

import jax
import jax.numpy as jnp
import numpy as np
from jax import lax
from jax.experimental import pallas as pl
from jax.experimental.pallas import tpu as pltpu
from jax.sharding import PartitionSpec as P

HEAD_DIM = 64
EPS = 1e-05
MESH = pl.DeviceIdType.MESH
BF16 = jnp.bfloat16
F32 = jnp.float32
TILE = 256
PIECE = 384
QK_BIAS, VALUE_BIAS, OUT_BIAS, OUT2_BIAS, GAINS, SHIFTS, IN_BIAS, SMALL_ROWS = 0, 2, 3, 4, 5, 7, 9, 16
HOP = -1
SMALLS = (
    ("qk_bias", QK_BIAS),
    ("value_bias", VALUE_BIAS),
    ("out_bias", OUT_BIAS),
    ("ffn_out_bias", OUT2_BIAS),
    ("norm_gains", GAINS),
    ("norm_biases", SHIFTS),
    ("ffn_in_bias", IN_BIAS),
)
GATHER_ORDERS = (
    "abcxy", "abcxy", "aybcx", "aybcx", "axbcy", "aybcx", "xabcy", "aybcx", "axbcy", "abcyx", "yabcx", "axbcy", "xabcy",
)
GATHER_PLAN = (
    ((8, 0), (2, 0), (0, 0), (1, 0), (3, 0)),
    ((0, 1), (2, 1), (4, 0), (1, 1), (11, 0), (7, 0), (8, 1), (3, 1), (0, 2), (6, 0), (4, 1), (2, 2), (5, 0), (1, 2), (9, 0), (0, 3), (10, 0), (7, 1), (6, 1), (5, 1), (3, 2), (4, 2), (1, 3), (11, 1), (2, 3), (0, 4), (3, 3), (12, 0), (6, 2), (5, 2), (1, 4), (2, 4), (7, 2), (4, 3), (3, 4)),
    ((4, 4), (8, 2), (9, 1), (6, 3), (11, 2)),
    ((6, 4), (5, 3)),
    ((5, 4),),
    (),
    (),
    ((10, 1),),
    ((7, 3),),
    (),
    ((9, 2),),
    ((8, 3),),
    (),
    ((9, 3), (12, 1), (7, 4)),
    ((10, 2),),
    ((11, 3),),
    ((8, 4),),
    (),
    (),
    (),
    ((9, 4), (10, 3), (12, 2)),
    (),
    ((11, 4),),
    (),
    ((12, 3),),
    (),
    (),
    ((10, 4),),
    ((12, 4),),
    (),
    (),
    (),
    (),
    (),
    (),
    (),
    (),
    (),
    (),
    (),
    (),
    (),
    (),
    (),
    (),
    (),
    (),
    (),
)
SCATTER_ORDERS = (
    "ycbax", "xcbay", "ycbax", "xcbay", "ycbxa", "xcbay", "xycba", "ycbxa", "yxcba", "xcbya", "xycba", "yxcba",
)
SCATTER_PLAN = (
    (),
    (),
    (),
    (),
    (),
    (),
    (),
    (),
    (),
    (),
    (),
    (),
    (),
    (),
    (),
    (),
    (),
    ((0, 1), (1, 1)),
    (),
    (),
    (),
    (),
    (),
    ((3, 1),),
    ((0, 2), (1, 2)),
    ((2, 1),),
    (),
    (),
    ((4, 1), (5, 1)),
    ((0, 3),),
    (),
    (),
    ((2, 2),),
    (),
    (),
    ((7, 1), (6, 1)),
    ((4, 2), (1, 3), (3, 2)),
    (),
    (),
    (),
    (),
    (),
    ((5, 2),),
    ((9, 1),),
    (),
    (),
    ((HOP, 1),),
    ((7, 2), (8, 1)),
    ((6, 2), (2, 3), (5, 3), (HOP, 2), (9, 2), (3, 3), (10, 1), (4, 3)),
    ((6, 3), (11, 1), (8, 2)),
    ((HOP, 3), (7, 3), (9, 3), (1, 4), (2, 4), (0, 4), (8, 3), (10, 2), (HOP, 4), (11, 2), (3, 4), (6, 4), (10, 3), (4, 4), (7, 4), (11, 3), (8, 4), (HOP, 5), (4, 5), (5, 4), (10, 4), (1, 5), (3, 5), (9, 4), (11, 4), (5, 5), (6, 5), (10, 5), (HOP, 6), (9, 5), (8, 5), (2, 5), (0, 5), (11, 5), (7, 5)),
)
BAND = 32


def nn(a, b):
    return jnp.dot(a, b, preferred_element_type=F32)


def nt(a, b):
    return lax.dot_general(a, b, (((1,), (1,)), ((), ())), preferred_element_type=F32)


def tn(a, b):
    return lax.dot_general(a, b, (((0,), (0,)), ((), ())), preferred_element_type=F32)


def place():
    f = lax.axis_index("fsdp")
    return lax.rem(f, 2), lax.rem(f // 2, 2), f // 4, lax.axis_index("tp")


def rank(x, y, z):
    return (z * 2 + y) * 2 + x


def greet(devices):
    barrier = pltpu.get_barrier_semaphore()
    for device in devices:
        pl.semaphore_signal(barrier, inc=1, device_id=device, device_id_type=MESH)


def await_greetings(count):
    pl.semaphore_wait(pltpu.get_barrier_semaphore(), count)


def remote(source, target, send_sem, recv_sem, device):
    return pltpu.make_async_remote_copy(
        src_ref=source,
        dst_ref=target,
        send_sem=send_sem,
        recv_sem=recv_sem,
        device_id=device,
        device_id_type=MESH,
    )


class Where:
    def __init__(self, condition, copy):
        self.condition, self.copy = condition, copy

    def wait_send(self):
        pl.when(self.condition)(self.copy.wait_send)


class Sends:
    def __init__(self):
        self.copies = []

    def start(self, *args):
        copy = remote(*args)
        copy.start()
        self.copies.append(copy)
        return copy

    def start_where(self, condition, *args):
        copy = remote(*args)
        pl.when(condition)(copy.start)
        self.copies.append(Where(condition, copy))

    def settle(self, copies):
        for copy in copies:
            copy.wait_send()
        self.copies = [c for c in self.copies if not any(c is copy for copy in copies)]

    def finish(self):
        self.settle(list(self.copies))


class Gather:
    SLOT = {"x": 0, "y": 1, "a": 2, "b": 3, "c": 4}

    def __init__(self, pieces, where, send, recv, sends):
        self.pieces, self.send, self.recv, self.sends = pieces, send, recv, sends
        self.x, self.y, self.z, t = where
        x, y, z = self.x, self.y, self.z
        self.half = z // 2
        self.inner = jnp.logical_or(z == 1, z == 2)
        self.outer = jnp.logical_not(self.inner)
        self.pair = z + 1 - 2 * lax.rem(z, 2)
        self.peer = {
            "x": (rank(1 - x, y, z), t),
            "y": (rank(x, 1 - y, z), t),
            "a": (rank(x, y, self.pair), t),
            "b": (rank(x, y, 3 - z), t),
            "c": (rank(x, y, self.pair), t),
        }
        self.orders = GATHER_ORDERS
        self.plan = iter(GATHER_PLAN)

    def view(self, piece, have, **at):
        whole, cols = self.pieces[piece]
        if "c" in have:
            along_z = slice(None)
        elif "a" in have:
            along_z = pl.ds(2 * self.half, 2)
        else:
            along_z = self.z
        index = [at.get("z", along_z)]
        for axis, own in (("y", self.y), ("x", self.x)):
            index.append(at.get(axis, slice(None) if axis in have else own))
        return whole.at[(*index, slice(None), cols)]

    def sems(self, piece, axis):
        slot = self.SLOT[axis]
        return self.send.at[piece, slot], self.recv.at[piece, slot]

    def arrive(self, piece, stage):
        order = self.orders[piece]
        axis, have = order[stage], order[:stage]
        if axis == "a":
            target = self.view(piece, have, z=self.pair)
        elif axis in "bc":
            target = self.view(piece, have, z=pl.ds(2 * (1 - self.half), 2))
        else:
            target = self.view(piece, have, **{axis: 1 - getattr(self, axis)})
        wait = remote(target, target, *self.sems(piece, axis), self.peer["x"]).wait_recv
        if axis in "bc":
            pl.when(self.inner if axis == "b" else self.outer)(wait)
        else:
            wait()

    def step(self, piece, stage):
        order = self.orders[piece]
        axis, have = order[stage], order[:stage]
        if stage:
            self.arrive(piece, stage - 1)
        if axis == "c":
            source = self.view(piece, have, z=pl.ds(2 * (1 - self.half), 2))
        else:
            source = self.view(piece, have)
        args = (source, source, *self.sems(piece, axis), self.peer[axis])
        if axis in "bc":
            self.sends.start_where(self.inner, *args)
        else:
            self.sends.start(*args)

    def turn(self):
        for piece, stage in next(self.plan):
            self.step(piece, stage)

    def need(self, *pieces):
        for piece in pieces:
            self.arrive(piece, len(self.orders[piece]) - 1)
            self.turn()


def slabs_of(order):
    counts, chips, lanes = [], 4, 2
    for axis in order[1:]:
        if axis in "xy":
            counts.append(chips)
            lanes = 1
        elif axis == "a":
            counts.append(lanes)
            chips = 1
        else:
            counts.append(2 * lanes)
            chips = 2
    return counts, [sum(counts[:k]) for k in range(len(counts))]


class Scatter:
    def __init__(self, pieces, where, held, pool, send, recv, sends):
        self.pieces, self.held, self.pool = pieces, held, pool
        self.send, self.recv, self.sends = send, recv, sends
        self.x, self.y, self.z, t = where
        x, y, z = self.x, self.y, self.z
        self.half = z // 2
        self.inner = jnp.logical_or(z == 1, z == 2)
        self.outer = jnp.logical_not(self.inner)
        self.pair = z + 1 - 2 * lax.rem(z, 2)
        self.peer = {
            "x": (rank(1 - x, y, z), t),
            "y": (rank(x, 1 - y, z), t),
            "a": (rank(x, y, self.pair), t),
            "b": (rank(x, y, 3 - z), t),
            "c": (rank(x, y, self.pair), t),
        }
        self.orders = SCATTER_ORDERS
        self.plan = iter(SCATTER_PLAN)
        self.base = [0]
        for order in self.orders:
            self.base.append(self.base[-1] + sum(slabs_of(order)[0]))

    def copies(self, piece, stage):
        order = self.orders[piece]
        axis, done = order[stage], order[:stage]
        if stage == 0:
            grads, cols, _ = self.pieces[piece]
            every, away = slice(None), 1 - getattr(self, axis)
            index = (every, every, away) if axis == "x" else (every, away, every)
            return [(grads.at[(*index, every, cols)], self.held.at[piece], 0)], None, None
        held, pool = self.held, self.pool
        at = self.base[piece] + slabs_of(order)[1][stage - 1]
        lane = "y" if order[0] == "x" else "x"
        own = getattr(self, lane)
        if axis == lane:
            if "a" in done:
                return [(held.at[piece, self.z, 1 - own], pool.at[at], 1)], None, None
            chips, count = (pl.ds(2 * self.half, 2), 2) if "b" in done else (slice(None), 4)
            return [(held.at[piece, chips, 1 - own], pool.at[pl.ds(at, count)], 1)], None, None
        if axis == "a":
            if lane in done:
                return [(held.at[piece, self.pair, own], pool.at[at], 2)], None, None
            return [(held.at[piece, self.pair], pool.at[pl.ds(at, 2)], 2)], None, None
        far = 2 * (1 - self.half)
        slot = 3 if axis == "c" else 5
        senders = self.outer if axis == "c" else self.inner
        if lane in done:
            return [(held.at[piece, pl.ds(far, 2), own], pool.at[pl.ds(at, 2)], slot)], senders, self.inner
        return (
            [(held.at[piece, far + k], pool.at[pl.ds(at + 2 * k, 2)], slot + k) for k in range(2)],
            senders,
            self.inner,
        )

    def emit(self, piece, stage):
        copies, senders, _ = self.copies(piece, stage)
        device = self.peer[self.orders[piece][stage]]
        for source, target, slot in copies:
            args = (source, target, self.send.at[piece, slot], self.recv.at[piece, slot], device)
            if senders is None:
                self.sends.start(*args)
            else:
                self.sends.start_where(senders, *args)

    def first(self, piece):
        self.emit(piece, 0)
        self.turn()

    def absorb(self, piece, stage, final):
        copies, _, receivers = self.copies(piece, stage)
        order = self.orders[piece]
        axis, done = order[stage], order[:stage]
        held, pool = self.held, self.pool

        def wait():
            for _, target, slot in copies:
                sems = self.send.at[piece, slot], self.recv.at[piece, slot]
                remote(target, target, *sems, self.peer["x"]).wait_recv()

        if stage == 0:
            wait()
            grads, cols, _ = self.pieces[piece]
            for q in range(4):
                for o in range(2):
                    mine = grads[q, o, self.x, :, cols] if axis == "x" else grads[q, self.y, o, :, cols]
                    held[piece, q, o] = (mine.astype(F32) + held[piece, q, o].astype(F32)).astype(BF16)
            return
        at = self.base[piece] + slabs_of(order)[1][stage - 1]
        lane = "y" if order[0] == "x" else "x"
        own = getattr(self, lane)
        lanes = [own] if lane in done or axis == lane else [0, 1]
        if axis == lane:
            chips = [self.z] if "a" in done else [2 * self.half, 2 * self.half + 1] if "b" in done else range(4)
        elif axis == "a":
            chips = [self.z]
        else:
            near = 2 * self.half if axis == "b" else 2 * (1 - self.half)
            chips = [near, near + 1]

        def add():
            wait()
            for k, (q, o) in enumerate([(q, o) for q in chips for o in lanes]):
                total = held[piece, q, o].astype(F32) + pool[at + k].astype(F32)
                if final:
                    self.pieces[piece][2](total)
                else:
                    held[piece, q, o] = total.astype(BF16)

        if receivers is None:
            add()
        else:
            pl.when(receivers)(add)

    def turn(self):
        for piece, stage in next(self.plan):
            if piece == HOP:
                self.hops[stage - 1]()
                continue
            self.absorb(piece, stage - 1, stage == len(self.orders[piece]))
            if stage < len(self.orders[piece]):
                self.emit(piece, stage)


def layer_kernel(fused, names, *refs):
    r = dict(zip(names, refs))
    where = x, y, z, t = place()
    partner = (lax.axis_index("fsdp"), 1 - t)
    sends = Sends()
    gy, xs = r["grad_out"], r["inputs"]
    wqkv, wo, wup, wdn = r["wqkv"], r["wo"], r["wup"], r["wdn"]
    gqkv, go, gup, gdn = r["gqkv"], r["go"], r["gup"], r["gdn"]
    X, HB, DF = r["X"], r["HB"], r["DF"]
    DATT = DF
    FQ, FK, VA, SS, DN = r["FQ"], r["FK"], r["VA"], r["SS"], r["DN"]
    DEN, CTX, N1, RS1, DR = r["DEN"], r["CTX"], r["N1"], r["RS1"], r["DR"]
    ACT, GP, DPRE, SB, RB = r["ACT"], r["GP"], r["DPRE"], r["SB"], r["RB"]
    BV, SG, table = r["BV"], r["SG"], r["table"]
    tps, tpr = r["tps"], r["tpr"]
    length, width = X.shape
    local = length // 2
    tiles = local // TILE
    cols = wo.shape[-1]
    hidden = wup.shape[-1]
    pairs = cols // 128
    chunks = length // TILE
    halves = hidden // (2 * PIECE)
    mine, other = t * local, (1 - t) * local

    def rows_at(base, tile):
        return pl.ds(pl.multiple_of(base + tile * TILE, TILE), TILE)

    passed = {}

    def to_partner(source, target, index):
        passed[index] = sends.start(source, target, tps.at[index], tpr.at[index], partner)

    def leave(first):
        sends.settle([passed[first + tile] for tile in range(tiles)])

    def from_partner(target, index):
        remote(target, target, tps.at[index], tpr.at[index], partner).wait_recv()

    def flat(ref, begin=0, size=None):
        size = ref.shape[-1] if size is None else size
        return ref[:, :, :, :, begin : begin + size].reshape(width, size)

    here = pltpu.make_async_copy(xs.at[0], X.at[pl.ds(mine, local)], r["own"].at[0])
    here.start()
    first_up = 2 + pairs
    first_dn = first_up + 2 * halves
    if fused:
        x_peer, y_peer = (rank(1 - x, y, z), t), (rank(x, 1 - y, z), t)
        central = jnp.logical_or(z == 1, z == 2)
        pair_peer = (rank(x, y, z + 1 - 2 * lax.rem(z, 2)), t)
        across_peer = (rank(x, y, 3 - z), t)
        friends = [x_peer, y_peer, pair_peer, partner]
        greet(friends)
        pl.when(central)(lambda: greet([across_peer]))
        f = lax.axis_index("fsdp")
        Z = r["Z"]
        owns = wqkv.shape[3]
        Z[...] = jnp.zeros_like(Z)
        for name, row in SMALLS:
            piece = r[name]
            Z[row : row + piece.shape[0], 0 : piece.shape[1]] = piece[...].astype(F32)
        inner = r["ffn_in_bias"].shape[1]
        per_row = width // inner
        table_row = lax.broadcasted_iota(jnp.int32, (SMALL_ROWS, width), 0)
        line = jnp.broadcast_to(Z[IN_BIAS : IN_BIAS + 1, :], (8, width))
        line = pltpu.roll(line, lax.rem(f, per_row) * inner, 1)[:1]
        placed = pltpu.roll(Z[...], f * owns, 1)
        own_row = table_row == IN_BIAS + f // per_row
        placed = jnp.where(table_row < IN_BIAS, placed, jnp.where(own_row, line, 0.0))
        r["SM"][z, y, x] = placed.astype(BF16)
        for p in range(pairs):
            for m in range(3):
                begin = p * 384 + m * 128
                wqkv[z, y, x, :, begin : begin + 128] = r["sqkv"][m, :, p * 128 : (p + 1) * 128]
        wo[z, y, x] = r["so"][...]
        wup[z, y, x] = r["sup"][...]
        wdn[z, y, x] = r["sdn"][...]
        span = [slice(k * PIECE, (k + 1) * PIECE) for k in range(max(pairs, 2 * halves))]
        sources = (
            [(r["SM"], slice(0, width))]
            + [(wqkv, span[p]) for p in range(pairs)]
            + [(wo, span[0])]
            + [(wup, span[k]) for k in range(2 * halves)]
            + [(wdn, span[k]) for k in range(2 * halves)]
        )
        gather = Gather(sources, where, r["ags"], r["agr"], sends)
        await_greetings(len(friends) + lax.rem((z + 1) // 2, 2))
        gather.turn()
        turn_in, need = gather.turn, gather.need
    else:
        greet([partner])
        await_greetings(1)
        turn_in, need = lambda: None, lambda *pieces: None
    to_partner(xs.at[0], X.at[pl.ds(mine, local)], 0)
    SG[...] = jnp.zeros_like(SG)
    r["SI"][...] = jnp.zeros_like(r["SI"])
    here.wait()
    from_partner(X.at[pl.ds(other, local)], 0)
    turn_in()

    lane = lax.broadcasted_iota(jnp.int32, (TILE, 128), 1)
    low = lane < 64

    def swap(v):
        return pltpu.roll(v, 64, 1)

    need(0)
    if fused:
        total = jnp.zeros((SMALL_ROWS, width), F32)
        for a in range(4):
            for b in range(2):
                for c in range(2):
                    total = total + r["SM"][a, b, c].astype(F32)
        BV[...] = total
    else:
        BV[...] = r["small"][...]

    def small_row(row):
        return BV[row : row + 1, :]

    def own_half(row):
        return jnp.where(t == 0, BV[row : row + 1, :cols], BV[row : row + 1, cols:])

    out_bias, out2_bias = small_row(OUT_BIAS), small_row(OUT2_BIAS)
    gain0, gain1 = small_row(GAINS), small_row(GAINS + 1)
    shift0, shift1 = small_row(SHIFTS), small_row(SHIFTS + 1)
    in_bias = [
        jnp.where(t == 0, small_row(IN_BIAS + j), small_row(IN_BIAS + halves + j)) for j in range(halves)
    ]
    bq, bk, bv = own_half(QK_BIAS), own_half(QK_BIAS + 1), own_half(VALUE_BIAS)
    turn_in()

    ahead = lax.broadcasted_iota(jnp.int32, (TILE, TILE), 0) >= lax.broadcasted_iota(
        jnp.int32, (TILE, TILE), 1
    )
    for p in range(pairs):
        need(1 + p)
        at = p * 128
        states = [None, None]
        for i in range(chunks):
            rows = slice(i * TILE, (i + 1) * TILE)
            pre = nn(X[rows, :], flat(wqkv, p * 384, 384))
            cs = table[rows, :]
            q = jnp.maximum(pre[:, :128] + bq[:, at : at + 128], 0.0)
            k = jnp.maximum(pre[:, 128:256] + bk[:, at : at + 128], 0.0)
            v = pre[:, 256:] + bv[:, at : at + 128]
            qs, ks, vs = swap(q), swap(k), swap(v)
            feats = (
                ((jnp.where(low, q, qs) * cs).astype(BF16), (jnp.where(low, qs, q) * cs).astype(BF16)),
                ((jnp.where(low, k, ks) * cs).astype(BF16), (jnp.where(low, ks, k) * cs).astype(BF16)),
                (jnp.where(low, v, 1.0).astype(BF16), jnp.where(low, vs, 1.0).astype(BF16)),
            )
            both = []
            for h in range(2):
                fq, fk, va = (feat[h] for feat in feats)
                FQ[2 * p + h, rows, :], FK[2 * p + h, rows, :], VA[2 * p + h, rows, :] = fq, fk, va
                scores = jnp.where(ahead, nt(fq, fk), 0.0).astype(BF16)
                sums = nn(scores, va)
                if i:
                    before = states[h].astype(BF16)
                    SS[2 * p + h, i] = before
                    sums = sums + nn(fq, before)
                both.append(sums)
                if i + 1 < chunks:
                    grown = tn(fk, va)
                    states[h] = states[h] + grown if i else grown
            num = jnp.where(low, both[0], swap(both[1]))
            den = jnp.where(low, swap(both[0]), both[1])
            DEN[rows, at : at + 128] = den
            CTX[rows, at : at + 128] = (num / jnp.maximum(den, 1.0)).astype(BF16)
            turn_in()

    P = r["P"]

    def bands(body, count):
        def step(b, sums):
            rows = pl.ds(pl.multiple_of(b * BAND, BAND), BAND)
            terms = body(rows, b * BAND)
            return tuple(
                total + jnp.sum(term.reshape(BAND // 8, 8, width), 0) for total, term in zip(sums, terms)
            )

        zero = jnp.zeros((8, width), F32)
        return lax.fori_loop(0, TILE // BAND, step, (zero,) * count, unroll=4)

    def mean(v):
        return jnp.mean(v, -1, keepdims=True)

    def normalize(resid):
        center = resid - mean(resid)
        rstd = lax.rsqrt(mean(center * center) + EPS)
        return center * rstd, rstd

    need(1 + pairs)
    for tile in range(tiles):
        rows = rows_at(other, tile)
        SB[0, tile] = nt(CTX[rows, :], flat(wo)).astype(BF16)
        to_partner(SB.at[0, tile], RB.at[0, tile], 1 + tile)
        turn_in()
    for tile in range(tiles):
        rows = rows_at(mine, tile)
        P[...] = nt(CTX[rows, :], flat(wo))
        from_partner(RB.at[0, tile], 1 + tile)

        def first_norm(band, begin):
            whole = pl.ds(pl.multiple_of(mine + tile * TILE + begin, BAND), BAND)
            local_rows = pl.ds(pl.multiple_of(tile * TILE + begin, BAND), BAND)
            resid = X[whole, :].astype(F32) + (P[band, :] + RB[0, tile, band, :].astype(F32) + out_bias)
            normed, rstd = normalize(resid)
            N1[local_rows, :] = normed
            RS1[local_rows, :] = jnp.broadcast_to(rstd, (BAND, 128))
            HB[whole, :] = (normed * gain0 + shift0).astype(BF16)
            return ()

        bands(first_norm, 0)
        to_partner(HB.at[rows], HB.at[rows], 3 + tile)
        turn_in()

    for j in range(halves):
        need(first_up + 2 * j, first_up + 2 * j + 1)
        for half in range(2):
            if j == 0 and half == 1:
                for tile in range(tiles):
                    from_partner(HB.at[rows_at(other, tile)], 3 + tile)
            begin = j * 2 * PIECE
            for tile in range(tiles):
                rows = rows_at(other if half else mine, tile)
                u = nn(HB[rows, :], flat(wup, begin, 2 * PIECE)) + in_bias[j]
                cdf = 0.5 * (1.0 + lax.erf(u * np.float32(0.5**0.5)))
                pdf = jnp.exp(-0.5 * u * u) * np.float32((2.0 * np.pi) ** -0.5)
                ACT[rows, begin : begin + 2 * PIECE] = (u * cdf).astype(BF16)
                GP[rows, begin : begin + 2 * PIECE] = (cdf + u * pdf).astype(BF16)
                turn_in()

    ACC = r["ACC"]
    early = hidden - PIECE
    need(*range(first_dn, first_dn + 2 * halves - 1))
    for base, partial_sums in ((other, ACC), (mine, DR)):
        for tile in range(tiles):
            partial_sums[rows_at(0, tile), :] = nt(ACT[rows_at(base, tile), :early], flat(wdn, 0, early))
            turn_in()
    need(first_dn + 2 * halves - 1)

    def whole_sum(base, tile, partial_sums):
        late = nt(ACT[rows_at(base, tile), early:], flat(wdn, early, PIECE))
        return partial_sums[rows_at(0, tile), :] + late

    for tile in range(tiles):
        SB[1, tile] = whole_sum(other, tile, ACC).astype(BF16)
        to_partner(SB.at[1, tile], RB.at[1, tile], 5 + tile)
        turn_in()
    N2 = ACC
    for tile in range(tiles):
        rows = rows_at(mine, tile)
        P[...] = whole_sum(mine, tile, DR)
        from_partner(RB.at[1, tile], 5 + tile)

        def second_norm(band, begin):
            whole = pl.ds(pl.multiple_of(mine + tile * TILE + begin, BAND), BAND)
            local_rows = pl.ds(pl.multiple_of(tile * TILE + begin, BAND), BAND)
            h1 = N1[local_rows, :] * gain0 + shift0
            resid = h1 + (P[band, :] + RB[1, tile, band, :].astype(F32)) + out2_bias
            normed, rstd = normalize(resid)
            N2[local_rows, :] = normed
            e = gy[0, local_rows, :].astype(F32) * gain1
            back = rstd * (e - mean(e) - normed * mean(e * normed))
            DR[local_rows, :] = back
            DF[whole, :] = back.astype(BF16)
            return ()

        bands(second_norm, 0)
        to_partner(DF.at[rows], DF.at[rows], 7 + tile)
        turn_in()

    def keep(row, vector):
        SG[row : row + 1, :] = vector


    if fused:

        def write(name, begin):
            def put(total):
                r[name][:, begin : begin + PIECE] = total

            return put

        def write_qkv(p):
            def put(total):
                for m in range(3):
                    r["oqkv"][m, :, p * 128 : (p + 1) * 128] = total[:, m * 128 : (m + 1) * 128]

            return put

        targets = (
            [(gdn, span[k], write("odn", k * PIECE)) for k in range(2 * halves)]
            + [(gup, span[k], write("oup", k * PIECE)) for k in range(2 * halves)]
            + [(go, span[0], write("oo", 0))]
            + [(gqkv, span[p], write_qkv(p)) for p in range(pairs)]
        )
        scatter = Scatter(targets, where, r["held"], r["pool"], r["rss"], r["rsr"], sends)
        first_out, turn_out = scatter.first, scatter.turn
    else:
        first_out, turn_out = lambda piece: None, lambda: None

    def store(ref, begin, value):
        ref[:, :, :, :, begin : begin + value.shape[1]] = value.astype(BF16).reshape(
            ref.shape[:4] + (value.shape[1],)
        )

    for tile in range(tiles):
        from_partner(DF.at[rows_at(other, tile)], 7 + tile)
    for j in range(halves):
        store(gdn, j * 2 * PIECE, tn(DF[...], ACT[:, j * 2 * PIECE : (j + 1) * 2 * PIECE]))
        turn_out()
        first_out(2 * j)
        first_out(2 * j + 1)
    for base in (mine, other):
        for tile in range(tiles):
            rows = rows_at(base, tile)
            for j in range(halves):
                at = slice(j * 2 * PIECE, (j + 1) * 2 * PIECE)
                dact = nn(DF[rows, :], flat(wdn, j * 2 * PIECE, 2 * PIECE))
                du = (dact * GP[rows, at].astype(F32)).astype(BF16)
                GP[rows, at] = du
                sums = jnp.sum(du.astype(F32), 0, keepdims=True)
                r["SI"][j : j + 1, :] = r["SI"][j : j + 1, :] + sums
            turn_out()

    for j in range(halves):
        sums = r["SI"][j : j + 1, :]
        keep(IN_BIAS + j, jnp.where(t == 0, sums, 0.0))
        keep(IN_BIAS + halves + j, jnp.where(t == 0, 0.0, sums))
    leave(1)
    for tile in range(tiles):
        rows = rows_at(other, tile)
        SB[0, tile] = nt(GP[rows, :], flat(wup)).astype(BF16)
        to_partner(SB.at[0, tile], RB.at[0, tile], 9 + tile)
        turn_out()
    for j in range(halves):
        store(gup, j * 2 * PIECE, tn(HB[...], GP[:, j * 2 * PIECE : (j + 1) * 2 * PIECE]))
        turn_out()
        first_out(2 * halves + 2 * j)
        first_out(2 * halves + 2 * j + 1)

    totals = []
    for tile in range(tiles):

        def second_norm_rest(band, begin):
            whole = pl.ds(pl.multiple_of(mine + tile * TILE + begin, BAND), BAND)
            local_rows = pl.ds(pl.multiple_of(tile * TILE + begin, BAND), BAND)
            normed, g = N2[local_rows, :], gy[0, local_rows, :].astype(F32)
            r["output"][0, local_rows, :] = (normed * gain1 + shift1).astype(BF16)
            return DF[whole, :].astype(F32), g * normed, g

        totals.append(bands(second_norm_rest, 3))
        turn_out()
    for row, parts in zip((OUT2_BIAS, GAINS + 1, SHIFTS + 1), zip(*totals)):
        keep(row, jnp.sum(sum(parts[1:], parts[0]), 0, keepdims=True))

    leave(7)
    totals = []
    for tile in range(tiles):
        rows = rows_at(mine, tile)
        P[...] = nt(GP[rows, :], flat(wup))
        from_partner(RB.at[0, tile], 9 + tile)

        def first_norm_back(band, begin):
            whole = pl.ds(pl.multiple_of(mine + tile * TILE + begin, BAND), BAND)
            local_rows = pl.ds(pl.multiple_of(tile * TILE + begin, BAND), BAND)
            g = DR[local_rows, :] + (P[band, :] + RB[0, tile, band, :].astype(F32))
            normed = N1[local_rows, :]
            e = g * gain0
            rstd = RS1[local_rows, :][:, :1]
            back = rstd * (e - mean(e) - normed * mean(e * normed))
            DR[local_rows, :] = back
            low_back = back.astype(BF16)
            DATT[whole, :] = low_back
            return low_back.astype(F32), g * normed, g

        totals.append(bands(first_norm_back, 3))
        to_partner(DATT.at[rows], DATT.at[rows], 11 + tile)
        turn_out()
    sum_da, sum_dn, sum_dh = [
        jnp.sum(sum(parts[1:], parts[0]), 0, keepdims=True) for parts in zip(*totals)
    ]
    keep(OUT_BIAS, sum_da)
    keep(GAINS, sum_dn)
    keep(SHIFTS, sum_dh)

    def project_back(base):
        for tile in range(tiles):
            rows = rows_at(base, tile)
            dctx = nn(DATT[rows, :], flat(wo))
            for p in range(pairs):
                at = slice(p * 128, (p + 1) * 128)
                d, den, ctx = dctx[:, at], DEN[rows, at], CTX[rows, at].astype(F32)
                dnum = d / jnp.maximum(den, 1.0)
                product = d * ctx
                shifted = swap(dnum)
                for h in range(2):
                    inside = low if h == 0 else jnp.logical_not(low)
                    total = den[:, h * 64 : h * 64 + 1]
                    dden = -jnp.sum(jnp.where(inside, product, 0.0), -1, keepdims=True) / total
                    dden = jnp.where(total > 1.0, dden, 0.0)
                    high = dden.astype(BF16).astype(F32)
                    rest = jnp.where(lane == 64, high, jnp.where(lane == 65, dden - high, 0.0))
                    DN[2 * p + h, rows, :] = jnp.where(low, shifted if h else dnum, rest).astype(BF16)
            turn_out()

    project_back(mine)
    for tile in range(tiles):
        from_partner(DATT.at[rows_at(other, tile)], 11 + tile)
    project_back(other)
    store(go, 0, tn(DATT[...], CTX[...]))
    turn_out()
    first_out(4 * halves)

    for p in range(pairs):
        at = p * 384

        states = [None, None]
        for i in reversed(range(chunks)):
            rows = slice(i * TILE, (i + 1) * TILE)
            cs = table[rows, :]
            dqs, dks, dvs = [], [], []
            for h in range(2):
                q, k, va = FQ[2 * p + h, rows, :], FK[2 * p + h, rows, :], VA[2 * p + h, rows, :]
                dn = DN[2 * p + h, rows, :]
                scores = jnp.where(ahead, nt(q, k), 0.0).astype(BF16)
                dscores = jnp.where(ahead, nt(dn, va), 0.0).astype(BF16)
                dq, dk, dv = nn(dscores, k), tn(dscores, q), tn(scores, dn)
                if i:
                    dq = dq + nt(dn, SS[2 * p + h, i])
                if i + 1 < chunks:
                    later = states[h].astype(BF16)
                    dk = dk + nt(va, later)
                    dv = dv + nn(k, later)
                if i:
                    grown = tn(q, dn)
                    states[h] = states[h] + grown if i + 1 < chunks else grown
                dq, dk = dq * cs, dk * cs
                dqs.append(dq + swap(dq))
                dks.append(dk + swap(dk))
                dvs.append(dv)

            def live(feat):
                a, b = feat[2 * p, rows, :].astype(F32), feat[2 * p + 1, rows, :].astype(F32)
                return jnp.where(low, a, swap(b)) > 0.0

            dq = jnp.where(live(FQ), jnp.where(low, dqs[0], dqs[1]), 0.0)
            dk = jnp.where(live(FK), jnp.where(low, dks[0], dks[1]), 0.0)
            dv = jnp.where(low, dvs[0], swap(dvs[1]))
            DPRE[rows, at : at + 384] = jnp.concatenate([dq, dk, dv], 1).astype(BF16)
            turn_out()
        piece = DPRE[:, at : at + 384]
        store(gqkv, at, tn(X[...], piece))
        sums = jnp.sum(piece.astype(F32), 0, keepdims=True)
        for m, row in enumerate((QK_BIAS, QK_BIAS + 1, VALUE_BIAS)):
            here_sums = sums[:, m * 128 : (m + 1) * 128]
            SG[row : row + 1, p * 128 : (p + 1) * 128] = jnp.where(t == 0, here_sums, 0.0)
            begin = cols + p * 128
            SG[row : row + 1, begin : begin + 128] = jnp.where(t == 0, 0.0, here_sums)
        turn_out()
        first_out(4 * halves + 1 + p)

    leave(5)
    if fused:
        Q, ss, sr = r["Q"], r["sms"], r["smr"]

        def arrive(slot, index):
            remote(Q.at[slot], Q.at[slot], ss.at[index], sr.at[index], partner).wait_recv()

        def hop(slot, index, before, device):
            arrive(slot, index)
            Q[slot + 1] = before[...] + Q[slot]
            sends.start(Q.at[slot + 1], Q.at[slot + 2], ss.at[index + 1], sr.at[index + 1], device)

        def across():
            arrive(6, 3)
            Q[7] = Q[5] + Q[6]
            sends.start_where(central, Q.at[7], Q.at[8], ss.at[4], sr.at[4], across_peer)

        def outward():
            pl.when(central)(lambda: arrive(8, 4))
            sends.start_where(central, Q.at[8], Q.at[8], ss.at[5], sr.at[5], pair_peer)

        scatter.hops = (
            lambda: hop(0, 0, SG, x_peer),
            lambda: hop(2, 1, Q.at[1], y_peer),
            lambda: hop(4, 2, Q.at[3], pair_peer),
            across,
            outward,
            lambda: pl.when(jnp.logical_not(central))(lambda: arrive(8, 5)),
        )
        sends.start(SG, Q.at[0], ss.at[0], sr.at[0], partner)
    for tile in range(tiles):
        rows = rows_at(other, tile)
        SB[1, tile] = nt(DPRE[rows, :], flat(wqkv)).astype(BF16)
        to_partner(SB.at[1, tile], RB.at[1, tile], 13 + tile)
        turn_out()
    for tile in range(tiles):
        rows, here_rows = rows_at(mine, tile), rows_at(0, tile)
        part = nt(DPRE[rows, :], flat(wqkv))
        from_partner(RB.at[1, tile], 13 + tile)
        r["grad_input"][0, here_rows, :] = DR[here_rows, :] + (part + RB[1, tile].astype(F32))
        turn_out()
    if fused:
        turn_out()
        total = Q[7] + Q[8]
        owned = pltpu.roll(total, lax.rem(width - f * owns, width), 1)
        line = jnp.sum(jnp.where(own_row, total, 0.0), 0, keepdims=True)
        line = jnp.broadcast_to(line, (8, width))
        line = pltpu.roll(line, lax.rem(width - lax.rem(f, per_row) * inner, width), 1)[:1]
        r["smalls"][...] = jnp.where(table_row < IN_BIAS, owned, line)
    else:
        r["smalls"][...] = SG[...]
    sends.finish()


def layer(fused, inputs, grad_out, slabs, small):
    sqkv, so, sup, sdn = slabs
    _, local, width = inputs.shape
    length, cols, hidden = 2 * local, sqkv.shape[-1] if fused else so.shape[-1], sup.shape[-1]
    heads, chunks, tiles = cols // HEAD_DIM, length // TILE, local // TILE
    part = width // 16
    lead = (4, 2, 2, part)
    angles = np.pi / 2.0 * np.arange(length, dtype=np.float64) / length
    table = np.concatenate(
        [np.repeat(np.cos(angles)[:, None], 64, 1), np.repeat(np.sin(angles)[:, None], 64, 1)], 1
    ).astype(np.float32)
    vmem = pl.BlockSpec(memory_space=pltpu.VMEM)
    hbm = pl.BlockSpec(memory_space=pl.ANY)
    dma = pltpu.SemaphoreType.DMA
    sizes = dict(qkv=3 * cols, o=cols, up=hidden, dn=hidden)
    pieces = (4 * cols + 2 * hidden) // PIECE

    ins = [("inputs", inputs, hbm), ("grad_out", grad_out, vmem), ("table", jnp.asarray(table), vmem)]
    if fused:
        ins += [("sqkv", sqkv, vmem), ("so", so, vmem), ("sup", sup, vmem), ("sdn", sdn, vmem)]
        ins += [(name, piece, vmem) for (name, _), piece in zip(SMALLS, small)]
    else:
        wholes = [slab.reshape(lead + slab.shape[-1:]) for slab in slabs]
        ins += [(name, value, vmem) for name, value in zip(("wqkv", "wo", "wup", "wdn"), wholes)]
        ins += [("small", small, vmem)]

    outs = [
        ("output", (1, local, width), BF16),
        ("grad_input", (1, local, width), F32),
        ("smalls", (SMALL_ROWS, width), F32),
    ]
    if fused:
        outs += [
            ("oqkv", (3, part, cols), F32),
            ("oo", (part, cols), F32),
            ("oup", (part, hidden), F32),
            ("odn", (part, hidden), F32),
        ]
    else:
        outs += [("g" + name, lead + (size,), BF16) for name, size in sizes.items()]

    def v(*shape, dtype=BF16):
        return pltpu.VMEM(shape, dtype)

    scratch = dict(
        X=v(length, width),
        HB=v(length, width),
        DF=v(length, width),
        FQ=v(heads, length, 128),
        FK=v(heads, length, 128),
        VA=v(heads, length, 128),
        DN=v(heads, length, 128),
        SS=v(heads, chunks, 128, 128),
        DEN=v(length, cols, dtype=F32),
        CTX=v(length, cols),
        N1=v(local, width, dtype=F32),
        RS1=v(local, 128, dtype=F32),
        DR=v(local, width, dtype=F32),
        ACT=v(length, hidden),
        GP=v(length, hidden),
        DPRE=v(length, 3 * cols),
        SB=v(2, tiles, TILE, width),
        RB=v(2, tiles, TILE, width),
        P=v(TILE, width, dtype=F32),
        ACC=v(local, width, dtype=F32),
        BV=v(SMALL_ROWS, width, dtype=F32),
        SG=v(SMALL_ROWS, width, dtype=F32),
        SI=v(8, 2 * PIECE, dtype=F32),
        tps=dma((16,)),
        tpr=dma((16,)),
        own=dma((1,)),
    )
    if fused:
        scratch.update({"w" + name: v(*lead, size) for name, size in sizes.items()})
        scratch.update({"g" + name: v(*lead, size) for name, size in sizes.items()})
        scratch.update(
            SM=v(4, 2, 2, SMALL_ROWS, width),
            Z=v(SMALL_ROWS, width, dtype=F32),
            Q=v(9, SMALL_ROWS, width, dtype=F32),
            held=v(pieces, 4, 2, part, PIECE),
            pool=v(sum(sum(slabs_of(order)[0]) for order in SCATTER_ORDERS), part, PIECE),
            ags=dma((pieces + 1, 5)),
            agr=dma((pieces + 1, 5)),
            rss=dma((pieces, 7)),
            rsr=dma((pieces, 7)),
            sms=dma((6,)),
            smr=dma((6,)),
        )
    names = [name for name, _, _ in ins] + [name for name, _, _ in outs] + list(scratch)
    results = pl.pallas_call(
        partial(layer_kernel, fused, names),
        name="layer",
        out_shape=tuple(jax.ShapeDtypeStruct(shape, dtype) for _, shape, dtype in outs),
        in_specs=[spec for _, _, spec in ins],
        out_specs=tuple(vmem for _ in outs),
        scratch_shapes=list(scratch.values()),
        compiler_params=pltpu.CompilerParams(
            collective_id=0, has_side_effects=True, vmem_limit_bytes=64 << 20
        ),
    )(*[value for _, value, _ in ins])
    output, grad_input, smalls, *grads = results
    return output, grad_input, smalls, grads


def hand_over_kernel(count, *refs):
    large, smalls, targets, pieces = refs[:count], refs[count], refs[count + 1 : 2 * count + 1], refs[2 * count + 1 :]
    for source, target in zip(large, targets):
        target[...] = source[...]
    for (_, row), piece in zip(SMALLS, pieces):
        piece[...] = smalls[row : row + piece.shape[0], 0 : piece.shape[1]]


def hand_over(large, smalls, shapes):
    steps = 4
    specs = []
    for v in large:
        axis = 1 if v.shape[0] == 1 else v.ndim - 1
        if v.shape[axis] % (steps * 128) == 0:
            block = v.shape[:axis] + (v.shape[axis] // steps,) + v.shape[axis + 1 :]
            specs.append(pl.BlockSpec(block, partial(lambda at, n, i: tuple(i * (k == at) for k in range(n)), axis, v.ndim)))
        else:
            specs.append(pl.BlockSpec(v.shape, partial(lambda n, i: (0,) * n, v.ndim)))
    whole = [pl.BlockSpec(shape, lambda i: (0, 0)) for shape in shapes]
    count = len(large)
    results = pl.pallas_call(
        partial(hand_over_kernel, count),
        name="hand_over",
        grid=(steps,),
        out_shape=tuple(jax.ShapeDtypeStruct(v.shape, v.dtype) for v in large)
        + tuple(jax.ShapeDtypeStruct(shape, F32) for shape in shapes),
        in_specs=specs + [pl.BlockSpec(smalls.shape, lambda i: (0, 0))],
        out_specs=tuple(specs + whole),
        compiler_params=pltpu.CompilerParams(vmem_limit_bytes=60 << 20),
    )(*large, smalls)
    return results[:count], results[count:]


def shards(
    inputs,
    query_key_value_weight,
    attention_out_weight,
    up_weight,
    down_weight,
    qk_bias,
    value_bias,
    out_bias,
    ffn_in_bias,
    ffn_out_bias,
    norm_gains,
    norm_biases,
    grad_out,
):
    rank_here, ranks = lax.axis_index("fsdp"), lax.axis_size("fsdp")
    _, rows, cols = query_key_value_weight.shape
    pairs = cols // 128
    width = inputs.shape[2]
    fused = ranks == 16 and rows % 16 == 0 and 4 * cols + 2 * up_weight.shape[1] == 12 * PIECE
    small = (
        qk_bias,
        value_bias[None],
        out_bias[None],
        ffn_out_bias[None],
        norm_gains,
        norm_biases,
        ffn_in_bias[None],
    )
    if fused:
        slabs = (query_key_value_weight, attention_out_weight.T, up_weight, down_weight.T)
    else:
        sqkv = query_key_value_weight.reshape(3, rows, pairs, 128)
        sqkv = jnp.transpose(sqkv, (1, 2, 0, 3)).reshape(rows, 3 * cols)
        slabs = (sqkv, attention_out_weight.T, up_weight, down_weight.T)
        small_shapes = small[:6]
        slabs = tuple(lax.all_gather(slab, "fsdp", axis=0, tiled=True) for slab in slabs)
        at_home = (jnp.arange(ranks) == rank_here).astype(F32)[None, :, None]
        vectors = (jnp.concatenate(small[:6], 0)[:, None, :].astype(F32) * at_home).reshape(-1, width)
        inner = (ffn_in_bias[None, None, :].astype(F32) * at_home).reshape(-1, width)
        small = jnp.concatenate([vectors, inner], 0)
        small = lax.psum(jnp.pad(small, ((0, SMALL_ROWS - small.shape[0]), (0, 0))), "fsdp")
    output, grad_input, smalls, grads = layer(fused, inputs, grad_out, slabs, small)
    if fused:
        large, small = hand_over((output, grad_input, *grads), smalls, [piece.shape for piece in small])
        output, grad_input, dqkv, do, dup, ddn = large
        dqk, dvalue, dout, dout2, dgains, dshifts, dinner = small
    else:
        dqkv, do, dup, ddn = [
            lax.psum_scatter(g.reshape(width, -1).astype(F32), "fsdp", scatter_dimension=0, tiled=True)
            for g in grads
        ]
        dqkv = jnp.transpose(dqkv.reshape(rows, pairs, 3, 128), (2, 0, 1, 3)).reshape(3, rows, cols)
        smalls = lax.psum(smalls, ("fsdp", "tp"))
        mine = lax.dynamic_slice_in_dim(smalls[:IN_BIAS], rank_here * rows, rows, 1)
        dqk, dvalue, dout, dout2, dgains, dshifts = [
            mine[row : row + piece.shape[0]] for (_, row), piece in zip(SMALLS, small_shapes)
        ]
        inner_rows = ffn_in_bias.shape[0]
        inner = smalls[IN_BIAS : IN_BIAS + inner_rows * ranks // width].reshape(-1)
        dinner = lax.dynamic_slice_in_dim(inner, rank_here * inner_rows, inner_rows, 0)
    return (
        output,
        grad_input,
        dqkv,
        do.T,
        dup,
        ddn.T,
        dqk,
        dvalue.reshape(-1),
        dout.reshape(-1),
        dinner.reshape(-1),
        dout2.reshape(-1),
        dgains,
        dshifts,
    )


def solution(mesh):
    return jax.shard_map(
        shards,
        mesh=mesh,
        in_specs=(
            P("fsdp", "tp", None),
            P(None, "fsdp", "tp"),
            P("tp", "fsdp"),
            P("fsdp", "tp"),
            P("tp", "fsdp"),
            P(None, "fsdp"),
            P("fsdp"),
            P("fsdp"),
            P("fsdp"),
            P("fsdp"),
            P(None, "fsdp"),
            P(None, "fsdp"),
            P("fsdp", "tp", None),
        ),
        out_specs=(
            P("fsdp", "tp", None),
            P("fsdp", "tp", None),
            P(None, "fsdp", "tp"),
            P("tp", "fsdp"),
            P("fsdp", "tp"),
            P("tp", "fsdp"),
            P(None, "fsdp"),
            P("fsdp"),
            P("fsdp"),
            P("fsdp"),
            P("fsdp"),
            P(None, "fsdp"),
            P(None, "fsdp"),
        ),
        check_vma=False,
    )
```

```python
from functools import partial

import jax
import jax.numpy as jnp
import numpy as np
from jax import lax
from jax.experimental import pallas as pl
from jax.experimental.pallas import tpu as pltpu
from jax.sharding import PartitionSpec as P

HEAD_DIM = 64
EPS = 1e-05
MESH = pl.DeviceIdType.MESH
BF16 = jnp.bfloat16
F32 = jnp.float32
TILE = 256
PIECE = 384
QK_BIAS, VALUE_BIAS, OUT_BIAS, OUT2_BIAS, GAINS, SHIFTS, IN_BIAS, SMALL_ROWS = 0, 2, 3, 4, 5, 7, 9, 16
HOP = -1
SMALLS = (
    ("qk_bias", QK_BIAS),
    ("value_bias", VALUE_BIAS),
    ("out_bias", OUT_BIAS),
    ("ffn_out_bias", OUT2_BIAS),
    ("norm_gains", GAINS),
    ("norm_biases", SHIFTS),
    ("ffn_in_bias", IN_BIAS),
)
GATHER_ORDERS = (
    "abcxy", "abcxy", "aybcx", "aybcx", "axbcy", "xabcy", "aybcx", "aybcx", "axbcy", "aybcx", "yabcx", "axbcy", "xabcy",
)
GATHER_PLAN = (
    ((1, 0), (2, 0), (0, 0), (3, 0)),
    ((2, 1), (8, 0), (0, 1), (6, 0), (3, 1), (5, 0), (1, 1), (7, 0), (4, 0), (8, 1), (9, 0), (12, 0), (2, 2), (10, 0), (0, 2), (1, 2), (4, 1), (11, 0), (0, 3), (7, 1), (1, 3), (3, 2), (6, 1), (5, 1), (2, 3), (9, 1), (11, 1), (4, 2), (6, 2), (0, 4), (2, 4), (3, 3), (4, 3), (5, 2), (1, 4)),
    ((3, 4), (10, 1)),
    ((6, 3), (7, 2), (5, 3), (8, 2), (9, 2), (4, 4), (6, 4)),
    (),
    (),
    ((7, 3),),
    (),
    ((11, 2), (8, 3)),
    ((5, 4), (12, 1)),
    (),
    ((10, 2), (7, 4)),
    (),
    (),
    ((9, 3), (11, 3), (8, 4)),
    (),
    (),
    (),
    (),
    (),
    (),
    ((10, 3), (12, 2), (9, 4)),
    ((11, 4),),
    (),
    (),
    (),
    ((12, 3),),
    ((10, 4),),
    (),
    ((12, 4),),
    (),
    (),
    (),
    (),
    (),
    (),
    (),
    (),
    (),
    (),
    (),
    (),
    (),
    (),
    (),
    (),
    (),
    (),
)
SCATTER_ORDERS = (
    "xcbay", "ycbax", "ycbax", "xcbay", "xcbay", "ycbxa", "xycba", "ycbxa", "yxcba", "xcbya", "xycba", "yxcba",
)
SCATTER_PLAN = (
    (),
    (),
    (),
    (),
    (),
    (),
    (),
    (),
    (),
    (),
    (),
    (),
    (),
    (),
    (),
    (),
    ((1, 1),),
    (),
    ((0, 1),),
    (),
    (),
    ((2, 1),),
    (),
    ((3, 1),),
    (),
    (),
    (),
    (),
    ((1, 2),),
    ((4, 1),),
    ((0, 2),),
    (),
    ((5, 1),),
    (),
    ((3, 2), (2, 2)),
    (),
    ((4, 2), (7, 1)),
    ((6, 1),),
    (),
    (),
    ((1, 3), (0, 3)),
    (),
    (),
    (),
    ((5, 2),),
    ((9, 1),),
    ((HOP, 1),),
    ((6, 2), (8, 1), (7, 2), (3, 3), (2, 3)),
    ((9, 2), (4, 3), (HOP, 2), (5, 3), (10, 1)),
    ((11, 1), (8, 2), (7, 3), (6, 3)),
    ((HOP, 3), (4, 4), (9, 3), (10, 2), (8, 3), (3, 4), (2, 4), (1, 4), (11, 2), (HOP, 4), (6, 4), (10, 3), (9, 4), (5, 4), (0, 4), (11, 3), (8, 4), (4, 5), (7, 4), (HOP, 5), (10, 4), (8, 5), (9, 5), (11, 4), (7, 5), (0, 5), (10, 5), (1, 5), (5, 5), (2, 5), (6, 5), (3, 5), (HOP, 6), (11, 5)),
)
BAND = 32


def nn(a, b):
    return jnp.dot(a, b, preferred_element_type=F32)


def nt(a, b):
    return lax.dot_general(a, b, (((1,), (1,)), ((), ())), preferred_element_type=F32)


def tn(a, b):
    return lax.dot_general(a, b, (((0,), (0,)), ((), ())), preferred_element_type=F32)


def place():
    f = lax.axis_index("fsdp")
    return lax.rem(f, 2), lax.rem(f // 2, 2), f // 4, lax.axis_index("tp")


def rank(x, y, z):
    return (z * 2 + y) * 2 + x


def greet(devices):
    barrier = pltpu.get_barrier_semaphore()
    for device in devices:
        pl.semaphore_signal(barrier, inc=1, device_id=device, device_id_type=MESH)


def await_greetings(count):
    pl.semaphore_wait(pltpu.get_barrier_semaphore(), count)


def remote(source, target, send_sem, recv_sem, device):
    return pltpu.make_async_remote_copy(
        src_ref=source,
        dst_ref=target,
        send_sem=send_sem,
        recv_sem=recv_sem,
        device_id=device,
        device_id_type=MESH,
    )


class Where:
    def __init__(self, condition, copy):
        self.condition, self.copy = condition, copy

    def wait_send(self):
        pl.when(self.condition)(self.copy.wait_send)


class Sends:
    def __init__(self):
        self.copies = []

    def start(self, *args):
        copy = remote(*args)
        copy.start()
        self.copies.append(copy)
        return copy

    def start_where(self, condition, *args):
        copy = remote(*args)
        pl.when(condition)(copy.start)
        self.copies.append(Where(condition, copy))

    def settle(self, copies):
        for copy in copies:
            copy.wait_send()
        self.copies = [c for c in self.copies if not any(c is copy for copy in copies)]

    def finish(self):
        self.settle(list(self.copies))


class Gather:
    SLOT = {"x": 0, "y": 1, "a": 2, "b": 3, "c": 4}

    def __init__(self, pieces, where, send, recv, sends):
        self.pieces, self.send, self.recv, self.sends = pieces, send, recv, sends
        self.x, self.y, self.z, t = where
        x, y, z = self.x, self.y, self.z
        self.half = z // 2
        self.inner = jnp.logical_or(z == 1, z == 2)
        self.outer = jnp.logical_not(self.inner)
        self.pair = z + 1 - 2 * lax.rem(z, 2)
        self.peer = {
            "x": (rank(1 - x, y, z), t),
            "y": (rank(x, 1 - y, z), t),
            "a": (rank(x, y, self.pair), t),
            "b": (rank(x, y, 3 - z), t),
            "c": (rank(x, y, self.pair), t),
        }
        self.orders = GATHER_ORDERS
        self.plan = iter(GATHER_PLAN)

    def view(self, piece, have, **at):
        whole, cols = self.pieces[piece]
        if "c" in have:
            along_z = slice(None)
        elif "a" in have:
            along_z = pl.ds(2 * self.half, 2)
        else:
            along_z = self.z
        index = [at.get("z", along_z)]
        for axis, own in (("y", self.y), ("x", self.x)):
            index.append(at.get(axis, slice(None) if axis in have else own))
        return whole.at[(*index, slice(None), cols)]

    def sems(self, piece, axis):
        slot = self.SLOT[axis]
        return self.send.at[piece, slot], self.recv.at[piece, slot]

    def arrive(self, piece, stage):
        order = self.orders[piece]
        axis, have = order[stage], order[:stage]
        if axis == "a":
            target = self.view(piece, have, z=self.pair)
        elif axis in "bc":
            target = self.view(piece, have, z=pl.ds(2 * (1 - self.half), 2))
        else:
            target = self.view(piece, have, **{axis: 1 - getattr(self, axis)})
        wait = remote(target, target, *self.sems(piece, axis), self.peer["x"]).wait_recv
        if axis in "bc":
            pl.when(self.inner if axis == "b" else self.outer)(wait)
        else:
            wait()

    def step(self, piece, stage):
        order = self.orders[piece]
        axis, have = order[stage], order[:stage]
        if stage:
            self.arrive(piece, stage - 1)
        if axis == "c":
            source = self.view(piece, have, z=pl.ds(2 * (1 - self.half), 2))
        else:
            source = self.view(piece, have)
        args = (source, source, *self.sems(piece, axis), self.peer[axis])
        if axis in "bc":
            self.sends.start_where(self.inner, *args)
        else:
            self.sends.start(*args)

    def turn(self):
        for piece, stage in next(self.plan):
            self.step(piece, stage)

    def need(self, *pieces):
        for piece in pieces:
            self.arrive(piece, len(self.orders[piece]) - 1)
            self.turn()


def slabs_of(order):
    counts, chips, lanes = [], 4, 2
    for axis in order[1:]:
        if axis in "xy":
            counts.append(chips)
            lanes = 1
        elif axis == "a":
            counts.append(lanes)
            chips = 1
        else:
            counts.append(2 * lanes)
            chips = 2
    return counts, [sum(counts[:k]) for k in range(len(counts))]


class Scatter:
    def __init__(self, pieces, where, held, pool, send, recv, sends):
        self.pieces, self.held, self.pool = pieces, held, pool
        self.send, self.recv, self.sends = send, recv, sends
        self.x, self.y, self.z, t = where
        x, y, z = self.x, self.y, self.z
        self.half = z // 2
        self.inner = jnp.logical_or(z == 1, z == 2)
        self.outer = jnp.logical_not(self.inner)
        self.pair = z + 1 - 2 * lax.rem(z, 2)
        self.peer = {
            "x": (rank(1 - x, y, z), t),
            "y": (rank(x, 1 - y, z), t),
            "a": (rank(x, y, self.pair), t),
            "b": (rank(x, y, 3 - z), t),
            "c": (rank(x, y, self.pair), t),
        }
        self.orders = SCATTER_ORDERS
        self.plan = iter(SCATTER_PLAN)
        self.base = [0]
        for order in self.orders:
            self.base.append(self.base[-1] + sum(slabs_of(order)[0]))

    def copies(self, piece, stage):
        order = self.orders[piece]
        axis, done = order[stage], order[:stage]
        if stage == 0:
            grads, cols, _ = self.pieces[piece]
            every, away = slice(None), 1 - getattr(self, axis)
            index = (every, every, away) if axis == "x" else (every, away, every)
            return [(grads.at[(*index, every, cols)], self.held.at[piece], 0)], None, None
        held, pool = self.held, self.pool
        at = self.base[piece] + slabs_of(order)[1][stage - 1]
        lane = "y" if order[0] == "x" else "x"
        own = getattr(self, lane)
        if axis == lane:
            if "a" in done:
                return [(held.at[piece, self.z, 1 - own], pool.at[at], 1)], None, None
            chips, count = (pl.ds(2 * self.half, 2), 2) if "b" in done else (slice(None), 4)
            return [(held.at[piece, chips, 1 - own], pool.at[pl.ds(at, count)], 1)], None, None
        if axis == "a":
            if lane in done:
                return [(held.at[piece, self.pair, own], pool.at[at], 2)], None, None
            return [(held.at[piece, self.pair], pool.at[pl.ds(at, 2)], 2)], None, None
        far = 2 * (1 - self.half)
        slot = 3 if axis == "c" else 5
        senders = self.outer if axis == "c" else self.inner
        if lane in done:
            return [(held.at[piece, pl.ds(far, 2), own], pool.at[pl.ds(at, 2)], slot)], senders, self.inner
        return (
            [(held.at[piece, far + k], pool.at[pl.ds(at + 2 * k, 2)], slot + k) for k in range(2)],
            senders,
            self.inner,
        )

    def emit(self, piece, stage):
        copies, senders, _ = self.copies(piece, stage)
        device = self.peer[self.orders[piece][stage]]
        for source, target, slot in copies:
            args = (source, target, self.send.at[piece, slot], self.recv.at[piece, slot], device)
            if senders is None:
                self.sends.start(*args)
            else:
                self.sends.start_where(senders, *args)

    def first(self, piece):
        self.emit(piece, 0)
        self.turn()

    def absorb(self, piece, stage, final):
        copies, _, receivers = self.copies(piece, stage)
        order = self.orders[piece]
        axis, done = order[stage], order[:stage]
        held, pool = self.held, self.pool

        def wait():
            for _, target, slot in copies:
                sems = self.send.at[piece, slot], self.recv.at[piece, slot]
                remote(target, target, *sems, self.peer["x"]).wait_recv()

        if stage == 0:
            wait()
            grads, cols, _ = self.pieces[piece]
            for q in range(4):
                for o in range(2):
                    mine = grads[q, o, self.x, :, cols] if axis == "x" else grads[q, self.y, o, :, cols]
                    held[piece, q, o] = (mine.astype(F32) + held[piece, q, o].astype(F32)).astype(BF16)
            return
        at = self.base[piece] + slabs_of(order)[1][stage - 1]
        lane = "y" if order[0] == "x" else "x"
        own = getattr(self, lane)
        lanes = [own] if lane in done or axis == lane else [0, 1]
        if axis == lane:
            chips = [self.z] if "a" in done else [2 * self.half, 2 * self.half + 1] if "b" in done else range(4)
        elif axis == "a":
            chips = [self.z]
        else:
            near = 2 * self.half if axis == "b" else 2 * (1 - self.half)
            chips = [near, near + 1]

        def add():
            wait()
            for k, (q, o) in enumerate([(q, o) for q in chips for o in lanes]):
                total = held[piece, q, o].astype(F32) + pool[at + k].astype(F32)
                if final:
                    self.pieces[piece][2](total)
                else:
                    held[piece, q, o] = total.astype(BF16)

        if receivers is None:
            add()
        else:
            pl.when(receivers)(add)

    def turn(self):
        for piece, stage in next(self.plan):
            if piece == HOP:
                self.hops[stage - 1]()
                continue
            self.absorb(piece, stage - 1, stage == len(self.orders[piece]))
            if stage < len(self.orders[piece]):
                self.emit(piece, stage)


def layer_kernel(fused, names, *refs):
    r = dict(zip(names, refs))
    where = x, y, z, t = place()
    partner = (lax.axis_index("fsdp"), 1 - t)
    sends = Sends()
    gy, xs = r["grad_out"], r["inputs"]
    wqkv, wo, wup, wdn = r["wqkv"], r["wo"], r["wup"], r["wdn"]
    gqkv, go, gup, gdn = r["gqkv"], r["go"], r["gup"], r["gdn"]
    X, HB, DF = r["X"], r["HB"], r["DF"]
    DATT = DF
    FQ, FK, VA, SS, DN = r["FQ"], r["FK"], r["VA"], r["SS"], r["DN"]
    DEN, CTX, N1, RS1, DR = r["DEN"], r["CTX"], r["N1"], r["RS1"], r["DR"]
    ACT, GP, DPRE, SB, RB = r["ACT"], r["GP"], r["DPRE"], r["SB"], r["RB"]
    BV, SG, table = r["BV"], r["SG"], r["table"]
    tps, tpr = r["tps"], r["tpr"]
    length, width = X.shape
    local = length // 2
    tiles = local // TILE
    cols = wo.shape[-1]
    hidden = wup.shape[-1]
    pairs = cols // 128
    chunks = length // TILE
    halves = hidden // (2 * PIECE)
    mine, other = t * local, (1 - t) * local

    def rows_at(base, tile):
        return pl.ds(pl.multiple_of(base + tile * TILE, TILE), TILE)

    passed = {}

    def to_partner(source, target, index):
        passed[index] = sends.start(source, target, tps.at[index], tpr.at[index], partner)

    def leave(first):
        sends.settle([passed[first + tile] for tile in range(tiles)])

    def from_partner(target, index):
        remote(target, target, tps.at[index], tpr.at[index], partner).wait_recv()

    def flat(ref, begin=0, size=None):
        size = ref.shape[-1] if size is None else size
        return ref[:, :, :, :, begin : begin + size].reshape(width, size)

    here = pltpu.make_async_copy(xs.at[0], X.at[pl.ds(mine, local)], r["own"].at[0])
    here.start()
    first_up = 2 + pairs
    first_dn = first_up + 2 * halves
    if fused:
        x_peer, y_peer = (rank(1 - x, y, z), t), (rank(x, 1 - y, z), t)
        central = jnp.logical_or(z == 1, z == 2)
        pair_peer = (rank(x, y, z + 1 - 2 * lax.rem(z, 2)), t)
        across_peer = (rank(x, y, 3 - z), t)
        friends = [x_peer, y_peer, pair_peer, partner]
        greet(friends)
        pl.when(central)(lambda: greet([across_peer]))
        f = lax.axis_index("fsdp")
        Z = r["Z"]
        owns = wqkv.shape[3]
        Z[...] = jnp.zeros_like(Z)
        for name, row in SMALLS:
            piece = r[name]
            Z[row : row + piece.shape[0], 0 : piece.shape[1]] = piece[...].astype(F32)
        inner = r["ffn_in_bias"].shape[1]
        per_row = width // inner
        table_row = lax.broadcasted_iota(jnp.int32, (SMALL_ROWS, width), 0)
        line = jnp.broadcast_to(Z[IN_BIAS : IN_BIAS + 1, :], (8, width))
        line = pltpu.roll(line, lax.rem(f, per_row) * inner, 1)[:1]
        placed = pltpu.roll(Z[...], f * owns, 1)
        own_row = table_row == IN_BIAS + f // per_row
        placed = jnp.where(table_row < IN_BIAS, placed, jnp.where(own_row, line, 0.0))
        r["SM"][z, y, x] = placed.astype(BF16)
        for p in range(pairs):
            for m in range(3):
                begin = p * 384 + m * 128
                wqkv[z, y, x, :, begin : begin + 128] = r["sqkv"][m, :, p * 128 : (p + 1) * 128]
        wo[z, y, x] = r["so"][...]
        wup[z, y, x] = r["sup"][...]
        wdn[z, y, x] = r["sdn"][...]
        span = [slice(k * PIECE, (k + 1) * PIECE) for k in range(max(pairs, 2 * halves))]
        sources = (
            [(r["SM"], slice(0, width))]
            + [(wqkv, span[p]) for p in range(pairs)]
            + [(wo, span[0])]
            + [(wup, span[k]) for k in range(2 * halves)]
            + [(wdn, span[k]) for k in range(2 * halves)]
        )
        gather = Gather(sources, where, r["ags"], r["agr"], sends)
        await_greetings(len(friends) + lax.rem((z + 1) // 2, 2))
        gather.turn()
        turn_in, need = gather.turn, gather.need
    else:
        greet([partner])
        await_greetings(1)
        turn_in, need = lambda: None, lambda *pieces: None
    to_partner(xs.at[0], X.at[pl.ds(mine, local)], 0)
    SG[...] = jnp.zeros_like(SG)
    r["SI"][...] = jnp.zeros_like(r["SI"])
    here.wait()
    from_partner(X.at[pl.ds(other, local)], 0)
    turn_in()

    lane = lax.broadcasted_iota(jnp.int32, (TILE, 128), 1)
    low = lane < 64

    def swap(v):
        return pltpu.roll(v, 64, 1)

    need(0)
    if fused:
        total = jnp.zeros((SMALL_ROWS, width), F32)
        for a in range(4):
            for b in range(2):
                for c in range(2):
                    total = total + r["SM"][a, b, c].astype(F32)
        BV[...] = total
    else:
        BV[...] = r["small"][...]

    def small_row(row):
        return BV[row : row + 1, :]

    def own_half(row):
        return jnp.where(t == 0, BV[row : row + 1, :cols], BV[row : row + 1, cols:])

    out_bias, out2_bias = small_row(OUT_BIAS), small_row(OUT2_BIAS)
    gain0, gain1 = small_row(GAINS), small_row(GAINS + 1)
    shift0, shift1 = small_row(SHIFTS), small_row(SHIFTS + 1)
    in_bias = [
        jnp.where(t == 0, small_row(IN_BIAS + j), small_row(IN_BIAS + halves + j)) for j in range(halves)
    ]
    bq, bk, bv = own_half(QK_BIAS), own_half(QK_BIAS + 1), own_half(VALUE_BIAS)
    turn_in()

    ahead = lax.broadcasted_iota(jnp.int32, (TILE, TILE), 0) >= lax.broadcasted_iota(
        jnp.int32, (TILE, TILE), 1
    )
    for p in range(pairs):
        need(1 + p)
        at = p * 128
        states = [None, None]
        for i in range(chunks):
            rows = slice(i * TILE, (i + 1) * TILE)
            pre = nn(X[rows, :], flat(wqkv, p * 384, 384))
            cs = table[rows, :]
            q = jnp.maximum(pre[:, :128] + bq[:, at : at + 128], 0.0)
            k = jnp.maximum(pre[:, 128:256] + bk[:, at : at + 128], 0.0)
            v = pre[:, 256:] + bv[:, at : at + 128]
            qs, ks, vs = swap(q), swap(k), swap(v)
            feats = (
                ((jnp.where(low, q, qs) * cs).astype(BF16), (jnp.where(low, qs, q) * cs).astype(BF16)),
                ((jnp.where(low, k, ks) * cs).astype(BF16), (jnp.where(low, ks, k) * cs).astype(BF16)),
                (jnp.where(low, v, 1.0).astype(BF16), jnp.where(low, vs, 1.0).astype(BF16)),
            )
            both = []
            for h in range(2):
                fq, fk, va = (feat[h] for feat in feats)
                FQ[2 * p + h, rows, :], FK[2 * p + h, rows, :], VA[2 * p + h, rows, :] = fq, fk, va
                scores = jnp.where(ahead, nt(fq, fk), 0.0).astype(BF16)
                sums = nn(scores, va)
                if i:
                    before = states[h].astype(BF16)
                    SS[2 * p + h, i] = before
                    sums = sums + nn(fq, before)
                both.append(sums)
                if i + 1 < chunks:
                    grown = tn(fk, va)
                    states[h] = states[h] + grown if i else grown
            num = jnp.where(low, both[0], swap(both[1]))
            den = jnp.where(low, swap(both[0]), both[1])
            DEN[rows, at : at + 128] = den
            CTX[rows, at : at + 128] = (num / jnp.maximum(den, 1.0)).astype(BF16)
            turn_in()

    P = r["P"]

    def bands(body, count):
        def step(b, sums):
            rows = pl.ds(pl.multiple_of(b * BAND, BAND), BAND)
            terms = body(rows, b * BAND)
            return tuple(
                total + jnp.sum(term.reshape(BAND // 8, 8, width), 0) for total, term in zip(sums, terms)
            )

        zero = jnp.zeros((8, width), F32)
        return lax.fori_loop(0, TILE // BAND, step, (zero,) * count, unroll=4)

    def mean(v):
        return jnp.mean(v, -1, keepdims=True)

    def normalize(resid):
        center = resid - mean(resid)
        rstd = lax.rsqrt(mean(center * center) + EPS)
        return center * rstd, rstd

    need(1 + pairs)
    for tile in range(tiles):
        rows = rows_at(other, tile)
        SB[0, tile] = nt(CTX[rows, :], flat(wo)).astype(BF16)
        to_partner(SB.at[0, tile], RB.at[0, tile], 1 + tile)
        turn_in()
    for tile in range(tiles):
        rows = rows_at(mine, tile)
        P[...] = nt(CTX[rows, :], flat(wo))
        from_partner(RB.at[0, tile], 1 + tile)

        def first_norm(band, begin):
            whole = pl.ds(pl.multiple_of(mine + tile * TILE + begin, BAND), BAND)
            local_rows = pl.ds(pl.multiple_of(tile * TILE + begin, BAND), BAND)
            resid = X[whole, :].astype(F32) + (P[band, :] + RB[0, tile, band, :].astype(F32) + out_bias)
            normed, rstd = normalize(resid)
            N1[local_rows, :] = normed
            RS1[local_rows, :] = jnp.broadcast_to(rstd, (BAND, 128))
            HB[whole, :] = (normed * gain0 + shift0).astype(BF16)
            return ()

        bands(first_norm, 0)
        to_partner(HB.at[rows], HB.at[rows], 3 + tile)
        turn_in()

    for j in range(halves):
        need(first_up + 2 * j, first_up + 2 * j + 1)
        for half in range(2):
            if j == 0 and half == 1:
                for tile in range(tiles):
                    from_partner(HB.at[rows_at(other, tile)], 3 + tile)
            begin = j * 2 * PIECE
            for tile in range(tiles):
                rows = rows_at(other if half else mine, tile)
                u = nn(HB[rows, :], flat(wup, begin, 2 * PIECE)) + in_bias[j]
                cdf = 0.5 * (1.0 + lax.erf(u * np.float32(0.5**0.5)))
                pdf = jnp.exp(-0.5 * u * u) * np.float32((2.0 * np.pi) ** -0.5)
                ACT[rows, begin : begin + 2 * PIECE] = (u * cdf).astype(BF16)
                GP[rows, begin : begin + 2 * PIECE] = (cdf + u * pdf).astype(BF16)
                turn_in()

    ACC = r["ACC"]
    early = hidden - PIECE
    need(*range(first_dn, first_dn + 2 * halves - 1))
    for base, partial_sums in ((other, ACC), (mine, DR)):
        for tile in range(tiles):
            partial_sums[rows_at(0, tile), :] = nt(ACT[rows_at(base, tile), :early], flat(wdn, 0, early))
            turn_in()
    need(first_dn + 2 * halves - 1)

    def whole_sum(base, tile, partial_sums):
        late = nt(ACT[rows_at(base, tile), early:], flat(wdn, early, PIECE))
        return partial_sums[rows_at(0, tile), :] + late

    for tile in range(tiles):
        SB[1, tile] = whole_sum(other, tile, ACC).astype(BF16)
        to_partner(SB.at[1, tile], RB.at[1, tile], 5 + tile)
        turn_in()
    N2 = ACC
    for tile in range(tiles):
        rows = rows_at(mine, tile)
        P[...] = whole_sum(mine, tile, DR)
        from_partner(RB.at[1, tile], 5 + tile)

        def second_norm(band, begin):
            whole = pl.ds(pl.multiple_of(mine + tile * TILE + begin, BAND), BAND)
            local_rows = pl.ds(pl.multiple_of(tile * TILE + begin, BAND), BAND)
            h1 = N1[local_rows, :] * gain0 + shift0
            resid = h1 + (P[band, :] + RB[1, tile, band, :].astype(F32)) + out2_bias
            normed, rstd = normalize(resid)
            N2[local_rows, :] = normed
            e = gy[0, local_rows, :].astype(F32) * gain1
            back = rstd * (e - mean(e) - normed * mean(e * normed))
            DR[local_rows, :] = back
            DF[whole, :] = back.astype(BF16)
            return ()

        bands(second_norm, 0)
        to_partner(DF.at[rows], DF.at[rows], 7 + tile)
        turn_in()

    def keep(row, vector):
        SG[row : row + 1, :] = vector


    if fused:

        def write(name, begin):
            def put(total):
                r[name][:, begin : begin + PIECE] = total

            return put

        def write_qkv(p):
            def put(total):
                for m in range(3):
                    r["oqkv"][m, :, p * 128 : (p + 1) * 128] = total[:, m * 128 : (m + 1) * 128]

            return put

        targets = (
            [(gdn, span[k], write("odn", k * PIECE)) for k in range(2 * halves)]
            + [(gup, span[k], write("oup", k * PIECE)) for k in range(2 * halves)]
            + [(go, span[0], write("oo", 0))]
            + [(gqkv, span[p], write_qkv(p)) for p in range(pairs)]
        )
        scatter = Scatter(targets, where, r["held"], r["pool"], r["rss"], r["rsr"], sends)
        first_out, turn_out = scatter.first, scatter.turn
    else:
        first_out, turn_out = lambda piece: None, lambda: None

    def store(ref, begin, value):
        ref[:, :, :, :, begin : begin + value.shape[1]] = value.astype(BF16).reshape(
            ref.shape[:4] + (value.shape[1],)
        )

    for tile in range(tiles):
        from_partner(DF.at[rows_at(other, tile)], 7 + tile)
    for j in range(halves):
        store(gdn, j * 2 * PIECE, tn(DF[...], ACT[:, j * 2 * PIECE : (j + 1) * 2 * PIECE]))
        turn_out()
        first_out(2 * j)
        first_out(2 * j + 1)
    for base in (mine, other):
        for tile in range(tiles):
            rows = rows_at(base, tile)
            for j in range(halves):
                at = slice(j * 2 * PIECE, (j + 1) * 2 * PIECE)
                dact = nn(DF[rows, :], flat(wdn, j * 2 * PIECE, 2 * PIECE))
                du = (dact * GP[rows, at].astype(F32)).astype(BF16)
                GP[rows, at] = du
                sums = jnp.sum(du.astype(F32), 0, keepdims=True)
                r["SI"][j : j + 1, :] = r["SI"][j : j + 1, :] + sums
            turn_out()

    for j in range(halves):
        sums = r["SI"][j : j + 1, :]
        keep(IN_BIAS + j, jnp.where(t == 0, sums, 0.0))
        keep(IN_BIAS + halves + j, jnp.where(t == 0, 0.0, sums))
    leave(1)
    for tile in range(tiles):
        rows = rows_at(other, tile)
        SB[0, tile] = nt(GP[rows, :], flat(wup)).astype(BF16)
        to_partner(SB.at[0, tile], RB.at[0, tile], 9 + tile)
        turn_out()
    for j in range(halves):
        store(gup, j * 2 * PIECE, tn(HB[...], GP[:, j * 2 * PIECE : (j + 1) * 2 * PIECE]))
        turn_out()
        first_out(2 * halves + 2 * j)
        first_out(2 * halves + 2 * j + 1)

    totals = []
    for tile in range(tiles):

        def second_norm_rest(band, begin):
            whole = pl.ds(pl.multiple_of(mine + tile * TILE + begin, BAND), BAND)
            local_rows = pl.ds(pl.multiple_of(tile * TILE + begin, BAND), BAND)
            normed, g = N2[local_rows, :], gy[0, local_rows, :].astype(F32)
            r["output"][0, local_rows, :] = (normed * gain1 + shift1).astype(BF16)
            return DF[whole, :].astype(F32), g * normed, g

        totals.append(bands(second_norm_rest, 3))
        turn_out()
    for row, parts in zip((OUT2_BIAS, GAINS + 1, SHIFTS + 1), zip(*totals)):
        keep(row, jnp.sum(sum(parts[1:], parts[0]), 0, keepdims=True))

    leave(7)
    totals = []
    for tile in range(tiles):
        rows = rows_at(mine, tile)
        P[...] = nt(GP[rows, :], flat(wup))
        from_partner(RB.at[0, tile], 9 + tile)

        def first_norm_back(band, begin):
            whole = pl.ds(pl.multiple_of(mine + tile * TILE + begin, BAND), BAND)
            local_rows = pl.ds(pl.multiple_of(tile * TILE + begin, BAND), BAND)
            g = DR[local_rows, :] + (P[band, :] + RB[0, tile, band, :].astype(F32))
            normed = N1[local_rows, :]
            e = g * gain0
            rstd = RS1[local_rows, :][:, :1]
            back = rstd * (e - mean(e) - normed * mean(e * normed))
            DR[local_rows, :] = back
            low_back = back.astype(BF16)
            DATT[whole, :] = low_back
            return low_back.astype(F32), g * normed, g

        totals.append(bands(first_norm_back, 3))
        to_partner(DATT.at[rows], DATT.at[rows], 11 + tile)
        turn_out()
    sum_da, sum_dn, sum_dh = [
        jnp.sum(sum(parts[1:], parts[0]), 0, keepdims=True) for parts in zip(*totals)
    ]
    keep(OUT_BIAS, sum_da)
    keep(GAINS, sum_dn)
    keep(SHIFTS, sum_dh)

    def project_back(base):
        for tile in range(tiles):
            rows = rows_at(base, tile)
            dctx = nn(DATT[rows, :], flat(wo))
            for p in range(pairs):
                at = slice(p * 128, (p + 1) * 128)
                d, den, ctx = dctx[:, at], DEN[rows, at], CTX[rows, at].astype(F32)
                dnum = d / jnp.maximum(den, 1.0)
                product = d * ctx
                shifted = swap(dnum)
                for h in range(2):
                    inside = low if h == 0 else jnp.logical_not(low)
                    total = den[:, h * 64 : h * 64 + 1]
                    dden = -jnp.sum(jnp.where(inside, product, 0.0), -1, keepdims=True) / total
                    dden = jnp.where(total > 1.0, dden, 0.0)
                    high = dden.astype(BF16).astype(F32)
                    rest = jnp.where(lane == 64, high, jnp.where(lane == 65, dden - high, 0.0))
                    DN[2 * p + h, rows, :] = jnp.where(low, shifted if h else dnum, rest).astype(BF16)
            turn_out()

    project_back(mine)
    for tile in range(tiles):
        from_partner(DATT.at[rows_at(other, tile)], 11 + tile)
    project_back(other)
    store(go, 0, tn(DATT[...], CTX[...]))
    turn_out()
    first_out(4 * halves)

    for p in range(pairs):
        at = p * 384

        states = [None, None]
        for i in reversed(range(chunks)):
            rows = slice(i * TILE, (i + 1) * TILE)
            cs = table[rows, :]
            dqs, dks, dvs = [], [], []
            for h in range(2):
                q, k, va = FQ[2 * p + h, rows, :], FK[2 * p + h, rows, :], VA[2 * p + h, rows, :]
                dn = DN[2 * p + h, rows, :]
                scores = jnp.where(ahead, nt(q, k), 0.0).astype(BF16)
                dscores = jnp.where(ahead, nt(dn, va), 0.0).astype(BF16)
                dq, dk, dv = nn(dscores, k), tn(dscores, q), tn(scores, dn)
                if i:
                    dq = dq + nt(dn, SS[2 * p + h, i])
                if i + 1 < chunks:
                    later = states[h].astype(BF16)
                    dk = dk + nt(va, later)
                    dv = dv + nn(k, later)
                if i:
                    grown = tn(q, dn)
                    states[h] = states[h] + grown if i + 1 < chunks else grown
                dq, dk = dq * cs, dk * cs
                dqs.append(dq + swap(dq))
                dks.append(dk + swap(dk))
                dvs.append(dv)

            def live(feat):
                a, b = feat[2 * p, rows, :].astype(F32), feat[2 * p + 1, rows, :].astype(F32)
                return jnp.where(low, a, swap(b)) > 0.0

            dq = jnp.where(live(FQ), jnp.where(low, dqs[0], dqs[1]), 0.0)
            dk = jnp.where(live(FK), jnp.where(low, dks[0], dks[1]), 0.0)
            dv = jnp.where(low, dvs[0], swap(dvs[1]))
            DPRE[rows, at : at + 384] = jnp.concatenate([dq, dk, dv], 1).astype(BF16)
            turn_out()
        piece = DPRE[:, at : at + 384]
        store(gqkv, at, tn(X[...], piece))
        sums = jnp.sum(piece.astype(F32), 0, keepdims=True)
        for m, row in enumerate((QK_BIAS, QK_BIAS + 1, VALUE_BIAS)):
            here_sums = sums[:, m * 128 : (m + 1) * 128]
            SG[row : row + 1, p * 128 : (p + 1) * 128] = jnp.where(t == 0, here_sums, 0.0)
            begin = cols + p * 128
            SG[row : row + 1, begin : begin + 128] = jnp.where(t == 0, 0.0, here_sums)
        turn_out()
        first_out(4 * halves + 1 + p)

    leave(5)
    if fused:
        Q, ss, sr = r["Q"], r["sms"], r["smr"]

        def arrive(slot, index):
            remote(Q.at[slot], Q.at[slot], ss.at[index], sr.at[index], partner).wait_recv()

        def hop(slot, index, before, device):
            arrive(slot, index)
            Q[slot + 1] = before[...] + Q[slot]
            sends.start(Q.at[slot + 1], Q.at[slot + 2], ss.at[index + 1], sr.at[index + 1], device)

        def across():
            arrive(6, 3)
            Q[7] = Q[5] + Q[6]
            sends.start_where(central, Q.at[7], Q.at[8], ss.at[4], sr.at[4], across_peer)

        def outward():
            pl.when(central)(lambda: arrive(8, 4))
            sends.start_where(central, Q.at[8], Q.at[8], ss.at[5], sr.at[5], pair_peer)

        scatter.hops = (
            lambda: hop(0, 0, SG, x_peer),
            lambda: hop(2, 1, Q.at[1], y_peer),
            lambda: hop(4, 2, Q.at[3], pair_peer),
            across,
            outward,
            lambda: pl.when(jnp.logical_not(central))(lambda: arrive(8, 5)),
        )
        sends.start(SG, Q.at[0], ss.at[0], sr.at[0], partner)
    for tile in range(tiles):
        rows = rows_at(other, tile)
        SB[1, tile] = nt(DPRE[rows, :], flat(wqkv)).astype(BF16)
        to_partner(SB.at[1, tile], RB.at[1, tile], 13 + tile)
        turn_out()
    for tile in range(tiles):
        rows, here_rows = rows_at(mine, tile), rows_at(0, tile)
        part = nt(DPRE[rows, :], flat(wqkv))
        from_partner(RB.at[1, tile], 13 + tile)
        r["grad_input"][0, here_rows, :] = DR[here_rows, :] + (part + RB[1, tile].astype(F32))
        turn_out()
    if fused:
        turn_out()
        total = Q[7] + Q[8]
        owned = pltpu.roll(total, lax.rem(width - f * owns, width), 1)
        line = jnp.sum(jnp.where(own_row, total, 0.0), 0, keepdims=True)
        line = jnp.broadcast_to(line, (8, width))
        line = pltpu.roll(line, lax.rem(width - lax.rem(f, per_row) * inner, width), 1)[:1]
        r["smalls"][...] = jnp.where(table_row < IN_BIAS, owned, line)
    else:
        r["smalls"][...] = SG[...]
    sends.finish()


def layer(fused, inputs, grad_out, slabs, small):
    sqkv, so, sup, sdn = slabs
    _, local, width = inputs.shape
    length, cols, hidden = 2 * local, sqkv.shape[-1] if fused else so.shape[-1], sup.shape[-1]
    heads, chunks, tiles = cols // HEAD_DIM, length // TILE, local // TILE
    part = width // 16
    lead = (4, 2, 2, part)
    angles = np.pi / 2.0 * np.arange(length, dtype=np.float64) / length
    table = np.concatenate(
        [np.repeat(np.cos(angles)[:, None], 64, 1), np.repeat(np.sin(angles)[:, None], 64, 1)], 1
    ).astype(np.float32)
    vmem = pl.BlockSpec(memory_space=pltpu.VMEM)
    hbm = pl.BlockSpec(memory_space=pl.ANY)
    dma = pltpu.SemaphoreType.DMA
    sizes = dict(qkv=3 * cols, o=cols, up=hidden, dn=hidden)
    pieces = (4 * cols + 2 * hidden) // PIECE

    ins = [("inputs", inputs, hbm), ("grad_out", grad_out, vmem), ("table", jnp.asarray(table), vmem)]
    if fused:
        ins += [("sqkv", sqkv, vmem), ("so", so, vmem), ("sup", sup, vmem), ("sdn", sdn, vmem)]
        ins += [(name, piece, vmem) for (name, _), piece in zip(SMALLS, small)]
    else:
        wholes = [slab.reshape(lead + slab.shape[-1:]) for slab in slabs]
        ins += [(name, value, vmem) for name, value in zip(("wqkv", "wo", "wup", "wdn"), wholes)]
        ins += [("small", small, vmem)]

    outs = [
        ("output", (1, local, width), BF16),
        ("grad_input", (1, local, width), F32),
        ("smalls", (SMALL_ROWS, width), F32),
    ]
    if fused:
        outs += [
            ("oqkv", (3, part, cols), F32),
            ("oo", (part, cols), F32),
            ("oup", (part, hidden), F32),
            ("odn", (part, hidden), F32),
        ]
    else:
        outs += [("g" + name, lead + (size,), BF16) for name, size in sizes.items()]

    def v(*shape, dtype=BF16):
        return pltpu.VMEM(shape, dtype)

    scratch = dict(
        X=v(length, width),
        HB=v(length, width),
        DF=v(length, width),
        FQ=v(heads, length, 128),
        FK=v(heads, length, 128),
        VA=v(heads, length, 128),
        DN=v(heads, length, 128),
        SS=v(heads, chunks, 128, 128),
        DEN=v(length, cols, dtype=F32),
        CTX=v(length, cols),
        N1=v(local, width, dtype=F32),
        RS1=v(local, 128, dtype=F32),
        DR=v(local, width, dtype=F32),
        ACT=v(length, hidden),
        GP=v(length, hidden),
        DPRE=v(length, 3 * cols),
        SB=v(2, tiles, TILE, width),
        RB=v(2, tiles, TILE, width),
        P=v(TILE, width, dtype=F32),
        ACC=v(local, width, dtype=F32),
        BV=v(SMALL_ROWS, width, dtype=F32),
        SG=v(SMALL_ROWS, width, dtype=F32),
        SI=v(8, 2 * PIECE, dtype=F32),
        tps=dma((16,)),
        tpr=dma((16,)),
        own=dma((1,)),
    )
    if fused:
        scratch.update({"w" + name: v(*lead, size) for name, size in sizes.items()})
        scratch.update({"g" + name: v(*lead, size) for name, size in sizes.items()})
        scratch.update(
            SM=v(4, 2, 2, SMALL_ROWS, width),
            Z=v(SMALL_ROWS, width, dtype=F32),
            Q=v(9, SMALL_ROWS, width, dtype=F32),
            held=v(pieces, 4, 2, part, PIECE),
            pool=v(sum(sum(slabs_of(order)[0]) for order in SCATTER_ORDERS), part, PIECE),
            ags=dma((pieces + 1, 5)),
            agr=dma((pieces + 1, 5)),
            rss=dma((pieces, 7)),
            rsr=dma((pieces, 7)),
            sms=dma((6,)),
            smr=dma((6,)),
        )
    names = [name for name, _, _ in ins] + [name for name, _, _ in outs] + list(scratch)
    results = pl.pallas_call(
        partial(layer_kernel, fused, names),
        name="layer",
        out_shape=tuple(jax.ShapeDtypeStruct(shape, dtype) for _, shape, dtype in outs),
        in_specs=[spec for _, _, spec in ins],
        out_specs=tuple(vmem for _ in outs),
        scratch_shapes=list(scratch.values()),
        compiler_params=pltpu.CompilerParams(
            collective_id=0, has_side_effects=True, vmem_limit_bytes=64 << 20
        ),
    )(*[value for _, value, _ in ins])
    output, grad_input, smalls, *grads = results
    return output, grad_input, smalls, grads


def hand_over_kernel(count, *refs):
    large, smalls, targets, pieces = refs[:count], refs[count], refs[count + 1 : 2 * count + 1], refs[2 * count + 1 :]
    for source, target in zip(large, targets):
        target[...] = source[...]
    for (_, row), piece in zip(SMALLS, pieces):
        piece[...] = smalls[row : row + piece.shape[0], 0 : piece.shape[1]]


def hand_over(large, smalls, shapes):
    steps = 2
    specs = []
    for v in large:
        axis = 1 if v.shape[0] == 1 else v.ndim - 1
        if v.shape[axis] % (steps * 128) == 0:
            block = v.shape[:axis] + (v.shape[axis] // steps,) + v.shape[axis + 1 :]
            specs.append(pl.BlockSpec(block, partial(lambda at, n, i: tuple(i * (k == at) for k in range(n)), axis, v.ndim)))
        else:
            specs.append(pl.BlockSpec(v.shape, partial(lambda n, i: (0,) * n, v.ndim)))
    whole = [pl.BlockSpec(shape, lambda i: (0, 0)) for shape in shapes]
    count = len(large)
    results = pl.pallas_call(
        partial(hand_over_kernel, count),
        name="hand_over",
        grid=(steps,),
        out_shape=tuple(jax.ShapeDtypeStruct(v.shape, v.dtype) for v in large)
        + tuple(jax.ShapeDtypeStruct(shape, F32) for shape in shapes),
        in_specs=specs + [pl.BlockSpec(smalls.shape, lambda i: (0, 0))],
        out_specs=tuple(specs + whole),
        compiler_params=pltpu.CompilerParams(vmem_limit_bytes=60 << 20),
    )(*large, smalls)
    return results[:count], results[count:]


def shards(
    inputs,
    query_key_value_weight,
    attention_out_weight,
    up_weight,
    down_weight,
    qk_bias,
    value_bias,
    out_bias,
    ffn_in_bias,
    ffn_out_bias,
    norm_gains,
    norm_biases,
    grad_out,
):
    rank_here, ranks = lax.axis_index("fsdp"), lax.axis_size("fsdp")
    _, rows, cols = query_key_value_weight.shape
    pairs = cols // 128
    width = inputs.shape[2]
    fused = ranks == 16 and rows % 16 == 0 and 4 * cols + 2 * up_weight.shape[1] == 12 * PIECE
    small = (
        qk_bias,
        value_bias[None],
        out_bias[None],
        ffn_out_bias[None],
        norm_gains,
        norm_biases,
        ffn_in_bias[None],
    )
    if fused:
        slabs = (query_key_value_weight, attention_out_weight.T, up_weight, down_weight.T)
    else:
        sqkv = query_key_value_weight.reshape(3, rows, pairs, 128)
        sqkv = jnp.transpose(sqkv, (1, 2, 0, 3)).reshape(rows, 3 * cols)
        slabs = (sqkv, attention_out_weight.T, up_weight, down_weight.T)
        small_shapes = small[:6]
        slabs = tuple(lax.all_gather(slab, "fsdp", axis=0, tiled=True) for slab in slabs)
        at_home = (jnp.arange(ranks) == rank_here).astype(F32)[None, :, None]
        vectors = (jnp.concatenate(small[:6], 0)[:, None, :].astype(F32) * at_home).reshape(-1, width)
        inner = (ffn_in_bias[None, None, :].astype(F32) * at_home).reshape(-1, width)
        small = jnp.concatenate([vectors, inner], 0)
        small = lax.psum(jnp.pad(small, ((0, SMALL_ROWS - small.shape[0]), (0, 0))), "fsdp")
    output, grad_input, smalls, grads = layer(fused, inputs, grad_out, slabs, small)
    if fused:
        large, small = hand_over((output, grad_input, *grads), smalls, [piece.shape for piece in small])
        output, grad_input, dqkv, do, dup, ddn = large
        dqk, dvalue, dout, dout2, dgains, dshifts, dinner = small
    else:
        dqkv, do, dup, ddn = [
            lax.psum_scatter(g.reshape(width, -1).astype(F32), "fsdp", scatter_dimension=0, tiled=True)
            for g in grads
        ]
        dqkv = jnp.transpose(dqkv.reshape(rows, pairs, 3, 128), (2, 0, 1, 3)).reshape(3, rows, cols)
        smalls = lax.psum(smalls, ("fsdp", "tp"))
        mine = lax.dynamic_slice_in_dim(smalls[:IN_BIAS], rank_here * rows, rows, 1)
        dqk, dvalue, dout, dout2, dgains, dshifts = [
            mine[row : row + piece.shape[0]] for (_, row), piece in zip(SMALLS, small_shapes)
        ]
        inner_rows = ffn_in_bias.shape[0]
        inner = smalls[IN_BIAS : IN_BIAS + inner_rows * ranks // width].reshape(-1)
        dinner = lax.dynamic_slice_in_dim(inner, rank_here * inner_rows, inner_rows, 0)
    return (
        output,
        grad_input,
        dqkv,
        do.T,
        dup,
        ddn.T,
        dqk,
        dvalue.reshape(-1),
        dout.reshape(-1),
        dinner.reshape(-1),
        dout2.reshape(-1),
        dgains,
        dshifts,
    )


def solution(mesh):
    return jax.shard_map(
        shards,
        mesh=mesh,
        in_specs=(
            P("fsdp", "tp", None),
            P(None, "fsdp", "tp"),
            P("tp", "fsdp"),
            P("fsdp", "tp"),
            P("tp", "fsdp"),
            P(None, "fsdp"),
            P("fsdp"),
            P("fsdp"),
            P("fsdp"),
            P("fsdp"),
            P(None, "fsdp"),
            P(None, "fsdp"),
            P("fsdp", "tp", None),
        ),
        out_specs=(
            P("fsdp", "tp", None),
            P("fsdp", "tp", None),
            P(None, "fsdp", "tp"),
            P("tp", "fsdp"),
            P("fsdp", "tp"),
            P("tp", "fsdp"),
            P(None, "fsdp"),
            P("fsdp"),
            P("fsdp"),
            P("fsdp"),
            P("fsdp"),
            P(None, "fsdp"),
            P(None, "fsdp"),
        ),
        check_vma=False,
    )
```
